32 devices in a mesh: fsdp: 8 (over z, x), seq: 4 (over y, core).
Axes of the slice: x: 2, y: 2, z: 4, core: 2. Of those that a mesh axis runs over, the one named last changes fastest.
Arguments:
- residual: bfloat16 [24, 1024, 767], P('fsdp', 'seq'), may hold values from -6 to 6
- out_grad: bfloat16 [24, 1024, 767], P('fsdp', 'seq'), may hold values from -6 to 6
- doc_lengths: int32 [24, 8], P('fsdp'), may hold values from 1 to 512, 1024 in all within a row
- gain_one: float32 [768], replicated, may hold values from 0.5 to 1.5
- qkv_weight: float32 [768, 2304], P('fsdp'), may hold values from -0.21875 to 0.21875
- qv_bias: float32 [12, 128], replicated, may hold values from -3 to 3
- out_weight: float32 [768, 767], P('fsdp'), may hold values from -0.875 to 0.875
- out_bias: float32 [767], replicated, may hold values from -3 to 3
- gain_two: float32 [768], replicated, may hold values from 0.5 to 1.5
- fc_weight: float32 [768, 3072], P('fsdp'), may hold values from -0.21875 to 0.21875
- fc_bias: float32 [3072], replicated, may hold values from -3 to 3
- proj_weight: float32 [3072, 767], P('fsdp'), may hold values from -0.15625 to 0.15625
- proj_bias: float32 [767], replicated, may hold values from -3 to 3
Outputs:
- output: bfloat16 [24, 1024, 767], P('fsdp', 'seq')
- input_grad: float32 [24, 1024, 767], P('fsdp', 'seq')
- gain_one_grad: float32 [768], replicated
- qkv_weight_grad: float32 [768, 2304], P('fsdp')
- qv_bias_grad: float32 [12, 128], replicated
- out_weight_grad: float32 [768, 767], P('fsdp')
- out_bias_grad: float32 [767], replicated
- gain_two_grad: float32 [768], replicated
- fc_weight_grad: float32 [768, 3072], P('fsdp')
- fc_bias_grad: float32 [3072], replicated
- proj_weight_grad: float32 [3072, 767], P('fsdp')
- proj_bias_grad: float32 [767], replicated
The draws below stay inside these ranges and needn't reach their ends.
Inputs may be any that keep to these rules, and one draw needn't show every extreme that they name: `doc_lengths`: each sequence's 8 document lengths sum to 1024; the longest is exactly 512 tokens.
All inputs are finite; a program needn't handle non-finite values.
Results may differ from the reference program's by a relative error of at most 0.014.
Values may be sent and summed in bfloat16 or wider, within the bound.
No kernel may reach another device: no remote copies, remote signals or barrier semaphores. Data moves between devices by JAX's collectives and lax.ppermute only.
A program may use at most 320 MiB of HBM per device.

```python
import math
import jax
import jax.numpy as jnp
import numpy as np
from jax import lax

D = 768
HEADS = 12
HEAD = 64
FF = 3072
DC = 767
LEN = 1024
NDOC = 8
SEQS = 24


def steps_of(own_key, shape, cuts, low, top_value):
    def one(axis_at, blocks):
        steps = jax.random.uniform(jax.random.fold_in(jax.random.fold_in(own_key, 6), axis_at), (blocks,), jnp.float32, low / len(cuts), top_value / len(cuts))
        return jnp.repeat(jnp.exp(steps), shape[axis_at] // blocks).reshape((-1,) + (1,) * (len(shape) - axis_at - 1))

    level = one(*cuts[0])
    for cut in cuts[1:]:
        level = level * one(*cut)
    return level


def length_profile(count, total, bound, lean):
    weights = [(1 << 20) // math.isqrt(grade ** lean) + 1 for grade in range(2, count + 1)]
    surplus, given = total - bound - (count - 1), [1] * (count - 1)
    while surplus > 0:
        movable = [i for i in range(count - 1) if given[i] < bound]
        whole, budget = sum([weights[i] for i in movable]), surplus
        for i in movable:
            addition = min(bound - given[i], max(1, budget * weights[i] // whole), surplus)
            given[i] = given[i] + addition
            surplus = surplus - addition
    return np.array([bound] + given)


def ragged(rng, amount, total, most, slope):
    if amount == 2:
        one = jax.random.randint(rng, (), max(1, total - most), min(most, total - 1) + 1)
        return jnp.stack([one, total - one])
    tallies = jnp.asarray(length_profile(amount, total, most, slope), jnp.int32)
    couples = (amount - 1) // 2
    giver, sink = tallies[1:1 + 2 * couples:2], tallies[2:2 + 2 * couples:2]
    margin = jnp.minimum(giver - 1, most - sink)
    moved = jax.random.randint(jax.random.fold_in(rng, 1), (couples,), 0, 1 << 20) % (margin + 1)
    tallies = tallies.at[1:1 + 2 * couples:2].set(giver - moved).at[2:2 + 2 * couples:2].set(sink + moved)
    return tallies[jax.random.permutation(jax.random.fold_in(rng, 2), amount)]


def scatter_about(key, shape, width, limit, split=(), kind=jnp.bfloat16):
    entries = jax.random.normal(key, shape, jnp.float32) * width
    if len(split) > 0:
        entries = steps_of(key, shape, split, -0.22, 0.18) * entries
    return jnp.clip(entries, min=-limit, max=limit).astype(kind)


def setup_inputs(seed: int = 0) -> dict:
    splits = jax.random.split(jax.random.key(seed), 14)
    residual = scatter_about(splits[0], (SEQS, LEN, DC), 1.0, 6.0, ((0, 8), (1, 4)))
    out_grad = scatter_about(splits[1], (SEQS, LEN, DC), 1.0, 6.0, ((0, 8), (1, 4)))
    doc_lengths = jax.vmap(lambda own: ragged(own, NDOC, LEN, LEN // 2, 2))(jax.random.split(splits[2], SEQS)).reshape((SEQS, NDOC)).astype(jnp.int32)
    gain_one = jnp.clip(1.0 + 0.1 * jax.random.normal(splits[3], (D,), jnp.float32), 0.5, 1.5)
    qkv_weight = scatter_about(splits[4], (D, 3 * D), D ** -0.5, 0.21875, ((0, 8),), jnp.float32)
    qv_bias = scatter_about(splits[5], (HEADS, 2 * HEAD), 0.5, 3.0, (), jnp.float32)
    out_weight = scatter_about(splits[6], (D, DC), (D // 16) ** -0.5, 0.875, ((0, 8),), jnp.float32)
    out_bias = scatter_about(splits[7], (DC,), 0.5, 3.0, (), jnp.float32)
    gain_two = jnp.clip(1.0 + 0.1 * jax.random.normal(splits[8], (D,), jnp.float32), 0.5, 1.5)
    fc_weight = scatter_about(splits[9], (D, FF), D ** -0.5, 0.21875, ((0, 8),), jnp.float32)
    fc_bias = scatter_about(splits[10], (FF,), 0.5, 3.0, (), jnp.float32)
    proj_weight = scatter_about(splits[11], (FF, DC), (FF // 2) ** -0.5, 0.15625, ((0, 8),), jnp.float32)
    proj_bias = scatter_about(splits[12], (DC,), 0.5, 3.0, (), jnp.float32)
    return dict(residual=residual, out_grad=out_grad, doc_lengths=doc_lengths, gain_one=gain_one, qkv_weight=qkv_weight, qv_bias=qv_bias, out_weight=out_weight, out_bias=out_bias, gain_two=gain_two, fc_weight=fc_weight, fc_bias=fc_bias, proj_weight=proj_weight, proj_bias=proj_bias)


@jax.custom_vjp
def low(v):
    return lax.optimization_barrier(v.astype(jnp.bfloat16)).astype(jnp.float32)

@jax.custom_vjp
def low_back(v):
    return v

def low_keep(v):
    return (low(v), None)

def low_pass(kept, grad):
    return (grad,)

def back_keep(v):
    return (v, None)

def back_low(kept, grad):
    return (low(grad),)
low.defvjp(low_keep, low_pass)
low_back.defvjp(back_keep, back_low)
EPS = 1e-06
HIGHEST = lax.Precision.HIGHEST

def centred_norm(residual, gain):
    row_total = lax.optimization_barrier(jnp.sum(residual, axis=-1, keepdims=True))
    full_row = jnp.concatenate([residual, -row_total], axis=-1)
    inv_rms = lax.rsqrt(lax.optimization_barrier(jnp.mean(full_row * full_row, axis=-1, keepdims=True)) + EPS)
    return full_row * inv_rms * gain

def document_index(lengths):
    starts = (jnp.cumsum(lengths) - lengths).astype(jnp.int32)
    position = jnp.arange(LEN, dtype=jnp.int32)
    inside = (position[:, None] >= starts[None, :]).astype(jnp.int32)
    return (lax.optimization_barrier(jnp.sum(inside, axis=1)) - 1).astype(jnp.int32)

def attend_sequence(operands):
    packed, doc_ids = operands
    queries = packed[:, :, 0]
    key_rows = packed[:, :, 1]
    values = packed[:, :, 2]
    scores = HEAD ** (-0.5) * jnp.einsum('qhe,khe->hqk', queries, key_rows, precision=HIGHEST)
    scores = low_back(scores)
    position = jnp.arange(LEN, dtype=jnp.int32)
    allowed = (doc_ids[:, None] == doc_ids[None, :]) & (position[None, :] <= position[:, None])
    scores = jnp.where(allowed[None], scores, -1e+30)
    prob_weights = low(jax.nn.softmax(scores, axis=-1))
    return jnp.einsum('hqk,khe->qhe', prob_weights, values, precision=HIGHEST)

def layer_forward(residual, doc_ids, gain_one, qkv_weight, qv_bias, out_weight, out_bias, gain_two, fc_weight, fc_bias, proj_weight, proj_bias):
    group_size = residual.shape[0]
    normed_one = low(centred_norm(residual, gain_one))
    zero_part = jnp.zeros((HEADS, HEAD), jnp.float32)
    bias_full = jnp.stack([qv_bias[:, :HEAD], zero_part, qv_bias[:, HEAD:]], axis=1).reshape(3 * D)
    packed = jnp.einsum('gtd,dc->gtc', normed_one, low(qkv_weight), precision=HIGHEST) + bias_full
    packed = low(low_back(packed)).reshape(group_size, LEN, HEADS, 3, HEAD)
    attended = lax.map(jax.checkpoint(attend_sequence), (packed, doc_ids))
    attended = low(low_back(attended)).reshape(group_size, LEN, D)
    branch = jnp.einsum('gtd,dc->gtc', attended, low(out_weight), precision=HIGHEST) + out_bias
    middle = residual + low_back(branch)
    normed_two = low(centred_norm(middle, gain_two))
    pre_act = jnp.einsum('gtd,df->gtf', normed_two, low(fc_weight), precision=HIGHEST) + fc_bias
    pre_act = low_back(pre_act)
    hidden = low(jax.nn.gelu(pre_act, approximate=True))
    branch_two = jnp.einsum('gtf,fc->gtc', hidden, low(proj_weight), precision=HIGHEST) + proj_bias
    return middle + low_back(branch_two)

def reference(residual, out_grad, doc_lengths, gain_one, qkv_weight, qv_bias, out_weight, out_bias, gain_two, fc_weight, fc_bias, proj_weight, proj_bias):
    per_group = math.gcd(SEQS, max(1, 4096 // LEN))
    groups = SEQS // per_group
    params = (gain_one, qkv_weight, qv_bias, out_weight, out_bias, gain_two, fc_weight, fc_bias, proj_weight, proj_bias)
    params = tuple((tensor.astype(jnp.float32) for tensor in params))
    doc_ids = jax.vmap(document_index)(doc_lengths)
    inputs = (residual.astype(jnp.float32).reshape(groups, per_group, LEN, DC), out_grad.astype(jnp.float32).reshape(groups, per_group, LEN, DC), doc_ids.reshape(groups, per_group, LEN))

    def one_group(totals, pieces):
        resid_part, grad_part, index_part = pieces

        def forward(resid_value, *weights):
            return layer_forward(resid_value, index_part, *weights)
        result, pullback = jax.vjp(forward, resid_part, *params)
        gradients = pullback(grad_part)
        totals = tuple((carried + fresh_sum for carried, fresh_sum in zip(totals, gradients[1:])))
        return (totals, (result, gradients[0]))
    initial = tuple((jnp.zeros_like(tensor) for tensor in params))
    totals, (results, input_grad) = lax.scan(one_group, initial, inputs)
    output = results.reshape(SEQS, LEN, DC).astype(jnp.bfloat16)
    input_grad = input_grad.reshape(SEQS, LEN, DC)
    return (output, input_grad, totals[0], totals[1], totals[2], totals[3], totals[4], totals[5], totals[6], totals[7], totals[8], totals[9])
```

```python
import functools

import jax
import jax.numpy as jnp
from jax import lax
from jax.experimental import pallas as pl
from jax.experimental.pallas import tpu as pltpu
from jax.sharding import Mesh, PartitionSpec as P

EPS = 1e-06
LONGEST = 512
BF = jnp.bfloat16
F32 = jnp.float32
VMEM_LIMIT = 60 * 1024 * 1024
SWAP = [(0, 1), (1, 0)]
GELU_K = 0.7978845608028654
GELU_C = 0.044715


def nn(a, b):
    return lax.dot_general(a, b, (((1,), (0,)), ((), ())), preferred_element_type=F32)


def nt(a, b):
    return lax.dot_general(a, b, (((1,), (1,)), ((), ())), preferred_element_type=F32)


def tn(a, b):
    return lax.dot_general(a, b, (((0,), (0,)), ((), ())), preferred_element_type=F32)


def lanes(shape):
    return lax.broadcasted_iota(jnp.int32, shape, 1)


def merge64(low, high):
    return jnp.where(lanes(low.shape) < 64, low, high)


def swap64(x):
    return pltpu.roll(x, 64, 1)


def fold_pair(x):
    n = x.shape[0] // 2
    top, bottom = x[:n], x[n:]
    return merge64(top, swap64(bottom)), merge64(swap64(top), bottom)


def unfold_pair(first, second):
    top = merge64(first, swap64(second))
    bottom = merge64(swap64(first), second)
    return jnp.concatenate([top, bottom], axis=0)


def vm():
    return pl.BlockSpec(memory_space=pltpu.VMEM)


def anyspace():
    return pl.BlockSpec(memory_space=pl.ANY)


def smem():
    return pl.BlockSpec(memory_space=pltpu.SMEM)


def cost(flops, nbytes, trans=0):
    return pl.CostEstimate(flops=int(flops), bytes_accessed=int(nbytes), transcendentals=int(trans))


def params(**kw):
    return pltpu.CompilerParams(vmem_limit_bytes=VMEM_LIMIT, **kw)


def unit_order(groups):
    order = []
    for head in range(3 * groups):
        order += [3 * head, 3 * head + 1]
    for group in range(groups):
        order += [9 * group + 2, 9 * group + 5]
    for group in range(groups):
        order += [9 * group + 8]
    return order


def pick_units(load, low, high):
    def half(unit, side):
        block = load(unit // 2)
        return block if unit % 2 == side else swap64(block)

    return merge64(half(low, 0), half(high, 1))


def prep_qkv(geo, idx, weight):
    rows = weight.shape[0] if not geo.fast else weight.shape[0] // 2
    width = weight.shape[1]
    order = unit_order(geo.ranks)

    def kernel(idx_ref, w_ref, o_ref):
        start = pl.multiple_of(idx_ref[3] * rows, 8) if geo.fast else 0
        for j in range(width // 128):
            block = pick_units(
                lambda b: w_ref[pl.ds(start, rows), b * 128 : (b + 1) * 128],
                order[2 * j],
                order[2 * j + 1],
            )
            o_ref[:, j * 128 : (j + 1) * 128] = block.astype(BF)

    return pl.pallas_call(
        kernel,
        out_shape=jax.ShapeDtypeStruct((rows, width), BF),
        in_specs=[smem(), vm()],
        out_specs=vm(),
        compiler_params=params(),
        cost_estimate=cost(0, weight.size * 6),
        name="prep_qkv",
    )(idx, weight)


def prep_rest(geo, idx, out_w, fc_w, proj_w):
    div = 2 if geo.fast else 1
    rows, prows = out_w.shape[0] // div, proj_w.shape[0] // div
    wide, ff, narrow = geo.wide, fc_w.shape[1], out_w.shape[1]

    def kernel(idx_ref, o_ref, f_ref, p_ref, fo_ref, pr_ref):
        start = pl.multiple_of(idx_ref[3] * rows, 8) if geo.fast else 0
        pstart = pl.multiple_of(idx_ref[3] * prows, 8) if geo.fast else 0
        fo_ref[:, :wide] = jnp.zeros((rows, wide), BF)
        fo_ref[:, :narrow] = o_ref[pl.ds(start, rows), :].astype(BF)
        fo_ref[:, wide:] = f_ref[pl.ds(start, rows), :].astype(BF)
        pr_ref[...] = jnp.zeros((prows, wide), BF)
        pr_ref[:, :narrow] = p_ref[pl.ds(pstart, prows), :].astype(BF)

    return pl.pallas_call(
        kernel,
        out_shape=(
            jax.ShapeDtypeStruct((rows, wide + ff), BF),
            jax.ShapeDtypeStruct((prows, wide), BF),
        ),
        in_specs=[smem(), vm(), vm(), vm()],
        out_specs=(vm(), vm()),
        compiler_params=params(),
        cost_estimate=cost(0, 6 * (out_w.size + fc_w.size + proj_w.size)),
        name="prep_rest",
    )(idx, out_w, fc_w, proj_w)


def qkv_forward(geo, idx, residual, gain, bias, parts, coords):
    ns, t, narrow = residual.shape
    wide, cols = geo.wide, 3 * geo.wide
    groups = geo.ranks
    count = len(parts)
    prow = parts[0].shape[0]
    slab_rows = 4 * t + t // 2

    def kernel(idx_ref, x_ref, gain_ref, bias_ref, *refs):
        w_parts = refs[:count]
        outs = refs[count : count + ns * groups]
        normed_ref, w_ref, slab, row, sem = refs[count + ns * groups :]
        copies = []
        for i in range(count):
            if geo.fast:
                dz, dx, dc = coords[i]
                block = (idx_ref[0] ^ dz) * 2 + (idx_ref[1] ^ dx)
                start = pl.multiple_of((block * 2 + (idx_ref[3] ^ dc)) * prow, 16)
            else:
                start = 0
            copies.append(
                pltpu.make_async_copy(w_parts[i], w_ref.at[pl.ds(start, prow)], sem.at[i])
            )
            copies[-1].start()
        row[...] = jnp.zeros((t, wide), F32)
        for s in range(ns):
            row[:, :narrow] = x_ref[s].astype(F32)
            x = row[...]
            full = jnp.where(lanes(x.shape) == narrow, -jnp.sum(x, 1, keepdims=True), x)
            inv = lax.rsqrt(jnp.sum(full * full, 1, keepdims=True) * (1.0 / wide) + EPS)
            normed_ref[s * t : (s + 1) * t, :] = (full * inv * gain_ref[...]).astype(BF)
        for copy in copies:
            copy.wait()

        def one(s, carry):
            n = normed_ref[pl.ds(pl.multiple_of(s * t, 16), t), :]
            for i in range(cols // 256):
                y = nn(n, w_ref[:, i * 256 : (i + 1) * 256]) + bias_ref[:, i * 256 : (i + 1) * 256]
                for half in range(2):
                    j, block = 2 * i + half, y[:, half * 128 : (half + 1) * 128]
                    if j < 3 * groups:
                        slab[s * groups + j // 3, (j % 3) * t : (j % 3 + 1) * t, :] = block.astype(BF)
                    elif j < 4 * groups:
                        slab[s * groups + j - 3 * groups, 3 * t : 4 * t, :] = block.astype(BF)
                    else:
                        g = 2 * (j - 4 * groups)
                        first, second = fold_pair(block)
                        slab[s * groups + g, 4 * t :, :] = first.astype(BF)
                        slab[s * groups + g + 1, 4 * t :, :] = second.astype(BF)
            return carry

        lax.fori_loop(0, ns, one, 0)
        for s in range(ns):
            for k in range(groups):
                outs[s * groups + k][...] = slab[s * groups + (idx_ref[4] ^ k)]

    shapes = [jax.ShapeDtypeStruct((slab_rows, 128), BF)] * (ns * groups)
    shapes += [jax.ShapeDtypeStruct((ns * t, wide), BF), jax.ShapeDtypeStruct((wide, cols), BF)]
    result = pl.pallas_call(
        kernel,
        out_shape=tuple(shapes),
        in_specs=[smem(), vm(), vm(), vm()] + [anyspace()] * count,
        out_specs=tuple([vm()] * len(shapes)),
        scratch_shapes=[
            pltpu.VMEM((ns * groups, slab_rows, 128), BF),
            pltpu.VMEM((t, wide), F32),
            pltpu.SemaphoreType.DMA((count,)),
        ],
        compiler_params=params(),
        cost_estimate=cost(2 * ns * t * wide * cols, 14e6),
        name="qkv_forward",
    )(idx, residual, gain, bias, *parts)
    return result[: ns * groups], result[-2], result[-1]


def doc_start(len_ref, s, pos, ndoc):
    start = jnp.zeros(pos.shape, jnp.int32)
    edge = len_ref[s, 0]
    for n in range(1, ndoc):
        start = jnp.where(pos >= edge, edge, start)
        edge = edge + len_ref[s, n]
    return start


def key_range(block, t):
    low = max(0, block * t - (LONGEST - 1)) // t
    return low * t, (block + 1) * t


def load_slabs(slab, refs, idx_ref):
    for k, ref in enumerate(refs):
        slab[idx_ref[4] ^ k] = ref[...]


def attention_forward(geo, s, idx, lengths, slabs):
    groups, t = geo.ranks, geo.t
    full = groups * t
    ndoc = lengths.shape[1]

    def kernel(idx_ref, len_ref, *refs):
        outs = refs[groups : 2 * groups]
        slab, qs, ks, vs, ov, osl = refs[2 * groups :]
        load_slabs(slab, refs[:groups], idx_ref)
        low = lanes((t, 128)) < 64
        for d in range(groups):
            rows = slice(d * t, (d + 1) * t)
            for h in range(3):
                qk = slab[d, h * t : (h + 1) * t, :].astype(F32)
                qs[h, rows, :] = jnp.where(low, qk * 0.125, 0.0).astype(BF)
                ks[h, rows, :] = swap64(qk).astype(BF)
            v01 = slab[d, 3 * t : 4 * t, :].astype(F32)
            vs[0, rows, :] = jnp.where(low, v01, 1.0).astype(BF)
            vs[1, rows, :] = jnp.where(low, swap64(v01), 1.0).astype(BF)
            v2 = slab[d, 4 * t :, :].astype(F32)
            half = low[: t // 2]
            vs[2, d * t : d * t + t // 2, :] = jnp.where(half, v2, 1.0).astype(BF)
            vs[2, d * t + t // 2 : (d + 1) * t, :] = jnp.where(half, swap64(v2), 1.0).astype(BF)

        def one(h, carry):
            for d in range(groups):
                first, last = key_range(d, t)
                n = last - first
                q_pos = d * t + lax.broadcasted_iota(jnp.int32, (t, 1), 0)
                start = doc_start(len_ref, s, q_pos, ndoc)
                k_pos = first + lanes((t, n))
                scores = nt(qs[h, d * t : (d + 1) * t, :], ks[h, first:last, :])
                scores = jnp.where((k_pos >= start) & (k_pos <= q_pos), scores, -1e30)
                top = jnp.max(scores, 1, keepdims=True)
                weight = jnp.exp(scores - top).astype(BF)
                o = nn(weight, vs[h, first:last, :])
                ov[h, d * t : (d + 1) * t, :] = o / swap64(o)
            return carry

        lax.fori_loop(0, 3, one, 0)
        for d in range(groups):
            rows = slice(d * t, (d + 1) * t)
            osl[d, :t, :] = merge64(ov[0, rows, :], swap64(ov[1, rows, :])).astype(BF)
            o2 = ov[2, rows, :]
            osl[d, t:, :] = merge64(o2[: t // 2], swap64(o2[t // 2 :])).astype(BF)
        for k in range(groups):
            outs[k][...] = osl[idx_ref[4] ^ k]

    shapes = [jax.ShapeDtypeStruct((t + t // 2, 128), BF)] * groups
    return pl.pallas_call(
        kernel,
        out_shape=tuple(shapes),
        in_specs=[smem(), smem()] + [vm()] * groups,
        out_specs=tuple([vm()] * groups),
        scratch_shapes=[
            pltpu.VMEM((groups, 4 * t + t // 2, 128), BF),
            pltpu.VMEM((3, full, 128), BF),
            pltpu.VMEM((3, full, 128), BF),
            pltpu.VMEM((3, full, 128), BF),
            pltpu.VMEM((3, full, 128), F32),
            pltpu.VMEM((groups, t + t // 2, 128), BF),
        ],
        compiler_params=params(),
        cost_estimate=cost(4 * 4 * 3 * full * full * 32, 4e6, 3 * full * full // 2),
        name="attention_forward",
    )(idx, lengths, *slabs)


def attention_backward(geo, s, idx, lengths, slabs, d_slabs):
    groups, t = geo.ranks, geo.t
    full = groups * t
    ndoc = lengths.shape[1]

    def kernel(idx_ref, len_ref, *refs):
        outs = refs[2 * groups : 3 * groups]
        slab, dosl, qs, ks, kt, vs, dos, dka, dva, dqa, dv, dsl = refs[3 * groups :]
        load_slabs(slab, refs[:groups], idx_ref)
        load_slabs(dosl, refs[groups : 2 * groups], idx_ref)
        low = lanes((t, 128)) < 64
        half = low[: t // 2]
        for d in range(groups):
            rows = slice(d * t, (d + 1) * t)
            first, second = slice(d * t, d * t + t // 2), slice(d * t + t // 2, (d + 1) * t)
            for h in range(3):
                qk = slab[d, h * t : (h + 1) * t, :].astype(F32)
                qs[h, rows, :] = jnp.where(low, qk * 0.125, 0.0).astype(BF)
                key = swap64(qk)
                ks[h, rows, :] = key.astype(BF)
                kt[h, :, rows] = key.T.astype(BF)
            v01 = slab[d, 3 * t : 4 * t, :].astype(F32)
            vs[0, rows, :] = v01.astype(BF)
            vs[1, rows, :] = swap64(v01).astype(BF)
            v2 = slab[d, 4 * t :, :].astype(F32)
            vs[2, first, :] = v2.astype(BF)
            vs[2, second, :] = swap64(v2).astype(BF)
            g01 = dosl[d, :t, :].astype(F32)
            dos[0, rows, :] = jnp.where(low, g01, 0.0).astype(BF)
            dos[1, rows, :] = jnp.where(low, swap64(g01), 0.0).astype(BF)
            g2 = dosl[d, t:, :].astype(F32)
            dos[2, first, :] = jnp.where(half, g2, 0.0).astype(BF)
            dos[2, second, :] = jnp.where(half, swap64(g2), 0.0).astype(BF)

        def one(h, carry):
            dka[...] = jnp.zeros((full, 128), F32)
            dva[...] = jnp.zeros((full, 128), F32)
            for d in range(groups):
                lo, hi = key_range(d, t)
                n = hi - lo
                rows = slice(d * t, (d + 1) * t)
                q_pos = d * t + lanes((1, t))
                start = doc_start(len_ref, s, q_pos, ndoc)
                k_pos = lo + lax.broadcasted_iota(jnp.int32, (n, t), 0)
                q, go = qs[h, rows, :], dos[h, rows, :]
                scores = nt(ks[h, lo:hi, :], q)
                scores = jnp.where((k_pos >= start) & (k_pos <= q_pos), scores, -1e30)
                weight = jnp.exp(scores - jnp.max(scores, 0, keepdims=True))
                prob = weight * (1.0 / jnp.sum(weight, 0, keepdims=True))
                d_prob = nt(vs[h, lo:hi, :], go)
                prod = prob * d_prob
                ds = (prod - prob * jnp.sum(prod, 0, keepdims=True)).astype(BF)
                dva[lo:hi, :] += nn(prob.astype(BF), go)
                dka[lo:hi, :] += nn(ds, q)
                dqa[rows, :] = nn(kt[h, :, lo:hi], ds).T * 0.125
            dv[h] = dva[...]
            for d in range(groups):
                rows = slice(d * t, (d + 1) * t)
                dsl[d, pl.ds(pl.multiple_of(h * t, 16), t), :] = merge64(
                    dqa[rows, :], swap64(dka[rows, :])
                ).astype(BF)
            return carry

        lax.fori_loop(0, 3, one, 0)
        for d in range(groups):
            rows = slice(d * t, (d + 1) * t)
            dsl[d, 3 * t : 4 * t, :] = merge64(dv[0, rows, :], swap64(dv[1, rows, :])).astype(BF)
            v2 = dv[2, rows, :]
            dsl[d, 4 * t :, :] = merge64(v2[: t // 2], swap64(v2[t // 2 :])).astype(BF)
        for k in range(groups):
            outs[k][...] = dsl[idx_ref[4] ^ k]

    slab_rows = 4 * t + t // 2
    shapes = [jax.ShapeDtypeStruct((slab_rows, 128), BF)] * groups
    wide_bf, wide_f32 = pltpu.VMEM((3, full, 128), BF), pltpu.VMEM((full, 128), F32)
    return pl.pallas_call(
        kernel,
        out_shape=tuple(shapes),
        in_specs=[smem(), smem()] + [vm()] * (2 * groups),
        out_specs=tuple([vm()] * groups),
        scratch_shapes=[
            pltpu.VMEM((groups, slab_rows, 128), BF),
            pltpu.VMEM((groups, t + t // 2, 128), BF),
            wide_bf,
            wide_bf,
            pltpu.VMEM((3, 128, full), BF),
            wide_bf,
            wide_bf,
            wide_f32,
            wide_f32,
            wide_f32,
            pltpu.VMEM((3, full, 128), F32),
            pltpu.VMEM((groups, slab_rows, 128), BF),
        ],
        compiler_params=params(),
        cost_estimate=cost(10 * 4 * 3 * full * full * 32, 5e6, 3 * full * full // 2),
        name="attention_backward",
    )(idx, lengths, *slabs, *d_slabs)


def mlp_block(geo, idx, o_slabs, residual, out_grad, gain, out_bias, fc_bias, proj_bias, fo_w, proj_w):
    ns, t, narrow = residual.shape
    groups, wide, ff = geo.ranks, geo.wide, geo.ff
    chunk = 512
    n_slab = ns * groups
    tokens = ns * t

    def kernel(idx_ref, *refs):
        slabs = refs[:n_slab]
        x_ref, og_ref, gain_ref, ob_ref, fb_ref, pb_ref, fo_ref, pw_ref = refs[n_slab : n_slab + 8]
        refs = refs[n_slab + 8 :]
        out_ref, hid_ref, dpre_ref, n_ref, a_ref, db_ref, ogp_ref, dmid_ref, vec_ref = refs[:9]
        d_outs = refs[9 : 9 + n_slab]
        wo, wf, wp, osl, dsl, row, mid, acc, dn, sem = refs[9 + n_slab :]
        s = pl.program_id(0)
        copies = []
        for g in range(groups):
            copies.append(
                pltpu.make_async_copy(
                    fo_ref.at[pl.ds(192 * g, 128), pl.ds(0, wide)], wo.at[pl.ds(128 * g, 128)], sem.at[0]
                )
            )
            copies.append(
                pltpu.make_async_copy(
                    fo_ref.at[pl.ds(192 * g + 128, 64), pl.ds(0, wide)],
                    wo.at[pl.ds(128 * groups + 64 * g, 64)],
                    sem.at[0],
                )
            )
        n_out = len(copies)
        copies.append(pltpu.make_async_copy(fo_ref.at[:, pl.ds(wide, ff)], wf, sem.at[1]))
        copies.append(pltpu.make_async_copy(pw_ref, wp, sem.at[2]))

        @pl.when(s == 0)
        def _():
            for copy in copies:
                copy.start()
            for q in range(ns):
                for k in range(groups):
                    osl[q * groups + (idx_ref[4] ^ k)] = slabs[q * groups + k][...]
            row[...] = jnp.zeros((t, wide), F32)
            vec_ref[...] = jnp.zeros(vec_ref.shape, F32)
            for copy in copies[:n_out]:
                copy.wait()

        for g in range(groups):
            a_ref[:, 128 * g : 128 * (g + 1)] = osl[s * groups + g, :t, :]
        for g in range(0, groups, 2):
            first = osl[s * groups + g, t:, :].astype(F32)
            second = osl[s * groups + g + 1, t:, :].astype(F32)
            base = 128 * groups + 64 * g
            a_ref[:, base : base + 128] = unfold_pair(first, second).astype(BF)
        row[:, :narrow] = og_ref[0].astype(F32)
        ogp_ref[...] = row[...].astype(BF)
        row[:, :narrow] = x_ref[0].astype(F32)
        lane = lanes((t, wide))
        middle = row[...] + nn(a_ref[...], wo[...]) + ob_ref[...]
        mid[...] = jnp.where(lane == narrow, -jnp.sum(middle, 1, keepdims=True), middle)
        acc[...] = middle + pb_ref[...]
        full = mid[...]
        inv = lax.rsqrt(jnp.sum(full * full, 1, keepdims=True) * (1.0 / wide) + EPS)
        n_ref[...] = (full * inv * gain_ref[...]).astype(BF)
        dn[...] = jnp.zeros((t, wide), F32)

        @pl.when(s == 0)
        def _():
            for copy in copies[n_out:]:
                copy.wait()

        def one(i, carry):
            cols = pl.ds(pl.multiple_of(i * chunk, 128), chunk)
            w1 = wf[:, cols]
            u = nn(n_ref[...], w1) + fb_ref[:, cols]
            square = u * u
            th = jnp.tanh(GELU_K * (u + GELU_C * square * u))
            half = 0.5 * (1.0 + th)
            hidden = (u * half).astype(BF)
            slope = half + 0.5 * u * (1.0 - th * th) * (GELU_K * (1.0 + 3.0 * GELU_C * square))
            hid_ref[:, cols] = hidden
            w2 = wp[cols, :]
            acc[...] += nn(hidden, w2)
            d_pre = (nt(ogp_ref[...], w2) * slope).astype(BF)
            dpre_ref[:, cols] = d_pre
            vec_ref[0:1, cols] += jnp.sum(d_pre.astype(F32), 0, keepdims=True)
            dn[...] += nt(d_pre, w1)
            return carry

        lax.fori_loop(0, ff // chunk, one, 0)
        out_ref[0] = acc[:, :narrow].astype(BF)
        m = mid[...] * inv
        grad = dn[...]
        vec_ref[1:2, :wide] += jnp.sum(grad * m, 0, keepdims=True)
        dm = grad * gain_ref[...]
        d_full = inv * (dm - m * (jnp.sum(dm * m, 1, keepdims=True) * (1.0 / wide)))
        last = jnp.sum(jnp.where(lane == narrow, d_full, 0.0), 1, keepdims=True)
        og = ogp_ref[...].astype(F32)
        d_mid = og + (d_full - last)
        dmid_ref[...] = d_mid
        d_branch = d_mid.astype(BF)
        db_ref[...] = d_branch
        vec_ref[2:3, :wide] += jnp.sum(d_branch.astype(F32), 0, keepdims=True)
        vec_ref[3:4, :wide] += jnp.sum(og, 0, keepdims=True)
        d_attn = nt(d_branch, wo[...])
        for g in range(groups):
            dsl[s * groups + g, :t, :] = d_attn[:, 128 * g : 128 * (g + 1)].astype(BF)
        for g in range(0, groups, 2):
            base = 128 * groups + 64 * g
            first, second = fold_pair(d_attn[:, base : base + 128])
            dsl[s * groups + g, t:, :] = first.astype(BF)
            dsl[s * groups + g + 1, t:, :] = second.astype(BF)

        @pl.when(s == ns - 1)
        def _():
            for q in range(ns):
                for k in range(groups):
                    d_outs[q * groups + k][...] = dsl[q * groups + (idx_ref[4] ^ k)]

    def rows(width):
        return pl.BlockSpec((t, width), lambda i: (i, 0))

    def whole(shape):
        return pl.BlockSpec(shape, lambda i: (0,) * len(shape))

    seq_block = pl.BlockSpec((1, t, narrow), lambda i: (i, 0, 0))
    o_shape = (t + t // 2, 128)
    sd = jax.ShapeDtypeStruct
    result = pl.pallas_call(
        kernel,
        grid=(ns,),
        out_shape=(
            sd((ns, t, narrow), BF),
            sd((tokens, ff), BF),
            sd((tokens, ff), BF),
            sd((tokens, wide), BF),
            sd((tokens, wide), BF),
            sd((tokens, wide), BF),
            sd((tokens, wide), BF),
            sd((tokens, wide), F32),
            sd((8, ff), F32),
        )
        + (sd(o_shape, BF),) * n_slab,
        in_specs=[smem()]
        + [whole(o_shape)] * n_slab
        + [seq_block, seq_block, whole((1, wide)), whole((1, wide)), whole((1, ff)), whole((1, wide))]
        + [anyspace(), anyspace()],
        out_specs=(
            seq_block,
            rows(ff),
            rows(ff),
            rows(wide),
            rows(wide),
            rows(wide),
            rows(wide),
            rows(wide),
            whole((8, ff)),
        )
        + (whole(o_shape),) * n_slab,
        scratch_shapes=[
            pltpu.VMEM((wide, wide), BF),
            pltpu.VMEM((wide, ff), BF),
            pltpu.VMEM((ff, wide), BF),
            pltpu.VMEM((n_slab, t + t // 2, 128), BF),
            pltpu.VMEM((n_slab, t + t // 2, 128), BF),
            pltpu.VMEM((t, wide), F32),
            pltpu.VMEM((t, wide), F32),
            pltpu.VMEM((t, wide), F32),
            pltpu.VMEM((t, wide), F32),
            pltpu.SemaphoreType.DMA((3,)),
        ],
        compiler_params=params(dimension_semantics=("arbitrary",)),
        cost_estimate=cost(2 * tokens * wide * (4 * ff + 2 * wide), 34e6, tokens * ff),
        name="mlp_block",
    )(
        idx, *o_slabs, residual, out_grad, gain, out_bias, fc_bias, proj_bias, fo_w, proj_w
    )
    return result[:9], result[9:]


def part_shapes(geo, rows, cols):
    if not geo.fast:
        return [jax.ShapeDtypeStruct((rows, cols), BF)]
    return [jax.ShapeDtypeStruct((rows // 4, cols), BF)] * 4


def emit_rows(geo, idx_ref, outs, tile, total, cols):
    if not geo.fast:
        outs[0][:, cols] = tile[...]
        return
    n = total // geo.fsdp // 2
    for zz in range(geo.fsdp // 2):
        for dc in range(2):
            for dx in range(2):
                block = zz * 2 + (idx_ref[1] ^ dx)
                start = pl.multiple_of((block * 2 + (idx_ref[3] ^ dc)) * n, 16)
                outs[2 * dc + dx][zz * n : (zz + 1) * n, cols] = tile[pl.ds(start, n), :]


def grad_proj(geo, idx, hidden, og):
    tokens, ff = hidden.shape
    wide = og.shape[1]
    shapes = part_shapes(geo, ff, wide)
    rows = ff // geo.fsdp if geo.fast else 384

    def kernel(idx_ref, h_ref, g_ref, *refs):
        outs, tile = refs[:-1], refs[-1]

        def one(zz, carry):
            if not geo.fast:
                at = pl.multiple_of(zz * rows, 128)
                outs[0][pl.ds(at, rows), :] = tn(h_ref[:, pl.ds(at, rows)], g_ref[...]).astype(BF)
                return carry
            for dx in range(2):
                at = pl.multiple_of((zz * 2 + (idx_ref[1] ^ dx)) * rows, 128)
                tile[...] = tn(h_ref[:, pl.ds(at, rows)], g_ref[...]).astype(BF)
                for dc in range(2):
                    start = pl.multiple_of((idx_ref[3] ^ dc) * (rows // 2), 16)
                    dest = pl.ds(pl.multiple_of(zz * (rows // 2), 16), rows // 2)
                    outs[2 * dc + dx][dest, :] = tile[pl.ds(start, rows // 2), :]
            return carry

        lax.fori_loop(0, geo.fsdp // 2 if geo.fast else ff // rows, one, 0)

    return pl.pallas_call(
        kernel,
        out_shape=tuple(shapes),
        in_specs=[smem(), vm(), vm()],
        out_specs=tuple([vm()] * len(shapes)),
        scratch_shapes=[pltpu.VMEM((rows, wide), BF)],
        compiler_params=params(),
        cost_estimate=cost(2 * tokens * ff * wide, 12e6),
        name="grad_proj",
    )(idx, hidden, og)


def grad_fo(geo, idx, attn, d_branch, normed, d_pre):
    tokens, ff = d_pre.shape
    wide = attn.shape[1]
    groups = geo.ranks
    shapes = part_shapes(geo, wide, wide + ff)
    chunk = 512

    def kernel(idx_ref, a_ref, db_ref, n_ref, dp_ref, *refs):
        outs, (nt_ref, tile, nat) = refs[:-3], refs[-3:]
        nt_ref[...] = n_ref[...].T
        nat[...] = tn(a_ref[...], db_ref[...]).astype(BF)
        for g in range(groups):
            tile[192 * g : 192 * g + 128, :] = nat[128 * g : 128 * (g + 1), :]
            base = 128 * groups + 64 * g
            tile[192 * g + 128 : 192 * (g + 1), :] = nat[base : base + 64, :]
        emit_rows(geo, idx_ref, outs, tile, wide, slice(0, wide))

        def one(i, carry):
            piece = tile.at[:, pl.ds(0, chunk)]
            piece[...] = nn(nt_ref[...], dp_ref[:, pl.ds(pl.multiple_of(i * chunk, 128), chunk)]).astype(BF)
            emit_rows(
                geo, idx_ref, outs, piece, wide, pl.ds(pl.multiple_of(wide + i * chunk, 128), chunk)
            )
            return carry

        lax.fori_loop(0, ff // chunk, one, 0)

    return pl.pallas_call(
        kernel,
        out_shape=tuple(shapes),
        in_specs=[smem(), vm(), vm(), vm(), vm()],
        out_specs=tuple([vm()] * len(shapes)),
        scratch_shapes=[
            pltpu.VMEM((wide, tokens), BF),
            pltpu.VMEM((wide, wide), BF),
            pltpu.VMEM((wide, wide), BF),
        ],
        compiler_params=params(),
        cost_estimate=cost(2 * tokens * (ff + wide) * wide, 16e6),
        name="grad_fo",
    )(idx, attn, d_branch, normed, d_pre)


def grad_qkv(geo, idx, slabs, normed):
    groups, t = geo.ranks, geo.t
    ns = len(slabs) // groups
    tokens, wide = normed.shape
    cols = 3 * wide
    shapes = part_shapes(geo, wide, cols)

    def kernel(idx_ref, *refs):
        ins, n_ref = refs[: ns * groups], refs[ns * groups]
        refs = refs[ns * groups + 1 :]
        outs = refs[: len(shapes)]
        dt_ref, nt_ref, slab, tile = refs[len(shapes) :]
        nt_ref[...] = n_ref[...].T
        for s in range(ns):
            for k in range(groups):
                slab[idx_ref[4] ^ k] = ins[s * groups + k][...]
            rows = slice(s * t, (s + 1) * t)
            for g in range(groups):
                for h in range(3):
                    j = 3 * g + h
                    dt_ref[rows, 128 * j : 128 * (j + 1)] = slab[g, h * t : (h + 1) * t, :]
                j = 3 * groups + g
                dt_ref[rows, 128 * j : 128 * (j + 1)] = slab[g, 3 * t : 4 * t, :]
            for g in range(0, groups, 2):
                j = 4 * groups + g // 2
                first, second = slab[g, 4 * t :, :].astype(F32), slab[g + 1, 4 * t :, :].astype(F32)
                dt_ref[rows, 128 * j : 128 * (j + 1)] = unfold_pair(first, second).astype(BF)

        def one(i, carry):
            at = pl.ds(pl.multiple_of(i * 256, 128), 256)
            tile[...] = nn(nt_ref[...], dt_ref[:, at]).astype(BF)
            emit_rows(geo, idx_ref, outs, tile, wide, at)
            return carry

        lax.fori_loop(0, cols // 256, one, 0)

    result = pl.pallas_call(
        kernel,
        out_shape=tuple(shapes) + (jax.ShapeDtypeStruct((tokens, cols), BF),),
        in_specs=[smem()] + [vm()] * (ns * groups + 1),
        out_specs=tuple([vm()] * (len(shapes) + 1)),
        scratch_shapes=[
            pltpu.VMEM((wide, tokens), BF),
            pltpu.VMEM((groups, 4 * t + t // 2, 128), BF),
            pltpu.VMEM((wide, 256), BF),
        ],
        compiler_params=params(),
        cost_estimate=cost(2 * tokens * cols * wide, 12e6),
        name="grad_qkv",
    )(idx, *slabs, normed)
    return result[:-1], result[-1]


def input_backward(geo, residual, gain, d_tokens, weight, d_mid, vectors):
    ns, t, narrow = residual.shape
    wide, ff, cols = geo.wide, geo.ff, 3 * geo.wide

    def kernel(x_ref, gain_ref, dt_ref, w_ref, dmid_ref, v_ref, o_ref, vec_ref, row):
        s = pl.program_id(0)

        @pl.when(s == 0)
        def _():
            row[...] = jnp.zeros((t, wide), F32)
            vec_ref[...] = jnp.zeros(vec_ref.shape, F32)
            for i in range(3):
                vec_ref[1 + i : 2 + i, :] = v_ref[1 + i : 2 + i, :wide]
            for i in range(ff // wide):
                vec_ref[4 + i : 5 + i, :] = v_ref[0:1, i * wide : (i + 1) * wide]

        row[:, :narrow] = x_ref[0].astype(F32)
        x = row[...]
        lane = lanes((t, wide))
        full = jnp.where(lane == narrow, -jnp.sum(x, 1, keepdims=True), x)
        inv = lax.rsqrt(jnp.sum(full * full, 1, keepdims=True) * (1.0 / wide) + EPS)
        m = full * inv
        dn = nt(dt_ref[...], w_ref[...])
        vec_ref[0:1, :] += jnp.sum(dn * m, 0, keepdims=True)
        for i in range(3):
            at = slice(i * wide, (i + 1) * wide)
            vec_ref[8 + i : 9 + i, :] += jnp.sum(dt_ref[:, at].astype(F32), 0, keepdims=True)
        dm = dn * gain_ref[...]
        d_full = inv * (dm - m * (jnp.sum(dm * m, 1, keepdims=True) * (1.0 / wide)))
        last = jnp.sum(jnp.where(lane == narrow, d_full, 0.0), 1, keepdims=True)
        o_ref[0] = (dmid_ref[...] + (d_full - last))[:, :narrow]

    def whole(shape):
        return pl.BlockSpec(shape, lambda i: (0,) * len(shape))

    seq_block = pl.BlockSpec((1, t, narrow), lambda i: (i, 0, 0))
    return pl.pallas_call(
        kernel,
        grid=(ns,),
        out_shape=(
            jax.ShapeDtypeStruct((ns, t, narrow), F32),
            jax.ShapeDtypeStruct((16, wide), F32),
        ),
        in_specs=[
            seq_block,
            whole((1, wide)),
            pl.BlockSpec((t, cols), lambda i: (i, 0)),
            whole((wide, cols)),
            pl.BlockSpec((t, wide), lambda i: (i, 0)),
            whole((8, ff)),
        ],
        out_specs=(seq_block, whole((16, wide))),
        scratch_shapes=[pltpu.VMEM((t, wide), F32)],
        compiler_params=params(dimension_semantics=("arbitrary",)),
        cost_estimate=cost(2 * ns * t * cols * wide, 14e6),
        name="input_backward",
    )(residual, gain, d_tokens, weight, d_mid, vectors)


def finish(geo, idx, own, other, narrow, qkv):
    half, cols = own.shape
    rows = 2 * half if geo.fast else half
    order = unit_order(geo.ranks)
    where = {unit: at for at, unit in enumerate(order)}

    def kernel(idx_ref, *refs):
        o_ref = refs[-1]
        for i, ref in enumerate(refs[:-1]):
            at = pl.ds(pl.multiple_of((idx_ref[3] ^ i) * half, 8), half) if geo.fast else slice(0, rows)
            if not qkv:
                o_ref[at, :] = ref[:, :narrow].astype(F32)
                continue
            for j in range(cols // 128):
                o_ref[at, j * 128 : (j + 1) * 128] = pick_units(
                    lambda b: ref[:, b * 128 : (b + 1) * 128].astype(F32),
                    where[2 * j],
                    where[2 * j + 1],
                )

    operands = (own, other) if geo.fast else (own,)
    return pl.pallas_call(
        kernel,
        out_shape=jax.ShapeDtypeStruct((rows, narrow), F32),
        in_specs=[smem()] + [vm()] * len(operands),
        out_specs=vm(),
        compiler_params=params(),
        cost_estimate=cost(0, rows * narrow * 6),
        name="finish",
    )(idx, *operands)


def add_bf(*terms):
    total = terms[0].astype(F32)
    for term in terms[1:]:
        total = total + term.astype(F32)
    return total.astype(BF)


def reduce_parts(geo, parts):
    if not geo.fast:
        share = lax.psum_scatter(parts[0], ("z", "x"), scatter_dimension=0, tiled=True)
        return lax.psum(share, ("y", "c")), None
    got_send = lax.ppermute(parts[3], "c", SWAP)
    got_keep = lax.ppermute(parts[2], "c", SWAP)
    from_x = lax.ppermute(add_bf(parts[1], got_send), "x", SWAP)
    partial = add_bf(parts[0], got_keep, from_x)
    share = lax.psum_scatter(partial, "z", scatter_dimension=0, tiled=True)
    total = add_bf(share, lax.ppermute(share, "y", SWAP))
    return total, lax.ppermute(total, "c", SWAP)


def sum_vectors(geo, v):
    if not geo.fast:
        return lax.psum(v, ("z", "x", "y", "c"))
    for axis in ("c", "x", "y"):
        v = v + lax.ppermute(v, axis, SWAP)
    size = geo.fsdp // 2
    step = 1
    while step < size:
        v = v + lax.ppermute(v, "z", [(i, i ^ step) for i in range(size)])
        step *= 2
    return v


class Geometry:
    pass


def local(
    geo,
    residual,
    out_grad,
    lengths,
    gain_one,
    qkv_weight,
    qv_bias,
    out_weight,
    out_bias,
    gain_two,
    fc_weight,
    fc_bias,
    proj_weight,
    proj_bias,
):
    geo.ranks = geo.seq
    ns, geo.t, narrow = residual.shape
    geo.wide, geo.ff = narrow + 1, fc_weight.shape[1]
    wide, groups, ff = geo.wide, geo.ranks, geo.ff
    heads, e = qv_bias.shape[0], qv_bias.shape[1] // 2
    size_z = geo.fsdp // 2
    geo.fast = (
        wide // geo.fsdp % 32 == 0 and ff // geo.fsdp % 128 == 0 and size_z & (size_z - 1) == 0
    )
    z, x, y, c = (lax.axis_index(a) for a in ("z", "x", "y", "c"))
    idx = jnp.stack([z, x, y, c, 2 * y + c, z, z, z]).astype(jnp.int32)
    pad = lambda v: jnp.pad(v, (0, wide - narrow)).reshape(1, wide)
    gain1, gain2 = gain_one.reshape(1, wide), gain_two.reshape(1, wide)

    v_bias = qv_bias[:, e:].reshape(groups, 3, e)
    bias = jnp.concatenate(
        [
            jnp.concatenate([qv_bias[:, :e], jnp.zeros((heads, e), F32)], axis=1).reshape(-1),
            v_bias[:, :2].reshape(-1),
            v_bias[:, 2].reshape(-1),
        ]
    ).reshape(1, 3 * wide)

    w_own = prep_qkv(geo, idx, qkv_weight)
    fo_own, proj_own = prep_rest(geo, idx, out_weight, fc_weight, proj_weight)
    if geo.fast:
        parts, coords = [w_own], [(0, 0, 0)]
        for dz in range(1, size_z):
            parts.append(lax.ppermute(w_own, "z", [(i, i ^ dz) for i in range(size_z)]))
            coords.append((dz, 0, 0))
        parts += [lax.ppermute(p, "x", SWAP) for p in parts]
        coords += [(a, 1, 0) for a, _, _ in coords]
        parts += [lax.ppermute(p, "c", SWAP) for p in parts]
        coords += [(a, b, 1) for a, b, _ in coords]
        fo_own, proj_own, _ = lax.optimization_barrier((fo_own, proj_own, parts[size_z - 1]))
        gather_axes = ("z", "x", "c")
    else:
        gather_axes = ("z", "x")
        parts, coords = [lax.all_gather(w_own, gather_axes, axis=0, tiled=True)], [(0, 0, 0)]
    fo_w = lax.all_gather(fo_own, gather_axes, axis=0, tiled=True)
    proj_w = lax.all_gather(proj_own, gather_axes, axis=0, tiled=True)

    def exchange(slabs):
        return [slabs[0]] + [
            lax.ppermute(slabs[k], ("y", "c"), [(i, i ^ k) for i in range(groups)])
            for k in range(1, groups)
        ]

    sends, normed_one, qkv_w = qkv_forward(geo, idx, residual, gain1, bias, parts, coords)
    slabs = [exchange(sends[s * groups : (s + 1) * groups]) for s in range(ns)]
    o_slabs = []
    for s in range(ns):
        o_slabs += exchange(attention_forward(geo, s, idx, lengths, slabs[s]))
    (output, hidden, d_pre, normed_two, attn, d_branch, og, d_mid, vectors), d_slabs = mlp_block(
        geo,
        idx,
        o_slabs,
        residual,
        out_grad,
        gain2,
        pad(out_bias),
        fc_bias.reshape(1, ff),
        pad(proj_bias),
        fo_w,
        proj_w,
    )
    d_slabs = [exchange(d_slabs[s * groups : (s + 1) * groups]) for s in range(ns)]
    proj_parts = grad_proj(geo, idx, hidden, og)
    fo_parts = grad_fo(geo, idx, attn, d_branch, normed_two, d_pre)
    proj_sum = reduce_parts(geo, proj_parts)
    fo_sum = reduce_parts(geo, fo_parts)
    dq_slabs = []
    for s in range(ns):
        dq_slabs += exchange(attention_backward(geo, s, idx, lengths, slabs[s], d_slabs[s]))
    qkv_parts, d_tokens = grad_qkv(geo, idx, dq_slabs, normed_one)
    qkv_sum = reduce_parts(geo, qkv_parts)
    input_grad, vecs = input_backward(geo, residual, gain1, d_tokens, qkv_w, d_mid, vectors)
    vecs = sum_vectors(geo, vecs)
    sums = vecs[8:11].reshape(-1)
    q_sum = sums[: 2 * wide].reshape(heads, 2 * e)[:, :e]
    v_two = sums[2 * wide : 2 * wide + 2 * groups * e].reshape(groups, 2, e)
    v_third = sums[2 * wide + 2 * groups * e :].reshape(groups, 1, e)
    v_sum = jnp.concatenate([v_two, v_third], axis=1).reshape(heads, e)

    cut = lambda part, a, b: None if part is None else part[:, a:b]
    return (
        output,
        input_grad,
        vecs[0],
        finish(geo, idx, *qkv_sum, 3 * wide, True),
        jnp.concatenate([q_sum, v_sum], axis=1),
        finish(geo, idx, fo_sum[0][:, :wide], cut(fo_sum[1], 0, wide), narrow, False),
        vecs[2, :narrow],
        vecs[1],
        finish(geo, idx, fo_sum[0][:, wide:], cut(fo_sum[1], wide, wide + ff), ff, False),
        vecs[4:8].reshape(-1),
        finish(geo, idx, *proj_sum, narrow, False),
        vecs[3, :narrow],
    )


def solution(mesh):
    geo = Geometry()
    geo.fsdp, geo.seq = mesh.devices.shape
    fine = Mesh(
        mesh.devices.reshape(geo.fsdp // 2, 2, geo.seq // 2, 2), ("z", "x", "y", "c")
    )
    fs, sq = ("z", "x"), ("y", "c")
    tokens, rows = P(fs, sq, None), P(fs, None)
    return jax.shard_map(
        functools.partial(local, geo),
        mesh=fine,
        in_specs=(
            tokens,
            tokens,
            rows,
            P(),
            rows,
            P(),
            rows,
            P(),
            P(),
            rows,
            P(),
            rows,
            P(),
        ),
        out_specs=(tokens, tokens, P(), rows, P(), rows, P(), P(), rows, P(), rows, P()),
        check_vma=False,
    )
```

```python
import functools

import jax
import jax.numpy as jnp
from jax import lax
from jax.experimental import pallas as pl
from jax.experimental.pallas import tpu as pltpu
from jax.sharding import Mesh, PartitionSpec as P

EPS = 1e-06
LONGEST = 512
BF = jnp.bfloat16
F32 = jnp.float32
VMEM_LIMIT = 60 * 1024 * 1024
SWAP = [(0, 1), (1, 0)]
GELU_K = 0.7978845608028654
GELU_C = 0.044715


def nn(a, b):
    return lax.dot_general(a, b, (((1,), (0,)), ((), ())), preferred_element_type=F32)


def nt(a, b):
    return lax.dot_general(a, b, (((1,), (1,)), ((), ())), preferred_element_type=F32)


def tn(a, b):
    return lax.dot_general(a, b, (((0,), (0,)), ((), ())), preferred_element_type=F32)


def lanes(shape):
    return lax.broadcasted_iota(jnp.int32, shape, 1)


def merge64(low, high):
    return jnp.where(lanes(low.shape) < 64, low, high)


def swap64(x):
    return pltpu.roll(x, 64, 1)


def fold_pair(x):
    n = x.shape[0] // 2
    top, bottom = x[:n], x[n:]
    return merge64(top, swap64(bottom)), merge64(swap64(top), bottom)


def unfold_pair(first, second):
    top = merge64(first, swap64(second))
    bottom = merge64(swap64(first), second)
    return jnp.concatenate([top, bottom], axis=0)


def vm():
    return pl.BlockSpec(memory_space=pltpu.VMEM)


def anyspace():
    return pl.BlockSpec(memory_space=pl.ANY)


def smem():
    return pl.BlockSpec(memory_space=pltpu.SMEM)


def cost(flops, nbytes, trans=0):
    scale = 0.1
    return pl.CostEstimate(
        flops=int(flops * scale), bytes_accessed=int(nbytes * scale), transcendentals=int(trans * scale)
    )


def params(**kw):
    return pltpu.CompilerParams(vmem_limit_bytes=VMEM_LIMIT, **kw)


def unit_order(groups):
    order = []
    for slot in range(3):
        for group in range(groups):
            order += [3 * (3 * group + slot), 3 * (3 * group + slot) + 1]
        for group in range(groups):
            order += [3 * (3 * group + slot) + 2]
    return order


def pick_units(load, low, high):
    def half(unit, side):
        block = load(unit // 2)
        return block if unit % 2 == side else swap64(block)

    return merge64(half(low, 0), half(high, 1))


def call(kernel, name, shapes, ins, specs, scratch, est, after=(), **kw):
    if after:
        count, extra = len(ins), len(after)
        inner = kernel

        def kernel(*refs):
            inner(*refs[:count], *refs[count + extra :])

    many = isinstance(shapes, (tuple, list))
    return pl.pallas_call(
        kernel,
        out_shape=tuple(shapes) if many else shapes,
        in_specs=list(specs) + [anyspace()] * len(after),
        out_specs=tuple([vm()] * len(shapes)) if many else vm(),
        scratch_shapes=scratch,
        compiler_params=params(**kw),
        cost_estimate=est,
        name=name,
    )(*ins, *after)


def sd(*shape, dtype=BF):
    return jax.ShapeDtypeStruct(shape, dtype)


def prep_qkv(geo, idx, weight):
    rows = weight.shape[0] // 2 if geo.fast else weight.shape[0]
    width = weight.shape[1]
    order = unit_order(geo.ranks)

    def kernel(idx_ref, w_ref, o_ref):
        start = pl.multiple_of(idx_ref[3] * rows, 8) if geo.fast else 0
        for j in range(width // 128):
            o_ref[:, j * 128 : (j + 1) * 128] = pick_units(
                lambda b: w_ref[pl.ds(start, rows), b * 128 : (b + 1) * 128],
                order[2 * j],
                order[2 * j + 1],
            ).astype(BF)

    return call(
        kernel, "prep_qkv", sd(rows, width), (idx, weight), [smem(), vm()], [], cost(0, weight.size * 6)
    )


def prep_rest(geo, idx, out_w, fc_w, proj_w):
    div = 2 if geo.fast else 1
    rows = out_w.shape[0] // div
    wide, ff, narrow = geo.wide, fc_w.shape[1], out_w.shape[1]
    blocks = ff // wide

    def kernel(idx_ref, o_ref, f_ref, p_ref, all_ref):
        start = pl.multiple_of(idx_ref[3] * rows, 8) if geo.fast else 0
        pstart = pl.multiple_of(idx_ref[3] * rows * blocks, 8) if geo.fast else 0
        all_ref[...] = jnp.zeros(all_ref.shape, BF)
        all_ref[:, :narrow] = o_ref[pl.ds(start, rows), :].astype(BF)
        all_ref[:, wide : wide + ff] = f_ref[pl.ds(start, rows), :].astype(BF)
        for i in range(blocks):
            at = wide + ff + i * wide
            all_ref[:, at : at + narrow] = p_ref[pl.ds(pstart + i * rows, rows), :].astype(BF)

    return call(
        kernel,
        "prep_rest",
        sd(rows, wide + 2 * ff),
        (idx, out_w, fc_w, proj_w),
        [smem(), vm(), vm(), vm()],
        [],
        cost(0, 6 * (out_w.size + fc_w.size + proj_w.size)),
    )


class Parts:
    def __init__(self, arrays, coords=None):
        self.arrays, self.coords = list(arrays), coords

    def copies(self, geo, idx_ref, refs, dst, sem, src_cols=None):
        made = []
        if self.coords is None:
            src = refs[0] if src_cols is None else refs[0].at[:, src_cols]
            return [pltpu.make_async_copy(src, dst, sem)]
        for ref, (dx, dc, first, count, relative) in zip(refs, self.coords):
            n = ref.shape[0] // count
            for zz in range(count):
                z = idx_ref[0] ^ (first + zz) if relative else first + zz
                start = ((z * 2 + (idx_ref[1] ^ dx)) * 2 + (idx_ref[3] ^ dc)) * n
                rows = pl.ds(zz * n, n)
                src = ref.at[rows] if src_cols is None else ref.at[rows, src_cols]
                made.append(
                    pltpu.make_async_copy(src, dst.at[pl.ds(pl.multiple_of(start, 16), n)], sem)
                )
        return made


def norm_rows(x, narrow, wide):
    full = jnp.where(lanes(x.shape) == narrow, -jnp.sum(x, 1, keepdims=True), x)
    return full, lax.rsqrt(jnp.sum(full * full, 1, keepdims=True) * (1.0 / wide) + EPS)


def qkv_forward(geo, idx, source, gain, bias, parts, slots, first):
    groups, t, ns, narrow = geo.ranks, geo.t, geo.ns, geo.narrow
    wide, tokens = geo.wide, geo.ns * geo.t
    cols, slab_rows = len(slots) * geo.wide, tokens + tokens // 2
    count = len(parts.arrays)
    n_out = len(slots) * 4

    def kernel(idx_ref, x_ref, gain_ref, bias_ref, *refs):
        w_parts, outs = refs[:count], refs[count : count + n_out]
        refs = refs[count + n_out :]
        w_ref, refs = refs[0], refs[1:]
        if first:
            normed_ref, trans_ref, slab, sem, row = refs
        else:
            slab, sem = refs
            normed_ref = x_ref
        copies = parts.copies(geo, idx_ref, w_parts, w_ref, sem)
        for copy in copies:
            copy.start()
        if first:
            row[...] = jnp.zeros((tokens, wide), F32)
            for s in range(ns):
                row[s * t : (s + 1) * t, :narrow] = x_ref[s].astype(F32)

            def norm(s, carry):
                at = pl.ds(pl.multiple_of(s * t, 16), t)
                full, inv = norm_rows(row[at, :], narrow, wide)
                normed_ref[at, :] = (full * inv * gain_ref[...]).astype(BF)
                return carry

            lax.fori_loop(0, ns, norm, 0)
            trans_ref[...] = normed_ref[...].T
        for copy in copies:
            copy.wait()

        def one(i, carry):
            base = pl.multiple_of(i * wide, 128)
            for j in range(groups // 2):
                at = pl.ds(base + 256 * j, 256)
                y = nn(normed_ref[...], w_ref[:, at]) + bias_ref[:, at]
                for half in range(2):
                    slab[i * groups + 2 * j + half, :tokens, :] = y[
                        :, half * 128 : (half + 1) * 128
                    ].astype(BF)
            at = pl.ds(base + 128 * groups, 64 * groups)
            y = nn(normed_ref[...], w_ref[:, at]) + bias_ref[:, at]
            for s in range(ns):
                rows = slice(tokens + s * (t // 2), tokens + (s + 1) * (t // 2))
                for p in range(groups // 2):
                    pair = fold_pair(y[s * t : (s + 1) * t, p * 128 : (p + 1) * 128])
                    for half in range(2):
                        slab[i * groups + 2 * p + half, rows, :] = pair[half].astype(BF)
            return carry

        lax.fori_loop(0, len(slots), one, 0)
        for i in range(len(slots)):
            store_slabs(outs[4 * i : 4 * i + 4], slab, idx_ref, i * groups)

    shapes = slab_set(slab_rows) * len(slots) + [sd(wide, cols)]
    scratch = [pltpu.VMEM((len(slots) * groups, slab_rows, 128), BF), pltpu.SemaphoreType.DMA]
    if first:
        shapes += [sd(tokens, wide), sd(wide, tokens)]
        scratch += [pltpu.VMEM((tokens, wide), F32)]
    out = call(
        kernel,
        "qkv_forward",
        shapes,
        (idx, source, gain, bias, *parts.arrays),
        [smem(), vm(), vm(), vm()] + [anyspace()] * count,
        scratch,
        cost(2 * tokens * wide * cols, 6e6),
    )
    return out[:n_out], out[n_out], out[n_out + 1 :]


def doc_start(len_ref, s, pos, ndoc):
    start = jnp.zeros(pos.shape, jnp.int32)
    edge = len_ref[s, 0]
    for n in range(1, ndoc):
        start = jnp.where(pos >= edge, edge, start)
        edge = edge + len_ref[s, n]
    return start


def first_key(block, t):
    return max(0, block * t - (LONGEST - 1)) // t


def allowed(start, block, key_block, t):
    k_pos = key_block * t + lax.broadcasted_iota(jnp.int32, (t, t), 0)
    seen = k_pos >= start
    if key_block == block:
        seen = seen & (k_pos <= block * t + lanes((1, t)))
    return seen


def store_slabs(outs, slab, idx_ref, base=0):
    for k, ref in enumerate(outs):
        ref[...] = slab[base + (idx_ref[4] ^ k)]


def load_slabs(slab, refs, idx_ref, base=0):
    for k, ref in enumerate(refs):
        slab[base + (idx_ref[4] ^ k)] = ref[...]


def slab_set(rows):
    return [sd(rows, 128)] * 4


class Stages:
    def __init__(self, idx):
        self.token = idx

    def end(self, *results):
        self.token = lax.optimization_barrier((self.token, *jax.tree.leaves(results)))[0]

    def now(self, x):
        return lax.optimization_barrier((x, self.token))[0]

    def permute(self, x, axis, pairs=SWAP):
        return lax.ppermute(self.now(x), axis, pairs)

    def exchange(self, slabs):
        return [slabs[0]] + [
            self.permute(slabs[k], ("y", "c"), xor_pairs(len(slabs), k)) for k in range(1, len(slabs))
        ]


def unfold_one(x):
    return jnp.concatenate([x, swap64(x)], axis=0)


def fold_one(x):
    n = x.shape[0] // 2
    return merge64(x[:n], swap64(x[n:]))


def attention_forward(geo, idx, lengths, slabs, after=()):
    groups, t, ns = geo.ranks, geo.t, geo.ns
    full, tokens, ndoc = groups * t, ns * t, lengths.shape[1]

    def kernel(idx_ref, len_ref, *refs):
        outs, lse_ref, ot_ref = refs[4:8], refs[8], refs[9]
        slab, qs, ks, vt, osl = refs[10:]
        load_slabs(slab, refs[:4], idx_ref)
        low = lanes((t, 128)) < 64

        def one(s, carry):
            at = pl.ds(pl.multiple_of(s * t, 16), t)
            folded = pl.ds(pl.multiple_of(tokens + s * (t // 2), 16), t // 2)
            for d in range(groups):
                rows = slice(d * t, (d + 1) * t)
                qk = slab[d, at, :].astype(F32)
                qs[rows, :] = jnp.where(low, qk * 0.125, 0.0).astype(BF)
                ks[rows, :] = swap64(qk).astype(BF)
                v = unfold_one(slab[d, folded, :].astype(F32))
                vt[:, rows] = jnp.where(low, v, 1.0).T.astype(BF)
            for d in range(groups):
                first = first_key(d, t)
                rows = slice(d * t, (d + 1) * t)
                start = doc_start(len_ref, s, d * t + lanes((1, t)), ndoc)
                blocks = []
                for b in range(first, d + 1):
                    scores = nt(ks[b * t : (b + 1) * t, :], qs[rows, :])
                    blocks.append(jnp.where(allowed(start, d, b, t), scores, -1e30))
                top = jnp.max(blocks[0], 0, keepdims=True)
                for block in blocks[1:]:
                    top = jnp.maximum(top, jnp.max(block, 0, keepdims=True))
                weight = jnp.concatenate([jnp.exp(block - top).astype(BF) for block in blocks], axis=0)
                o = nn(vt[:, first * t : (d + 1) * t], weight)
                total = o[64:65, :]
                lse_ref[s, d : d + 1, :] = top + jnp.log(total)
                o = o * (1.0 / total)
                ot_ref[s, d] = o[:64]
                osl[d, pl.ds(pl.multiple_of(s * (t // 2), 16), t // 2), :] = fold_one(o.T).astype(BF)
            return carry

        lax.fori_loop(0, ns, one, 0)
        store_slabs(outs, osl, idx_ref)

    shapes = slab_set(tokens // 2) + [sd(ns, 8, t, dtype=F32), sd(ns, groups, 64, t, dtype=F32)]
    out = call(
        kernel,
        "attention_forward",
        shapes,
        (idx, lengths, *slabs),
        [smem(), smem()] + [vm()] * 4,
        [
            pltpu.VMEM((groups, tokens + tokens // 2, 128), BF),
            pltpu.VMEM((full, 128), BF),
            pltpu.VMEM((full, 128), BF),
            pltpu.VMEM((128, full), BF),
            pltpu.VMEM((groups, tokens // 2, 128), BF),
        ],
        cost(4 * 4 * ns * full * full * 32, 4e6, ns * full * full // 2),
        after,
    )
    return out[:4], out[4:]


def attention_backward(geo, idx, slot, lengths, slabs, saved, d_slabs, after=()):
    groups, t, ns = geo.ranks, geo.t, geo.ns
    full, tokens, ndoc = groups * t, ns * t, lengths.shape[1]

    def kernel(idx_ref, len_ref, lse_ref, ot_ref, *refs):
        outs = refs[8:12]
        slab, gsl, qs, ks, kt, vs, right, delta, dvk, dq, dsl = refs[12:]
        load_slabs(slab, refs[:4], idx_ref)
        part = slice(slot * (tokens // 2), (slot + 1) * (tokens // 2))
        load_slabs(gsl, [ref.at[part] for ref in refs[4:8]], idx_ref)
        low = lanes((t, 128)) < 64

        def one(s, carry):
            at = pl.ds(pl.multiple_of(s * t, 16), t)
            folded = pl.ds(pl.multiple_of(tokens + s * (t // 2), 16), t // 2)
            o_rows = pl.ds(pl.multiple_of(s * (t // 2), 16), t // 2)
            for d in range(groups):
                rows = slice(d * t, (d + 1) * t)
                qk = slab[d, at, :].astype(F32)
                key = swap64(qk)
                q = jnp.where(low, qk * 0.125, 0.0)
                qs[rows, :] = q.astype(BF)
                ks[rows, :] = key.astype(BF)
                kt[:, rows] = key.T[:64].astype(BF)
                vs[rows, :] = unfold_one(slab[d, folded, :].astype(F32)).astype(BF)
                grad = jnp.where(low, unfold_one(gsl[d, o_rows, :].astype(F32)), 0.0)
                right[d, :t, :] = grad.astype(BF)
                right[d, t:, :] = swap64(q).astype(BF)
                delta[d : d + 1, :] = jnp.sum(grad.T[:64] * ot_ref[s, d], 0, keepdims=True)
            dvk[...] = jnp.zeros((full, 128), F32)
            for d in range(groups):
                rows = slice(d * t, (d + 1) * t)
                start = doc_start(len_ref, s, d * t + lanes((1, t)), ndoc)
                lse_row, delta_row = lse_ref[s, d : d + 1, :], delta[d : d + 1, :]
                total = jnp.zeros((64, t), F32)
                for b in range(first_key(d, t), d + 1):
                    keys = slice(b * t, (b + 1) * t)
                    scores = nt(ks[keys, :], qs[rows, :])
                    scores = jnp.where(allowed(start, d, b, t), scores, -1e30)
                    prob = jnp.exp(scores - lse_row)
                    d_prob = nt(vs[keys, :], right[d, :t, :])
                    ds = (prob * (d_prob - delta_row)).astype(BF)
                    dvk[keys, :] += nn(jnp.concatenate([prob.astype(BF), ds], axis=1), right[d])
                    total = total + nn(kt[:, keys], ds)
                dq[rows, :] = jnp.concatenate([total, total], axis=0).T * 0.125
            for d in range(groups):
                rows = slice(d * t, (d + 1) * t)
                both = dvk[rows, :]
                dsl[d, at, :] = merge64(dq[rows, :], both).astype(BF)
                dsl[d, folded, :] = fold_one(both).astype(BF)
            return carry

        lax.fori_loop(0, ns, one, 0)
        store_slabs(outs, dsl, idx_ref)

    slab_rows = tokens + tokens // 2
    flat = pltpu.VMEM((full, 128), BF)
    return call(
        kernel,
        "attention_backward",
        slab_set(slab_rows),
        (idx, lengths, *saved, *slabs, *d_slabs),
        [smem(), smem()] + [vm()] * 10,
        [
            pltpu.VMEM((groups, slab_rows, 128), BF),
            pltpu.VMEM((groups, tokens // 2, 128), BF),
            flat,
            flat,
            pltpu.VMEM((64, full), BF),
            flat,
            pltpu.VMEM((groups, 2 * t, 128), BF),
            pltpu.VMEM((8, t), F32),
            pltpu.VMEM((full, 128), F32),
            pltpu.VMEM((full, 128), F32),
            pltpu.VMEM((groups, slab_rows, 128), BF),
        ],
        cost(10 * 4 * ns * full * full * 32, 5e6, ns * full * full // 2),
        after,
    )


def mlp_forward(geo, idx, o_slabs, residual, out_grad, gain, out_bias, fc_bias, proj_bias, weights):
    groups, t, ns, narrow = geo.ranks, geo.t, geo.ns, geo.narrow
    wide, ff, tokens = geo.wide, geo.ff, geo.ns * geo.t
    n_slab, blocks = len(o_slabs), geo.ff // geo.wide
    rows = (wide // geo.fsdp) // (2 if geo.fast else 1)
    shares = wide // rows
    proj_shapes = part_shapes(geo, ff, wide)
    size_z = geo.fsdp // 2

    def kernel(idx_ref, *refs):
        slabs, refs = refs[:n_slab], refs[n_slab:]
        x_ref, og_ref, gain_ref, ob_ref, fb_ref, pb_ref = refs[:6]
        w_refs, refs = refs[6 : 6 + len(weights)], refs[6 + len(weights) :]
        out_ref, dpre_ref, n_ref, a_ref, ogp_ref, mid_ref, bias_ref, wo_ref, dn_ref = refs[:9]
        p_refs = refs[9 : 9 + len(proj_shapes)]
        wf, wp, osl, acc, tile, sem = refs[9 + len(proj_shapes) :]
        if geo.fast:
            (all_ref,) = w_refs
            out_src, fc_src = all_ref.at[:, pl.ds(0, wide)], all_ref.at[:, pl.ds(wide, ff)]
            to_proj = [
                pltpu.make_async_copy(
                    all_ref.at[pl.ds(share * rows, rows), pl.ds(wide + ff + i * wide, wide)],
                    wp.at[pl.ds((share * blocks + i) * rows, rows)],
                    sem.at[2],
                )
                for share in range(shares)
                for i in range(blocks)
            ]
        else:
            out_src, fc_src, proj_src = w_refs
            to_proj = [pltpu.make_async_copy(proj_src, wp, sem.at[2])]
        to_out = pltpu.make_async_copy(out_src, wp.at[pl.ds(0, wide)], sem.at[0])
        to_fc = pltpu.make_async_copy(fc_src, wf, sem.at[1])
        to_out.start()
        to_fc.start()
        for i in range(3):
            load_slabs(osl, slabs[4 * i : 4 * i + 4], idx_ref, i * groups)
        acc[...] = jnp.zeros((tokens, wide), F32)
        for s in range(ns):
            acc[s * t : (s + 1) * t, :narrow] = og_ref[s].astype(F32)
        ogp_ref[...] = acc[...].astype(BF)
        for s in range(ns):
            acc[s * t : (s + 1) * t, :narrow] = x_ref[s].astype(F32)

        def assemble(i, carry):
            for p in range(groups // 2):
                at = pl.ds(pl.multiple_of(i * 64 * groups + 128 * p, 128), 128)
                for s in range(ns):
                    folded = slice(s * (t // 2), (s + 1) * (t // 2))
                    a_ref[s * t : (s + 1) * t, at] = unfold_pair(
                        osl[i * groups + 2 * p, folded, :].astype(F32),
                        osl[i * groups + 2 * p + 1, folded, :].astype(F32),
                    ).astype(BF)
            return carry

        lax.fori_loop(0, 3, assemble, 0)
        to_out.wait()
        for slot in range(3):
            for g in range(groups):
                at, head = 64 * (slot * groups + g), 3 * g + slot
                wo_ref[at : at + 64, :] = wp[64 * head : 64 * (head + 1), :]
        for copy in to_proj:
            copy.start()
        acc[...] += nn(a_ref[...], wo_ref[...]) + ob_ref[...]

        def norm(s, carry):
            at = pl.ds(pl.multiple_of(s * t, 16), t)
            full, inv = norm_rows(acc[at, :], narrow, wide)
            mid_ref[at, :] = full
            n_ref[at, :] = (full * inv * gain_ref[...]).astype(BF)
            return carry

        lax.fori_loop(0, ns, norm, 0)
        to_fc.wait()
        for copy in to_proj:
            copy.wait()
        dn_ref[...] = jnp.zeros((tokens, wide), F32)

        def one(i, carry):
            cols = pl.ds(pl.multiple_of(i * wide, 128), wide)
            w1, w2 = wf[:, cols], wp[cols, :]
            u = nn(n_ref[...], w1) + fb_ref[:, cols]
            square = u * u
            th = jnp.tanh(u * (GELU_K + GELU_K * GELU_C * square))
            half = 0.5 + 0.5 * th
            hidden = (u * half).astype(BF)
            slope = half + (0.5 * u) * (1.0 - th * th) * (GELU_K + 3.0 * GELU_K * GELU_C * square)
            acc[...] += nn(hidden, w2)
            d_pre = (nt(ogp_ref[...], w2) * slope).astype(BF)
            dpre_ref[:, cols] = d_pre
            bias_ref[0:1, cols] = jnp.sum(d_pre.astype(F32), 0, keepdims=True)
            dn_ref[...] += nt(d_pre, w1)
            tile[...] = tn(hidden, ogp_ref[...]).astype(BF)
            if not geo.fast:
                p_refs[0][cols, :] = tile[...]
                return carry
            per_z = ff // size_z
            n = per_z // 4
            for k in range(wide // per_z):
                for dx in range(2):
                    for dc in range(2):
                        start = k * per_z + ((idx_ref[1] ^ dx) * 2 + (idx_ref[3] ^ dc)) * n
                        dest = (dx * size_z + i * (wide // per_z) + k) * n
                        p_refs[dc][pl.ds(pl.multiple_of(dest, 16), n), :] = tile[
                            pl.ds(pl.multiple_of(start, 16), n), :
                        ]
            return carry

        lax.fori_loop(0, blocks, one, 0)
        for s in range(ns):
            out_ref[s] = (acc[s * t : (s + 1) * t, :] + pb_ref[...])[:, :narrow].astype(BF)

    shapes = [
        sd(ns, t, narrow),
        sd(tokens, ff),
        sd(tokens, wide),
        sd(tokens, wide),
        sd(tokens, wide),
        sd(tokens, wide, dtype=F32),
        sd(8, ff, dtype=F32),
        sd(wide, wide),
        sd(tokens, wide, dtype=F32),
    ]
    out = call(
        kernel,
        "mlp_forward",
        shapes + proj_shapes,
        (idx, *o_slabs, residual, out_grad, gain, out_bias, fc_bias, proj_bias, *weights),
        [smem()] + [vm()] * (n_slab + 6) + [anyspace()] * len(weights),
        [
            pltpu.VMEM((wide, ff), BF),
            pltpu.VMEM((ff, wide), BF),
            pltpu.VMEM((3 * groups, tokens // 2, 128), BF),
            pltpu.VMEM((tokens, wide), F32),
            pltpu.VMEM((wide, wide), BF),
            pltpu.SemaphoreType.DMA((3,)),
        ],
        cost(2 * tokens * wide * (5 * ff + wide), 34e6, tokens * ff),
    )
    return out[: len(shapes)], out[len(shapes) :]


def mlp_backward(geo, idx, d_norm, out_w, og, middle, gain, bias_sums):
    groups, t, ns, narrow = geo.ranks, geo.t, geo.ns, geo.narrow
    wide, ff, tokens = geo.wide, geo.ff, geo.ns * geo.t
    n_slab = 4

    def kernel(idx_ref, dn, wo_ref, og_ref, mid_ref, gain_ref, bias_ref, *refs):
        db_ref, dmid_ref, vec_ref = refs[:3]
        outs = refs[3 : 3 + n_slab]
        da, dsl = refs[3 + n_slab :]
        vec_ref[0:1, :] = bias_ref[0:1, :]
        vec_ref[1:8, :] = jnp.zeros((7, ff), F32)

        def norm(s, carry):
            at = pl.ds(pl.multiple_of(s * t, 16), t)
            full = mid_ref[at, :]
            inv = lax.rsqrt(jnp.sum(full * full, 1, keepdims=True) * (1.0 / wide) + EPS)
            m, grad = full * inv, dn[at, :]
            dm = grad * gain_ref[...]
            d_full = inv * (dm - m * (jnp.sum(dm * m, 1, keepdims=True) * (1.0 / wide)))
            last = jnp.sum(jnp.where(lanes((t, wide)) == narrow, d_full, 0.0), 1, keepdims=True)
            og_f = og_ref[at, :].astype(F32)
            d_mid = og_f + (d_full - last)
            d_branch = d_mid.astype(BF)
            dmid_ref[at, :] = d_mid
            db_ref[at, :] = d_branch
            vec_ref[1:2, :wide] += jnp.sum(grad * m, 0, keepdims=True)
            vec_ref[2:3, :wide] += jnp.sum(d_branch.astype(F32), 0, keepdims=True)
            vec_ref[3:4, :wide] += jnp.sum(og_f, 0, keepdims=True)
            return carry

        lax.fori_loop(0, ns, norm, 0)
        da[...] = nt(db_ref[...], wo_ref[...])

        def fold(i, carry):
            for p in range(groups // 2):
                at = pl.ds(pl.multiple_of(i * 64 * groups + 128 * p, 128), 128)
                for s in range(ns):
                    pair = fold_pair(da[s * t : (s + 1) * t, at])
                    for half in range(2):
                        dest = pl.multiple_of(i * (tokens // 2) + s * (t // 2), 16)
                        dsl[2 * p + half, pl.ds(dest, t // 2), :] = pair[half].astype(BF)
            return carry

        lax.fori_loop(0, 3, fold, 0)
        store_slabs(outs, dsl, idx_ref)

    out = call(
        kernel,
        "mlp_backward",
        [sd(tokens, wide), sd(tokens, wide, dtype=F32), sd(8, ff, dtype=F32)] + slab_set(3 * tokens // 2),
        (idx, d_norm, out_w, og, middle, gain, bias_sums),
        [smem()] + [vm()] * 6,
        [
            pltpu.VMEM((tokens, wide), F32),
            pltpu.VMEM((groups, 3 * tokens // 2, 128), BF),
        ],
        cost(2 * tokens * wide * wide, 12e6),
    )
    return out[:3], out[3:]


def part_shapes(geo, rows, cols):
    return [sd(rows // 2, cols)] * 2 if geo.fast else [sd(rows, cols)]


def emit_rows(geo, idx_ref, outs, tile, total, cols, relative):
    if not geo.fast:
        outs[0][:, cols] = tile[...]
        return
    size_z = geo.fsdp // 2
    n = total // geo.fsdp // 2
    for dx in range(2):
        for zz in range(size_z):
            z = idx_ref[0] ^ zz if relative else zz
            for dc in range(2):
                start = ((z * 2 + (idx_ref[1] ^ dx)) * 2 + (idx_ref[3] ^ dc)) * n
                at = (dx * size_z + zz) * n
                outs[dc][at : at + n, cols] = tile[pl.ds(pl.multiple_of(start, 16), n), :]


def grad_fo(geo, idx, attn, d_branch, normed, d_pre, after=()):
    tokens, ff = d_pre.shape
    wide, groups, chunk = geo.wide, geo.ranks, 768
    shapes = part_shapes(geo, wide, wide + ff)

    def kernel(idx_ref, a_ref, db_ref, n_ref, dp_ref, *refs):
        outs, (trans, tile, nat) = refs[:-3], refs[-3:]
        trans[...] = n_ref[...].T
        nat[...] = tn(a_ref[...], db_ref[...]).astype(BF)
        for slot in range(3):
            for g in range(groups):
                at, head = 64 * (slot * groups + g), 3 * g + slot
                tile[64 * head : 64 * (head + 1), :] = nat[at : at + 64, :]
        emit_rows(geo, idx_ref, outs, tile, wide, slice(0, wide), False)

        def one(i, carry):
            at = pl.multiple_of(i * chunk, 128)
            tile[...] = nn(trans[...], dp_ref[:, pl.ds(at, chunk)]).astype(BF)
            emit_rows(geo, idx_ref, outs, tile, wide, pl.ds(at + wide, chunk), False)
            return carry

        lax.fori_loop(0, ff // chunk, one, 0)

    return call(
        kernel,
        "grad_fo",
        shapes,
        (idx, attn, d_branch, normed, d_pre),
        [smem()] + [vm()] * 4,
        [
            pltpu.VMEM((wide, tokens), BF),
            pltpu.VMEM((wide, wide), BF),
            pltpu.VMEM((wide, wide), BF),
        ],
        cost(2 * tokens * (ff + wide) * wide, 16e6),
        after,
    )


def grad_qkv(geo, idx, slabs, trans, after=()):
    groups, t, ns, wide = geo.ranks, geo.t, geo.ns, geo.wide
    slots, tokens = len(slabs) // 4, geo.ns * geo.t
    shapes = part_shapes(geo, wide, slots * wide)

    def kernel(idx_ref, *refs):
        ins, t_ref = refs[: slots * 4], refs[slots * 4]
        refs = refs[slots * 4 + 1 :]
        outs = refs[: len(shapes)]
        dt_ref, tile = refs[len(shapes)], refs[len(shapes) + 1]
        slab = refs[-1]
        for i in range(slots):
            load_slabs(slab.at[i], ins[4 * i : 4 * i + 4], idx_ref)

        def one(i, carry):
            base = pl.multiple_of(i * wide, 128)
            for g in range(groups):
                dt_ref[:, pl.ds(base + 128 * g, 128)] = slab[i, g, :tokens, :]
            for p in range(groups // 2):
                at = pl.ds(base + 128 * (groups + p), 128)
                for s in range(ns):
                    folded = slice(tokens + s * (t // 2), tokens + (s + 1) * (t // 2))
                    dt_ref[s * t : (s + 1) * t, at] = unfold_pair(
                        slab[i, 2 * p, folded, :].astype(F32), slab[i, 2 * p + 1, folded, :].astype(F32)
                    ).astype(BF)
            at = pl.ds(base, wide)
            tile[...] = nn(t_ref[...], dt_ref[:, at]).astype(BF)
            emit_rows(geo, idx_ref, outs, tile, wide, at, True)
            return carry

        lax.fori_loop(0, slots, one, 0)

    out = call(
        kernel,
        "grad_qkv",
        shapes + [sd(tokens, slots * wide)],
        (idx, *slabs, trans),
        [smem()] + [vm()] * (slots * 4 + 1),
        [
            pltpu.VMEM((wide, wide), BF),
            pltpu.VMEM((slots, groups, tokens + tokens // 2, 128), BF),
        ],
        cost(2 * tokens * slots * wide * wide, 4e6 * slots),
        after,
    )
    return out[:-1], out[-1]


def input_backward(geo, residual, gain, d_tokens, weights, d_mid, vectors, after=()):
    ns, t, narrow, wide, ff = geo.ns, geo.t, geo.narrow, geo.wide, geo.ff
    tokens, n, nw = ns * t, len(d_tokens), len(weights)

    def kernel(x_ref, gain_ref, dmid_ref, v_ref, *refs):
        dts, ws, (o_ref, vec_ref, row, dn) = refs[:n], refs[n : n + nw], refs[n + nw : n + nw + 4]
        vec_ref[...] = jnp.zeros(vec_ref.shape, F32)
        for i in range(3):
            vec_ref[1 + i : 2 + i, :] = v_ref[1 + i : 2 + i, :wide]
        for i in range(ff // wide):
            vec_ref[4 + i : 5 + i, :] = v_ref[0:1, i * wide : (i + 1) * wide]
        at = 8
        for i in range(n):
            for j in range(dts[i].shape[1] // wide):
                part = dts[i][:, j * wide : (j + 1) * wide].astype(F32)
                vec_ref[at : at + 1, :] = jnp.sum(part, 0, keepdims=True)
                at += 1
        slot = lambda refs: [
            ref[:, j * wide : (j + 1) * wide] for ref in refs for j in range(ref.shape[1] // wide)
        ]
        for i, (d_tok, weight) in enumerate(zip(slot(dts), slot(ws))):
            if i == 0:
                dn[...] = nt(d_tok, weight)
            else:
                dn[...] += nt(d_tok, weight)
        row[...] = jnp.zeros((tokens, wide), F32)
        for s in range(ns):
            row[s * t : (s + 1) * t, :narrow] = x_ref[s].astype(F32)

        def one(s, carry):
            rows = pl.ds(pl.multiple_of(s * t, 16), t)
            full, inv = norm_rows(row[rows, :], narrow, wide)
            m, grad = full * inv, dn[rows, :]
            vec_ref[0:1, :] += jnp.sum(grad * m, 0, keepdims=True)
            dm = grad * gain_ref[...]
            d_full = inv * (dm - m * (jnp.sum(dm * m, 1, keepdims=True) * (1.0 / wide)))
            last = jnp.sum(jnp.where(lanes((t, wide)) == narrow, d_full, 0.0), 1, keepdims=True)
            o_ref[s] = (dmid_ref[rows, :] + (d_full - last))[:, :narrow]
            return carry

        lax.fori_loop(0, ns, one, 0)

    return call(
        kernel,
        "input_backward",
        [sd(ns, t, narrow, dtype=F32), sd(16, wide, dtype=F32)],
        (residual, gain, d_mid, vectors, *d_tokens, *weights),
        [vm()] * (4 + n + nw),
        [pltpu.VMEM((tokens, wide), F32), pltpu.VMEM((tokens, wide), F32)],
        cost(2 * tokens * 3 * wide * wide, 14e6),
        after,
    )


def finish(geo, idx, pairs, plan, name):
    n = len(pairs)
    half = pairs[0][0].shape[0]
    rows = 2 * half if geo.fast else half
    sides = 2 if geo.fast else 1

    def kernel(idx_ref, *refs):
        outs = refs[n * sides :]
        for side in range(sides):
            at = pl.ds(pl.multiple_of((idx_ref[3] ^ side) * half, 8), half) if geo.fast else slice(0, rows)
            plan([refs[i * sides + side] for i in range(n)], outs, at)

    return lambda shapes: call(
        kernel,
        name,
        shapes,
        (idx, *[a for pair in pairs for a in pair[:sides]]),
        [smem()] + [vm()] * (n * sides),
        [],
        cost(0, rows * 3072 * 6),
    )


def add_bf(*terms):
    total = terms[0].astype(F32)
    for term in terms[1:]:
        total = total + term.astype(F32)
    return total.astype(BF)


def xor_pairs(size, step):
    return [(i, i ^ step) for i in range(size)]


class Reduction:
    def __init__(self, geo, stages, parts, pieces):
        self.st, self.parts, self.fast, self.pieces = stages, parts, geo.fast, pieces
        self.size_z = geo.fsdp // 2
        self.from_x, self.terms = [], []
        if self.fast:
            self.n = parts[0].shape[0] // 2
            self.m = self.n // self.size_z

    def over_cores(self):
        if self.fast:
            self.got = self.st.permute(self.parts[1], "c")
            return self.got

    def over_x(self):
        if self.fast:
            size = self.n // self.pieces
            at = self.n + size * len(self.from_x)
            keep = self.st.now(self.parts[0])
            half = add_bf(keep[at : at + size], self.got[at : at + size])
            self.from_x.append(lax.ppermute(half, "x", SWAP))
            return self.from_x[-1]

    def over_z(self, *steps):
        if not self.fast:
            return self.scatter_z() if 0 in steps else None
        keep, m, sent = self.st.now(self.parts[0]), self.m, []
        for k in steps:
            piece, inside = divmod(k * m, self.n // self.pieces)
            rows = slice(k * m, (k + 1) * m)
            term = add_bf(keep[rows], self.got[rows], self.from_x[piece][inside : inside + m])
            if k:
                sent.append(lax.ppermute(term, "z", xor_pairs(self.size_z, k)))
            self.terms.append(sent[-1] if k else term)
        return sent or self.terms

    def scatter_z(self):
        part = self.st.now(self.parts[0])
        if self.fast:
            n, got = self.n // self.pieces, self.got
            part = jnp.concatenate(
                [
                    add_bf(part[i * n : (i + 1) * n], got[i * n : (i + 1) * n], self.from_x[i])
                    for i in range(self.pieces)
                ],
                axis=0,
            )
            self.terms = [lax.psum_scatter(part, "z", scatter_dimension=0, tiled=True)]
        else:
            self.terms = [lax.psum_scatter(part, ("z", "x"), scatter_dimension=0, tiled=True)]

    def over_y(self):
        if self.fast:
            self.share = self.st.now(self.terms[0])
            if len(self.terms) > 1:
                self.share = add_bf(self.share, *self.terms[1:])
            self.got_y = lax.ppermute(self.share, "y", SWAP)
            return self.got_y

    def total(self):
        if not self.fast:
            return lax.psum(self.terms[0], ("y", "c")), None
        total = add_bf(self.st.now(self.share), self.got_y)
        return total, lax.ppermute(total, "c", SWAP)


def fold_in(v, axis, size, step=1):
    return v + lax.ppermute(v, axis, xor_pairs(size, step))


def gather_whole(own):
    return Parts([lax.all_gather(own, ("z", "x"), axis=0, tiled=True)])


class Geometry:
    pass


def local(
    geo,
    residual,
    out_grad,
    lengths,
    gain_one,
    qkv_weight,
    qv_bias,
    out_weight,
    out_bias,
    gain_two,
    fc_weight,
    fc_bias,
    proj_weight,
    proj_bias,
):
    geo.ranks = geo.seq
    geo.ns, geo.t, geo.narrow = residual.shape
    geo.wide, geo.ff = geo.narrow + 1, fc_weight.shape[1]
    narrow, wide, groups, ff = geo.narrow, geo.wide, geo.ranks, geo.ff
    heads, e = qv_bias.shape[0], qv_bias.shape[1] // 2
    size_z = geo.fsdp // 2
    geo.fast = (
        wide // geo.fsdp % 32 == 0
        and size_z & (size_z - 1) == 0
        and wide % (ff // size_z) == 0
        and ff // size_z % 64 == 0
    )
    z, x, y, c = (lax.axis_index(a) for a in ("z", "x", "y", "c"))
    idx = jnp.stack([z, x, y, c, 2 * y + c, z, z, z]).astype(jnp.int32)
    pad = lambda v: jnp.pad(v, (0, wide - narrow)).reshape(1, wide)
    gain1, gain2 = gain_one.reshape(1, wide), gain_two.reshape(1, wide)

    by_slot = qv_bias.reshape(groups, 3, 2 * e).transpose(1, 0, 2)
    q_bias = jnp.pad(by_slot[:, :, :e], ((0, 0), (0, 0), (0, e))).reshape(3, -1)
    bias = jnp.concatenate([q_bias, by_slot[:, :, e:].reshape(3, -1)], axis=1).reshape(1, -1)

    st = Stages(idx)
    own = prep_qkv(geo, idx, qkv_weight)
    bias_a, bias_b = bias[:, :wide], bias[:, wide:]
    if geo.fast:
        sides = [(dx, dc, 0, size_z, True) for dc in range(2) for dx in range(2)]
        whole = [own] + [lax.ppermute(own, "z", xor_pairs(size_z, i)) for i in range(1, size_z)]
        rest_own = prep_rest(geo, idx, out_weight, fc_weight, proj_weight)
        rest_own = lax.optimization_barrier((rest_own, whole[-1]))[0]
        rest = [lax.all_gather(rest_own, ("z", "x", "c"), axis=0, tiled=True)]
        st.end(whole)
        rows_a, rows_b = (
            jnp.concatenate([w[:, cut] for w in whole], axis=0)
            for cut in (slice(0, wide), slice(wide, 3 * wide))
        )
        other_a = st.permute(rows_a, "x")
        st.end(other_a)
        other_b = st.permute(rows_b, "x")
        w_a = [rows_a, other_a, st.permute(rows_a, "c"), st.permute(other_a, "c")]
        st.end(w_a)
        w_a = Parts(w_a, sides)
    else:
        w_a = gather_whole(own[:, :wide])
        w_b = gather_whole(own[:, wide:])
        widen = lambda w: jnp.pad(w, ((0, 0), (0, wide - narrow))).astype(BF)
        rest = [
            gather_whole(w).arrays[0]
            for w in (widen(out_weight), fc_weight.astype(BF), widen(proj_weight))
        ]
    sends, wq_a, (normed_one, normed_t) = qkv_forward(
        geo, st.token, residual, gain1, bias_a, w_a, (0,), True
    )
    st.end(sends)
    if geo.fast:
        w_b = Parts([rows_b, other_b, st.permute(rows_b, "c"), st.permute(other_b, "c")], sides)
    sends_b, wq_b, _ = qkv_forward(geo, idx, normed_one, gain1, bias_b, w_b, (1, 2), False)
    sends = list(sends) + list(sends_b)
    free = Stages(idx)
    slabs, saved, o_slabs = [], [], []
    for i in range(3):
        slabs.append(free.exchange(sends[4 * i : 4 * i + 4]))
    for i in range(3):
        o, stats = attention_forward(geo, idx, lengths, slabs[i])
        saved.append(stats)
        o_slabs += free.exchange(o)
    st.end(o_slabs)
    (output, d_pre, normed_two, attn, og, middle, bias_sums, out_w, d_norm), proj_parts = mlp_forward(
        geo,
        st.token,
        o_slabs,
        residual,
        out_grad,
        gain2,
        pad(out_bias),
        fc_bias.reshape(1, ff),
        pad(proj_bias),
        rest,
    )
    st.end(proj_parts)
    proj_red = Reduction(geo, st, proj_parts, 2)
    got = proj_red.over_cores()
    (d_branch, d_mid, vectors), d_sends = mlp_backward(
        geo, st.token, d_norm, out_w, og, middle, gain2, bias_sums
    )
    st.end(got, d_branch)
    d_slabs = st.exchange(d_sends)
    got = proj_red.over_x()
    fo_red = Reduction(geo, st, grad_fo(geo, st.token, attn, d_branch, normed_two, d_pre), 2)
    st.end(d_slabs, got, fo_red.parts)
    got = proj_red.over_x(), fo_red.over_cores()
    dq = attention_backward(geo, st.token, 0, lengths, slabs[0], saved[0], d_slabs)
    st.end(got, dq)
    dq_slabs = [st.exchange(dq)]
    proj_red.scatter_z()
    got = fo_red.over_x()
    dq = attention_backward(geo, st.token, 1, lengths, slabs[1], saved[1], d_slabs)
    st.end(got, dq, dq_slabs)
    dq_slabs.append(st.exchange(dq))
    got = fo_red.over_x()
    dq = attention_backward(geo, st.token, 2, lengths, slabs[2], saved[2], d_slabs)
    st.end(got, dq, dq_slabs)
    dq_slabs.append(st.exchange(dq))
    fo_red.scatter_z()
    parts_a, dt_a = grad_qkv(geo, st.token, dq_slabs[0] + dq_slabs[1], normed_t)
    red_a = Reduction(geo, st, parts_a, 1)
    st.end(dq_slabs, parts_a)
    got = red_a.over_cores()
    parts_b, dt_b = grad_qkv(geo, st.token, dq_slabs[2], normed_t)
    red_b = Reduction(geo, st, parts_b, 1)
    st.end(got, parts_b)
    got = red_a.over_x(), proj_red.over_y(), red_b.over_cores()
    input_grad, vecs = input_backward(
        geo,
        st.now(residual),
        gain1,
        (dt_a, dt_b),
        (wq_a, wq_b),
        d_mid,
        vectors,
    )
    st.end(got, vecs)
    got = red_a.over_z(*range(size_z)), red_b.over_x()
    if geo.fast:
        vecs = fold_in(fold_in(st.now(vecs), "c", 2), "x", 2)
    else:
        vecs = lax.psum(vecs, ("z", "x", "y", "c"))
    proj_sum = proj_red.total()
    st.end(got, vecs, proj_sum)
    got = red_b.over_z(*range(size_z)), red_a.over_y(), fo_red.over_y()
    if geo.fast:
        vecs = fold_in(st.now(vecs), "y", 2)
    st.end(got, vecs)
    got = red_b.over_y()
    sum_a, fo_sum = red_a.total(), fo_red.total()
    if geo.fast:
        vecs = fold_in(st.now(vecs), "z", size_z, 1)
    st.end(got, vecs, sum_a, fo_sum)
    sum_b = red_b.total()
    step = 2
    while geo.fast and step < size_z:
        vecs = fold_in(vecs, "z", size_z, step)
        step *= 2
    sums = vecs[8:11].reshape(3, 3 * groups, e)
    q_sum = sums[:, : 2 * groups].reshape(3, groups, 2, e)[:, :, 0]
    v_sum = sums[:, 2 * groups :]
    qv_grad = jnp.concatenate([q_sum, v_sum], axis=2).transpose(1, 0, 2).reshape(heads, 2 * e)

    order = unit_order(groups)
    where = {unit: at for at, unit in enumerate(order)}

    def plan_qkv(ins, outs, at):
        def read(b):
            if b < 2 * wide // 128:
                return ins[0][:, b * 128 : (b + 1) * 128].astype(F32)
            return ins[1][:, b * 128 - 2 * wide : (b + 1) * 128 - 2 * wide].astype(F32)

        for j in range(3 * wide // 128):
            outs[0][at, j * 128 : (j + 1) * 128] = pick_units(read, where[2 * j], where[2 * j + 1])

    def plan_fo(ins, outs, at):
        outs[0][at, :] = ins[0][:, :narrow].astype(F32)
        outs[1][at, :] = ins[0][:, wide:].astype(F32)

    def plan_proj(ins, outs, at):
        outs[0][at, :] = ins[0][:, :narrow].astype(F32)

    block = wide // geo.fsdp
    (qkv_grad,) = finish(geo, idx, [sum_a, sum_b], plan_qkv, "finish_qkv")([sd(block, 3 * wide, dtype=F32)])
    out_w_grad, fc_w_grad = finish(geo, idx, [fo_sum], plan_fo, "finish_fo")(
        [sd(block, narrow, dtype=F32), sd(block, ff, dtype=F32)]
    )
    (proj_w_grad,) = finish(geo, idx, [proj_sum], plan_proj, "finish_proj")(
        [sd(ff // geo.fsdp, narrow, dtype=F32)]
    )
    return (
        output,
        input_grad,
        vecs[0],
        qkv_grad,
        qv_grad,
        out_w_grad,
        vecs[2, :narrow],
        vecs[1],
        fc_w_grad,
        vecs[4:8].reshape(-1),
        proj_w_grad,
        vecs[3, :narrow],
    )


def solution(mesh):
    geo = Geometry()
    geo.fsdp, geo.seq = mesh.devices.shape
    fine = Mesh(
        mesh.devices.reshape(geo.fsdp // 2, 2, geo.seq // 2, 2), ("z", "x", "y", "c")
    )
    fs, sq = ("z", "x"), ("y", "c")
    tokens, rows = P(fs, sq, None), P(fs, None)
    return jax.shard_map(
        functools.partial(local, geo),
        mesh=fine,
        in_specs=(
            tokens,
            tokens,
            rows,
            P(),
            rows,
            P(),
            rows,
            P(),
            P(),
            rows,
            P(),
            rows,
            P(),
        ),
        out_specs=(tokens, tokens, P(), rows, P(), rows, P(), P(), rows, P(), rows, P()),
        check_vma=False,
    )
```

```python
import functools

import jax
import jax.numpy as jnp
from jax import lax
from jax.experimental import pallas as pl
from jax.experimental.pallas import tpu as pltpu
from jax.sharding import Mesh, PartitionSpec as P

EPS = 1e-06
LONGEST = 512
BF = jnp.bfloat16
F32 = jnp.float32
VMEM_LIMIT = 60 * 1024 * 1024
SWAP = [(0, 1), (1, 0)]
GELU_K = 0.7978845608028654
GELU_C = 0.044715


def nn(a, b):
    return lax.dot_general(a, b, (((1,), (0,)), ((), ())), preferred_element_type=F32)


def nt(a, b):
    return lax.dot_general(a, b, (((1,), (1,)), ((), ())), preferred_element_type=F32)


def tn(a, b):
    return lax.dot_general(a, b, (((0,), (0,)), ((), ())), preferred_element_type=F32)


def lanes(shape):
    return lax.broadcasted_iota(jnp.int32, shape, 1)


def merge64(low, high):
    return jnp.where(lanes(low.shape) < 64, low, high)


def swap64(x):
    return pltpu.roll(x, 64, 1)


def fold_pair(x):
    n = x.shape[0] // 2
    top, bottom = x[:n], x[n:]
    return merge64(top, swap64(bottom)), merge64(swap64(top), bottom)


def unfold_pair(first, second):
    top = merge64(first, swap64(second))
    bottom = merge64(swap64(first), second)
    return jnp.concatenate([top, bottom], axis=0)


def vm():
    return pl.BlockSpec(memory_space=pltpu.VMEM)


def anyspace():
    return pl.BlockSpec(memory_space=pl.ANY)


def smem():
    return pl.BlockSpec(memory_space=pltpu.SMEM)


def cost(flops, nbytes, trans=0):
    scale = 0.1
    return pl.CostEstimate(
        flops=int(flops * scale), bytes_accessed=int(nbytes * scale), transcendentals=int(trans * scale)
    )


def params(**kw):
    return pltpu.CompilerParams(vmem_limit_bytes=VMEM_LIMIT, **kw)


def unit_order(groups):
    order = []
    for slot in range(3):
        for group in range(groups):
            order += [3 * (3 * group + slot), 3 * (3 * group + slot) + 1]
        for group in range(groups):
            order += [3 * (3 * group + slot) + 2]
    return order


def pick_units(load, low, high):
    def half(unit, side):
        block = load(unit // 2)
        return block if unit % 2 == side else swap64(block)

    return merge64(half(low, 0), half(high, 1))


def call(kernel, name, shapes, ins, specs, scratch, est, after=(), out_specs=None, **kw):
    if after:
        count, extra = len(ins), len(after)
        inner = kernel

        def kernel(*refs):
            inner(*refs[:count], *refs[count + extra :])

    many = isinstance(shapes, (tuple, list))
    return pl.pallas_call(
        kernel,
        out_shape=tuple(shapes) if many else shapes,
        in_specs=list(specs) + [anyspace()] * len(after),
        out_specs=out_specs or (tuple([vm()] * len(shapes)) if many else vm()),
        scratch_shapes=scratch,
        compiler_params=params(**kw),
        cost_estimate=est,
        name=name,
    )(*ins, *after)


def sd(*shape, dtype=BF):
    return jax.ShapeDtypeStruct(shape, dtype)


def prep_qkv(geo, idx, weight):
    rows = weight.shape[0] // 2 if geo.fast else weight.shape[0]
    width = weight.shape[1]
    order = unit_order(geo.ranks)

    def kernel(idx_ref, w_ref, o_ref):
        start = pl.multiple_of(idx_ref[3] * rows, 8) if geo.fast else 0
        for j in range(width // 128):
            o_ref[:, j * 128 : (j + 1) * 128] = pick_units(
                lambda b: w_ref[pl.ds(start, rows), b * 128 : (b + 1) * 128],
                order[2 * j],
                order[2 * j + 1],
            ).astype(BF)

    return call(
        kernel, "prep_qkv", sd(rows, width), (idx, weight), [smem(), vm()], [], cost(0, weight.size * 6)
    )


def prep_rest(geo, idx, out_w, fc_w, proj_w):
    div = 2 if geo.fast else 1
    rows = out_w.shape[0] // div
    wide, ff, narrow = geo.wide, fc_w.shape[1], out_w.shape[1]
    blocks = ff // wide

    def kernel(idx_ref, o_ref, f_ref, p_ref, all_ref):
        start = pl.multiple_of(idx_ref[3] * rows, 8) if geo.fast else 0
        pstart = pl.multiple_of(idx_ref[3] * rows * blocks, 8) if geo.fast else 0
        all_ref[...] = jnp.zeros(all_ref.shape, BF)
        all_ref[:, :narrow] = o_ref[pl.ds(start, rows), :].astype(BF)
        all_ref[:, wide : wide + ff] = f_ref[pl.ds(start, rows), :].astype(BF)
        for i in range(blocks):
            at = wide + ff + i * wide
            all_ref[:, at : at + narrow] = p_ref[pl.ds(pstart + i * rows, rows), :].astype(BF)

    return call(
        kernel,
        "prep_rest",
        sd(rows, wide + 2 * ff),
        (idx, out_w, fc_w, proj_w),
        [smem(), vm(), vm(), vm()],
        [],
        cost(0, 6 * (out_w.size + fc_w.size + proj_w.size)),
    )


class Parts:
    def __init__(self, arrays, coords=None):
        self.arrays, self.coords = list(arrays), coords

    def copies(self, geo, idx_ref, refs, dst, sem, src_cols=None):
        made = []
        if self.coords is None:
            src = refs[0] if src_cols is None else refs[0].at[:, src_cols]
            return [pltpu.make_async_copy(src, dst, sem)]
        for ref, (dx, dc, first, count, relative) in zip(refs, self.coords):
            n = ref.shape[0] // count
            for zz in range(count):
                z = idx_ref[0] ^ (first + zz) if relative else first + zz
                start = ((z * 2 + (idx_ref[1] ^ dx)) * 2 + (idx_ref[3] ^ dc)) * n
                rows = pl.ds(zz * n, n)
                src = ref.at[rows] if src_cols is None else ref.at[rows, src_cols]
                made.append(
                    pltpu.make_async_copy(src, dst.at[pl.ds(pl.multiple_of(start, 16), n)], sem)
                )
        return made


def norm_rows(x, narrow, wide):
    full = jnp.where(lanes(x.shape) == narrow, -jnp.sum(x, 1, keepdims=True), x)
    return full, lax.rsqrt(jnp.sum(full * full, 1, keepdims=True) * (1.0 / wide) + EPS)


def qkv_forward(geo, idx, source, gain, bias, parts, slots, first):
    groups, t, ns, narrow = geo.ranks, geo.t, geo.ns, geo.narrow
    wide, tokens = geo.wide, geo.ns * geo.t
    cols, slab_rows = len(slots) * geo.wide, tokens + tokens // 2
    count = len(parts.arrays)
    n_out = len(slots) * 4

    def kernel(idx_ref, x_ref, gain_ref, bias_ref, *refs):
        w_parts, outs = refs[:count], refs[count : count + n_out]
        refs = refs[count + n_out :]
        w_ref, refs = refs[0], refs[1:]
        if first:
            normed_ref, trans_ref, slab, sem, row = refs
        else:
            slab, sem = refs
            normed_ref = x_ref
        copies = parts.copies(geo, idx_ref, w_parts, w_ref, sem)
        for copy in copies:
            copy.start()
        if first:
            def norm(s, carry):
                at = pl.ds(pl.multiple_of(s * t, 16), t)
                row[at, :] = jnp.zeros((t, wide), F32)
                row[at, :narrow] = x_ref[s].astype(F32)
                full, inv = norm_rows(row[at, :], narrow, wide)
                normed_ref[at, :] = (full * inv * gain_ref[...]).astype(BF)
                return carry

            lax.fori_loop(0, ns, norm, 0)
            trans_ref[...] = normed_ref[...].T
        for copy in copies:
            copy.wait()

        def one(i, carry):
            base = pl.multiple_of(i * wide, 128)
            for j in range(groups // 2):
                at = pl.ds(base + 256 * j, 256)
                y = nn(normed_ref[...], w_ref[:, at]) + bias_ref[:, at]
                for half in range(2):
                    slab[i * groups + 2 * j + half, :tokens, :] = y[
                        :, half * 128 : (half + 1) * 128
                    ].astype(BF)
            at = pl.ds(base + 128 * groups, 64 * groups)
            y = nn(normed_ref[...], w_ref[:, at]) + bias_ref[:, at]
            for s in range(ns):
                rows = slice(tokens + s * (t // 2), tokens + (s + 1) * (t // 2))
                for p in range(groups // 2):
                    pair = fold_pair(y[s * t : (s + 1) * t, p * 128 : (p + 1) * 128])
                    for half in range(2):
                        slab[i * groups + 2 * p + half, rows, :] = pair[half].astype(BF)
            return carry

        lax.fori_loop(0, len(slots), one, 0)
        for i in range(len(slots)):
            store_slabs(outs[4 * i : 4 * i + 4], slab, idx_ref, i * groups)

    shapes = slab_set(slab_rows) * len(slots) + [sd(wide, cols)]
    scratch = [pltpu.VMEM((len(slots) * groups, slab_rows, 128), BF), pltpu.SemaphoreType.DMA]
    if first:
        shapes += [sd(tokens, wide), sd(wide, tokens)]
        scratch += [pltpu.VMEM((tokens, wide), F32)]
    out = call(
        kernel,
        "qkv_forward",
        shapes,
        (idx, source, gain, bias, *parts.arrays),
        [smem(), vm(), vm(), vm()] + [anyspace()] * count,
        scratch,
        cost(2 * tokens * wide * cols, 6e6),
    )
    return out[:n_out], out[n_out], out[n_out + 1 :]


def doc_start(len_ref, s, pos, ndoc):
    start = jnp.zeros(pos.shape, jnp.int32)
    edge = len_ref[s, 0]
    for n in range(1, ndoc):
        start = jnp.where(pos >= edge, edge, start)
        edge = edge + len_ref[s, n]
    return start


def first_key(block, t):
    return max(0, block * t - (LONGEST - 1)) // t


def allowed(start, block, key_block, t):
    k_pos = key_block * t + lax.broadcasted_iota(jnp.int32, (t, t), 0)
    seen = k_pos >= start
    if key_block == block:
        seen = seen & (k_pos <= block * t + lanes((1, t)))
    return seen


def store_slabs(outs, slab, idx_ref, base=0):
    for k, ref in enumerate(outs):
        ref[...] = slab[base + (idx_ref[4] ^ k)]


def load_slabs(slab, refs, idx_ref, base=0):
    for k, ref in enumerate(refs):
        slab[base + (idx_ref[4] ^ k)] = ref[...]


def slab_set(rows):
    return [sd(rows, 128)] * 4


class Stages:
    def __init__(self, idx):
        self.token = idx

    def end(self, *results):
        self.token = lax.optimization_barrier((self.token, *jax.tree.leaves(results)))[0]

    def now(self, x):
        return lax.optimization_barrier((x, self.token))[0]

    def permute(self, x, axis, pairs=SWAP):
        return lax.ppermute(self.now(x), axis, pairs)

    def exchange(self, slabs):
        return [slabs[0]] + [
            self.permute(slabs[k], ("y", "c"), xor_pairs(len(slabs), k)) for k in range(1, len(slabs))
        ]


def unfold_one(x):
    return jnp.concatenate([x, swap64(x)], axis=0)


def fold_one(x):
    n = x.shape[0] // 2
    return merge64(x[:n], swap64(x[n:]))


def attention_forward(geo, idx, lengths, slabs, after=()):
    groups, t, ns = geo.ranks, geo.t, geo.ns
    full, tokens, ndoc = groups * t, ns * t, lengths.shape[1]

    def kernel(idx_ref, len_ref, *refs):
        outs, lse_ref, ot_ref = refs[4:8], refs[8], refs[9]
        slab, qs, ks, vt, osl = refs[10:]
        load_slabs(slab, refs[:4], idx_ref)
        low = lanes((t, 128)) < 64

        def one(s, carry):
            at = pl.ds(pl.multiple_of(s * t, 16), t)
            folded = pl.ds(pl.multiple_of(tokens + s * (t // 2), 16), t // 2)
            for d in range(groups):
                rows = slice(d * t, (d + 1) * t)
                qk = slab[d, at, :].astype(F32)
                qs[rows, :] = jnp.where(low, qk * 0.125, 0.0).astype(BF)
                ks[rows, :] = swap64(qk).astype(BF)
                v = unfold_one(slab[d, folded, :].astype(F32))
                vt[:, rows] = jnp.where(low, v, 1.0).T.astype(BF)
            for d in range(groups):
                first = first_key(d, t)
                rows = slice(d * t, (d + 1) * t)
                start = doc_start(len_ref, s, d * t + lanes((1, t)), ndoc)
                blocks = []
                for b in range(first, d + 1):
                    scores = nt(ks[b * t : (b + 1) * t, :], qs[rows, :])
                    blocks.append(jnp.where(allowed(start, d, b, t), scores, -1e30))
                top = jnp.max(blocks[0], 0, keepdims=True)
                for block in blocks[1:]:
                    top = jnp.maximum(top, jnp.max(block, 0, keepdims=True))
                weight = jnp.concatenate([jnp.exp(block - top).astype(BF) for block in blocks], axis=0)
                o = nn(vt[:, first * t : (d + 1) * t], weight)
                total = o[64:65, :]
                lse_ref[s, d : d + 1, :] = top + jnp.log(total)
                o = o * (1.0 / total)
                ot_ref[s, d] = o[:64]
                osl[d, pl.ds(pl.multiple_of(s * (t // 2), 16), t // 2), :] = fold_one(o.T).astype(BF)
            return carry

        lax.fori_loop(0, ns, one, 0)
        store_slabs(outs, osl, idx_ref)

    shapes = slab_set(tokens // 2) + [sd(ns, 8, t, dtype=F32), sd(ns, groups, 64, t, dtype=F32)]
    out = call(
        kernel,
        "attention_forward",
        shapes,
        (idx, lengths, *slabs),
        [smem(), smem()] + [vm()] * 4,
        [
            pltpu.VMEM((groups, tokens + tokens // 2, 128), BF),
            pltpu.VMEM((full, 128), BF),
            pltpu.VMEM((full, 128), BF),
            pltpu.VMEM((128, full), BF),
            pltpu.VMEM((groups, tokens // 2, 128), BF),
        ],
        cost(4 * 4 * ns * full * full * 32, 4e6, ns * full * full // 2),
        after,
    )
    return out[:4], out[4:]


def attention_backward(geo, idx, slot, lengths, slabs, saved, d_slabs, after=()):
    groups, t, ns = geo.ranks, geo.t, geo.ns
    full, tokens, ndoc = groups * t, ns * t, lengths.shape[1]

    def kernel(idx_ref, len_ref, slot_ref, lse_ref, ot_ref, *refs):
        outs = refs[8:12]
        slab, gsl, qs, ks, kt, vs, right, delta, dvk, dq, dsl = refs[12:]
        load_slabs(slab, refs[:4], idx_ref)
        part = pl.ds(pl.multiple_of(slot_ref[0] * (tokens // 2), 128), tokens // 2)
        load_slabs(gsl, [ref.at[part] for ref in refs[4:8]], idx_ref)
        low = lanes((t, 128)) < 64

        def one(s, carry):
            at = pl.ds(pl.multiple_of(s * t, 16), t)
            folded = pl.ds(pl.multiple_of(tokens + s * (t // 2), 16), t // 2)
            o_rows = pl.ds(pl.multiple_of(s * (t // 2), 16), t // 2)
            for d in range(groups):
                rows = slice(d * t, (d + 1) * t)
                qk = slab[d, at, :].astype(F32)
                key = swap64(qk)
                q = jnp.where(low, qk * 0.125, 0.0)
                qs[rows, :] = q.astype(BF)
                ks[rows, :] = key.astype(BF)
                kt[:, rows] = key.T[:64].astype(BF)
                vs[rows, :] = unfold_one(slab[d, folded, :].astype(F32)).astype(BF)
                grad = jnp.where(low, unfold_one(gsl[d, o_rows, :].astype(F32)), 0.0)
                right[d, :t, :] = grad.astype(BF)
                right[d, t:, :] = swap64(q).astype(BF)
                delta[d : d + 1, :] = jnp.sum(grad.T[:64] * ot_ref[s, d], 0, keepdims=True)
            dvk[...] = jnp.zeros((full, 128), F32)
            for d in range(groups):
                rows = slice(d * t, (d + 1) * t)
                start = doc_start(len_ref, s, d * t + lanes((1, t)), ndoc)
                lse_row, delta_row = lse_ref[s, d : d + 1, :], delta[d : d + 1, :]
                total = jnp.zeros((64, t), F32)
                for b in range(first_key(d, t), d + 1):
                    keys = slice(b * t, (b + 1) * t)
                    scores = nt(ks[keys, :], qs[rows, :])
                    scores = jnp.where(allowed(start, d, b, t), scores, -1e30)
                    prob = jnp.exp(scores - lse_row)
                    d_prob = nt(vs[keys, :], right[d, :t, :])
                    ds = (prob * (d_prob - delta_row)).astype(BF)
                    dvk[keys, :] += nn(jnp.concatenate([prob.astype(BF), ds], axis=1), right[d])
                    total = total + nn(kt[:, keys], ds)
                dq[rows, :] = jnp.concatenate([total, total], axis=0).T * 0.125
            for d in range(groups):
                rows = slice(d * t, (d + 1) * t)
                both = dvk[rows, :]
                dsl[d, at, :] = merge64(dq[rows, :], both).astype(BF)
                dsl[d, folded, :] = fold_one(both).astype(BF)
            return carry

        lax.fori_loop(0, ns, one, 0)
        store_slabs(outs, dsl, idx_ref)

    slab_rows = tokens + tokens // 2
    flat = pltpu.VMEM((full, 128), BF)
    return call(
        kernel,
        "attention_backward",
        slab_set(slab_rows),
        (idx, lengths, jnp.array([slot], jnp.int32), *saved, *slabs, *d_slabs),
        [smem()] * 3 + [vm()] * 10,
        [
            pltpu.VMEM((groups, slab_rows, 128), BF),
            pltpu.VMEM((groups, tokens // 2, 128), BF),
            flat,
            flat,
            pltpu.VMEM((64, full), BF),
            flat,
            pltpu.VMEM((groups, 2 * t, 128), BF),
            pltpu.VMEM((8, t), F32),
            pltpu.VMEM((full, 128), F32),
            pltpu.VMEM((full, 128), F32),
            pltpu.VMEM((groups, slab_rows, 128), BF),
        ],
        cost(10 * 4 * ns * full * full * 32, 5e6, ns * full * full // 2),
        after,
    )


def mlp_forward(geo, idx, o_slabs, residual, out_grad, gain, out_bias, fc_bias, proj_bias, weights):
    groups, t, ns, narrow = geo.ranks, geo.t, geo.ns, geo.narrow
    wide, ff, tokens = geo.wide, geo.ff, geo.ns * geo.t
    n_slab, blocks = len(o_slabs), geo.ff // geo.wide
    rows = (wide // geo.fsdp) // (2 if geo.fast else 1)
    shares = wide // rows
    proj_shapes = part_shapes(geo, ff, wide)
    chunk = 512
    size_z = geo.fsdp // 2 if geo.fast else 1
    per_z = ff // size_z

    def kernel(idx_ref, *refs):
        slabs, refs = refs[:n_slab], refs[n_slab:]
        x_ref, og_ref, gain_ref, ob_ref, fb_ref, pb_ref = refs[:6]
        w_refs, refs = refs[6 : 6 + len(weights)], refs[6 + len(weights) :]
        out_ref, dpre_out, n_out, a_out, ogp_out, mid_out, bias_ref, wo_out, dn_ref = refs[:9]
        p_refs = refs[9 : 9 + len(proj_shapes)]
        refs = refs[9 + len(proj_shapes) :]
        wf, wp, osl, acc, tile, dpre_ref, n_ref, a_ref, ogp_ref, mid_ref, wo_ref, sem = refs
        early = [
            pltpu.make_async_copy(src, dst, sem.at[3 + i])
            for i, (src, dst) in enumerate(
                (
                    (ogp_ref, ogp_out),
                    (wo_ref, wo_out),
                    (a_ref, a_out),
                    (mid_ref, mid_out),
                    (n_ref, n_out),
                )
            )
        ]

        def d_pre_copy(i):
            cols = pl.ds(pl.multiple_of(i * chunk, 128), chunk)
            return pltpu.make_async_copy(dpre_ref.at[:, cols], dpre_out.at[:, cols], sem.at[8])

        def part_copies(zz):
            if not geo.fast:
                rows = pl.ds(zz * per_z, per_z)
                return [pltpu.make_async_copy(tile.at[rows], p_refs[0].at[rows], sem.at[9])]
            n = per_z // 4
            made = []
            for dx in range(2):
                for dc in range(2):
                    start = zz * per_z + ((idx_ref[1] ^ dx) * 2 + (idx_ref[3] ^ dc)) * n
                    made.append(
                        pltpu.make_async_copy(
                            tile.at[pl.ds(pl.multiple_of(start, 16), n)],
                            p_refs[dc].at[pl.ds((dx * size_z + zz) * n, n)],
                            sem.at[9],
                        )
                    )
            return made

        if geo.fast:
            (all_ref,) = w_refs
            out_src, fc_src = all_ref.at[:, pl.ds(0, wide)], all_ref.at[:, pl.ds(wide, ff)]
            to_proj = [
                pltpu.make_async_copy(
                    all_ref.at[pl.ds(share * rows, rows), pl.ds(wide + ff + i * wide, wide)],
                    wp.at[pl.ds((share * blocks + i) * rows, rows)],
                    sem.at[2],
                )
                for share in range(shares)
                for i in range(blocks)
            ]
        else:
            out_src, fc_src, proj_src = w_refs
            to_proj = [pltpu.make_async_copy(proj_src, wp, sem.at[2])]
        to_out = pltpu.make_async_copy(out_src, wp.at[pl.ds(0, wide)], sem.at[0])
        to_fc = pltpu.make_async_copy(fc_src, wf, sem.at[1])
        to_out.start()
        to_fc.start()
        for i in range(3):
            load_slabs(osl, slabs[4 * i : 4 * i + 4], idx_ref, i * groups)

        def load(s, carry):
            at = pl.ds(pl.multiple_of(s * t, 16), t)
            acc[at, :] = jnp.zeros((t, wide), F32)
            acc[at, :narrow] = og_ref[s].astype(F32)
            ogp_ref[at, :] = acc[at, :].astype(BF)
            acc[at, :narrow] = x_ref[s].astype(F32)
            dn_ref[at, :] = jnp.zeros((t, wide), F32)
            return carry

        lax.fori_loop(0, ns, load, 0)
        early[0].start()

        def assemble(i, carry):
            for p in range(groups // 2):
                at = pl.ds(pl.multiple_of(i * 64 * groups + 128 * p, 128), 128)
                for s in range(ns):
                    folded = slice(s * (t // 2), (s + 1) * (t // 2))
                    a_ref[s * t : (s + 1) * t, at] = unfold_pair(
                        osl[i * groups + 2 * p, folded, :].astype(F32),
                        osl[i * groups + 2 * p + 1, folded, :].astype(F32),
                    ).astype(BF)
            return carry

        lax.fori_loop(0, 3, assemble, 0)
        to_out.wait()
        for slot in range(3):
            for g in range(groups):
                at, head = 64 * (slot * groups + g), 3 * g + slot
                wo_ref[at : at + 64, :] = wp[64 * head : 64 * (head + 1), :]
        for copy in to_proj + early[1:3]:
            copy.start()

        def project(i, carry):
            cols = pl.ds(pl.multiple_of(i * 256, 128), 256)
            acc[:, cols] += nn(a_ref[...], wo_ref[:, cols]) + ob_ref[:, cols]
            return carry

        lax.fori_loop(0, wide // 256, project, 0)

        def norm(s, carry):
            at = pl.ds(pl.multiple_of(s * t, 16), t)
            full, inv = norm_rows(acc[at, :], narrow, wide)
            mid_ref[at, :] = full
            n_ref[at, :] = (full * inv * gain_ref[...]).astype(BF)
            return carry

        lax.fori_loop(0, ns, norm, 0)
        for copy in early[3:]:
            copy.start()
        to_fc.wait()
        for copy in to_proj:
            copy.wait()

        def one(i, carry):
            cols = pl.ds(pl.multiple_of(i * chunk, 128), chunk)
            w1, w2 = wf[:, cols], wp[cols, :]
            u = nn(n_ref[...], w1) + fb_ref[:, cols]
            square = u * u
            th = jnp.tanh(u * (GELU_K + GELU_K * GELU_C * square))
            half = 0.5 + 0.5 * th
            hidden = (u * half).astype(BF)
            slope = half + (0.5 * u) * (1.0 - th * th) * (GELU_K + 3.0 * GELU_K * GELU_C * square)
            acc[...] += nn(hidden, w2)
            d_pre = (nt(ogp_ref[...], w2) * slope).astype(BF)
            dpre_ref[:, cols] = d_pre
            d_pre_copy(i).start()
            bias_ref[0:1, cols] = jnp.sum(d_pre.astype(F32), 0, keepdims=True)
            dn_ref[...] += nt(d_pre, w1)
            tile[cols, :] = tn(hidden, ogp_ref[...]).astype(BF)
            for zz in range(size_z):

                @pl.when(i == ((zz + 1) * per_z - 1) // chunk)
                def _(zz=zz):
                    for copy in part_copies(zz):
                        copy.start()

            return carry

        lax.fori_loop(0, ff // chunk, one, 0)

        def store(s, carry):
            at = pl.ds(pl.multiple_of(s * t, 16), t)
            out_ref[s] = (acc[at, :] + pb_ref[...])[:, :narrow].astype(BF)
            return carry

        lax.fori_loop(0, ns, store, 0)
        for copy in early + [d_pre_copy(i) for i in range(ff // chunk)]:
            copy.wait()
        for zz in range(size_z):
            for copy in part_copies(zz):
                copy.wait()

    shapes = [
        sd(ns, t, narrow),
        sd(tokens, ff),
        sd(tokens, wide),
        sd(tokens, wide),
        sd(tokens, wide),
        sd(tokens, wide, dtype=F32),
        sd(8, ff, dtype=F32),
        sd(wide, wide),
        sd(tokens, wide, dtype=F32),
    ]
    out = call(
        kernel,
        "mlp_forward",
        shapes + proj_shapes,
        (idx, *o_slabs, residual, out_grad, gain, out_bias, fc_bias, proj_bias, *weights),
        [smem()] + [vm()] * (n_slab + 6) + [anyspace()] * len(weights),
        [
            pltpu.VMEM((wide, ff), BF),
            pltpu.VMEM((ff, wide), BF),
            pltpu.VMEM((3 * groups, tokens // 2, 128), BF),
            pltpu.VMEM((tokens, wide), F32),
            pltpu.VMEM((ff, wide), BF),
            pltpu.VMEM((tokens, ff), BF),
            pltpu.VMEM((tokens, wide), BF),
            pltpu.VMEM((tokens, wide), BF),
            pltpu.VMEM((tokens, wide), BF),
            pltpu.VMEM((tokens, wide), F32),
            pltpu.VMEM((wide, wide), BF),
            pltpu.SemaphoreType.DMA((10,)),
        ],
        cost(2 * tokens * wide * (5 * ff + wide), 34e6, tokens * ff),
        out_specs=tuple(
            vm() if i in (0, 6, 8) else anyspace() for i in range(len(shapes) + len(proj_shapes))
        ),
    )
    return out[: len(shapes)], out[len(shapes) :]


def mlp_backward(geo, idx, d_norm, out_w, og, middle, gain, bias_sums):
    groups, t, ns, narrow = geo.ranks, geo.t, geo.ns, geo.narrow
    wide, ff, tokens = geo.wide, geo.ff, geo.ns * geo.t
    n_slab = 4

    def kernel(idx_ref, dn, wo_ref, og_ref, mid_ref, gain_ref, bias_ref, *refs):
        db_ref, dmid_ref, vec_ref = refs[:3]
        outs = refs[3 : 3 + n_slab]
        da, dsl = refs[3 + n_slab :]
        vec_ref[0:1, :] = bias_ref[0:1, :]
        vec_ref[1:8, :] = jnp.zeros((7, ff), F32)

        def norm(s, carry):
            at = pl.ds(pl.multiple_of(s * t, 16), t)
            full = mid_ref[at, :]
            inv = lax.rsqrt(jnp.sum(full * full, 1, keepdims=True) * (1.0 / wide) + EPS)
            m, grad = full * inv, dn[at, :]
            dm = grad * gain_ref[...]
            d_full = inv * (dm - m * (jnp.sum(dm * m, 1, keepdims=True) * (1.0 / wide)))
            last = jnp.sum(jnp.where(lanes((t, wide)) == narrow, d_full, 0.0), 1, keepdims=True)
            og_f = og_ref[at, :].astype(F32)
            d_mid = og_f + (d_full - last)
            d_branch = d_mid.astype(BF)
            dmid_ref[at, :] = d_mid
            db_ref[at, :] = d_branch
            vec_ref[1:2, :wide] += jnp.sum(grad * m, 0, keepdims=True)
            vec_ref[2:3, :wide] += jnp.sum(d_branch.astype(F32), 0, keepdims=True)
            vec_ref[3:4, :wide] += jnp.sum(og_f, 0, keepdims=True)
            da[at, :] = nt(d_branch, wo_ref[...])
            return carry

        lax.fori_loop(0, ns, norm, 0)

        def fold(i, carry):
            for p in range(groups // 2):
                at = pl.ds(pl.multiple_of(i * 64 * groups + 128 * p, 128), 128)
                for s in range(ns):
                    pair = fold_pair(da[s * t : (s + 1) * t, at])
                    for half in range(2):
                        dest = pl.multiple_of(i * (tokens // 2) + s * (t // 2), 16)
                        dsl[2 * p + half, pl.ds(dest, t // 2), :] = pair[half].astype(BF)
            return carry

        lax.fori_loop(0, 3, fold, 0)
        store_slabs(outs, dsl, idx_ref)

    out = call(
        kernel,
        "mlp_backward",
        [sd(tokens, wide), sd(tokens, wide, dtype=F32), sd(8, ff, dtype=F32)] + slab_set(3 * tokens // 2),
        (idx, d_norm, out_w, og, middle, gain, bias_sums),
        [smem()] + [vm()] * 6,
        [
            pltpu.VMEM((tokens, wide), F32),
            pltpu.VMEM((groups, 3 * tokens // 2, 128), BF),
        ],
        cost(2 * tokens * wide * wide, 12e6),
    )
    return out[:3], out[3:]


def part_shapes(geo, rows, cols):
    return [sd(rows // 2, cols)] * 2 if geo.fast else [sd(rows, cols)]


def emit_rows(geo, idx_ref, outs, tile, total, cols, relative):
    if not geo.fast:
        outs[0][:, cols] = tile[...]
        return
    size_z = geo.fsdp // 2
    n = total // geo.fsdp // 2
    for dx in range(2):
        for zz in range(size_z):
            z = idx_ref[0] ^ zz if relative else zz
            for dc in range(2):
                start = ((z * 2 + (idx_ref[1] ^ dx)) * 2 + (idx_ref[3] ^ dc)) * n
                at = (dx * size_z + zz) * n
                outs[dc][at : at + n, cols] = tile[pl.ds(pl.multiple_of(start, 16), n), :]


def grad_fo(geo, idx, attn, d_branch, normed, d_pre, after=()):
    tokens, ff = d_pre.shape
    wide, groups, chunk = geo.wide, geo.ranks, 768
    shapes = part_shapes(geo, wide, wide + ff)

    def kernel(idx_ref, a_ref, db_ref, n_ref, dp_ref, *refs):
        outs, (trans, tile, nat) = refs[:-3], refs[-3:]
        trans[...] = n_ref[...].T
        nat[...] = tn(a_ref[...], db_ref[...]).astype(BF)
        for slot in range(3):
            for g in range(groups):
                at, head = 64 * (slot * groups + g), 3 * g + slot
                tile[64 * head : 64 * (head + 1), :] = nat[at : at + 64, :]
        emit_rows(geo, idx_ref, outs, tile, wide, slice(0, wide), False)

        def one(i, carry):
            at = pl.multiple_of(i * chunk, 128)
            tile[...] = nn(trans[...], dp_ref[:, pl.ds(at, chunk)]).astype(BF)
            emit_rows(geo, idx_ref, outs, tile, wide, pl.ds(at + wide, chunk), False)
            return carry

        lax.fori_loop(0, ff // chunk, one, 0)

    return call(
        kernel,
        "grad_fo",
        shapes,
        (idx, attn, d_branch, normed, d_pre),
        [smem()] + [vm()] * 4,
        [
            pltpu.VMEM((wide, tokens), BF),
            pltpu.VMEM((wide, wide), BF),
            pltpu.VMEM((wide, wide), BF),
        ],
        cost(2 * tokens * (ff + wide) * wide, 16e6),
        after,
    )


def grad_qkv(geo, idx, slabs, trans, last=False, after=()):
    groups, t, ns, wide = geo.ranks, geo.t, geo.ns, geo.wide
    slots, tokens = len(slabs) // 4, geo.ns * geo.t
    shapes = part_shapes(geo, wide, slots * wide)
    by_y = last and geo.fast
    width = wide // 2 if by_y else wide
    if by_y:
        shapes = [sd(wide // 2, width), sd(wide // 2, width), sd(wide, width)]

    def kernel(idx_ref, *refs):
        ins, t_ref = refs[: slots * 4], refs[slots * 4]
        refs = refs[slots * 4 + 1 :]
        outs = refs[: len(shapes)]
        dt_ref, tile = refs[len(shapes)], refs[len(shapes) + 1]
        slab = refs[-1]
        for i in range(slots):
            load_slabs(slab.at[i], ins[4 * i : 4 * i + 4], idx_ref)

        def one(i, carry):
            base = pl.multiple_of(i * wide, 128)
            for g in range(groups):
                dt_ref[:, pl.ds(base + 128 * g, 128)] = slab[i, g, :tokens, :]
            for p in range(groups // 2):
                at = pl.ds(base + 128 * (groups + p), 128)
                for s in range(ns):
                    folded = slice(tokens + s * (t // 2), tokens + (s + 1) * (t // 2))
                    dt_ref[s * t : (s + 1) * t, at] = unfold_pair(
                        slab[i, 2 * p, folded, :].astype(F32), slab[i, 2 * p + 1, folded, :].astype(F32)
                    ).astype(BF)
            return carry

        def multiply(i, carry):
            at = pl.ds(pl.multiple_of(i * width, 128), width)
            tile[...] = nn(t_ref[...], dt_ref[:, at]).astype(BF)
            emit_rows(geo, idx_ref, outs, tile, wide, at, True)
            return carry

        def multiply_half(i):
            at = pl.ds(pl.multiple_of((idx_ref[2] ^ i) * width, 128), width)
            tile[...] = nn(t_ref[...], dt_ref[:, at]).astype(BF)
            pair = (outs[i], outs[2].at[pl.ds(i * (wide // 2), wide // 2)])
            emit_rows(geo, idx_ref, pair, tile, wide, slice(0, width), True)

        lax.fori_loop(0, slots, one, 0)
        if by_y:
            multiply_half(0)
            multiply_half(1)
        else:
            lax.fori_loop(0, slots * wide // width, multiply, 0)

    out = call(
        kernel,
        "grad_qkv",
        shapes + [sd(tokens, slots * wide)],
        (idx, *slabs, trans),
        [smem()] + [vm()] * (slots * 4 + 1),
        [
            pltpu.VMEM((wide, width), BF),
            pltpu.VMEM((slots, groups, tokens + tokens // 2, 128), BF),
        ],
        cost(2 * tokens * slots * wide * wide, 4e6 * slots),
        after,
    )
    return out[:-1], out[-1]


def input_backward(geo, residual, gain, d_tokens, weights, d_mid, vectors, after=()):
    ns, t, narrow, wide, ff = geo.ns, geo.t, geo.narrow, geo.wide, geo.ff
    tokens, n, nw = ns * t, len(d_tokens), len(weights)

    def kernel(x_ref, gain_ref, dmid_ref, v_ref, *refs):
        dts, ws, (o_ref, vec_ref, row) = refs[:n], refs[n : n + nw], refs[n + nw :]
        vec_ref[...] = jnp.zeros(vec_ref.shape, F32)
        for i in range(3):
            vec_ref[1 + i : 2 + i, :] = v_ref[1 + i : 2 + i, :wide]
        for i in range(ff // wide):
            vec_ref[4 + i : 5 + i, :] = v_ref[0:1, i * wide : (i + 1) * wide]
        row[...] = jnp.zeros((t, wide), F32)
        slots = lambda refs: [
            (ref, slice(j * wide, (j + 1) * wide)) for ref in refs for j in range(ref.shape[1] // wide)
        ]

        def one(s, carry):
            rows = pl.ds(pl.multiple_of(s * t, 16), t)
            row[:, :narrow] = x_ref[s].astype(F32)
            full, inv = norm_rows(row[...], narrow, wide)
            grad = jnp.zeros((t, wide), F32)
            for i, ((dt, cols), (w, w_cols)) in enumerate(zip(slots(dts), slots(ws))):
                d_tok = dt[rows, cols]
                vec_ref[8 + i : 9 + i, :] += jnp.sum(d_tok.astype(F32), 0, keepdims=True)
                grad = grad + nt(d_tok, w[:, w_cols])
            m = full * inv
            vec_ref[0:1, :] += jnp.sum(grad * m, 0, keepdims=True)
            dm = grad * gain_ref[...]
            d_full = inv * (dm - m * (jnp.sum(dm * m, 1, keepdims=True) * (1.0 / wide)))
            last = jnp.sum(jnp.where(lanes((t, wide)) == narrow, d_full, 0.0), 1, keepdims=True)
            o_ref[s] = (dmid_ref[rows, :] + (d_full - last))[:, :narrow]
            return carry

        lax.fori_loop(0, ns, one, 0)

    return call(
        kernel,
        "input_backward",
        [sd(ns, t, narrow, dtype=F32), sd(16, wide, dtype=F32)],
        (residual, gain, d_mid, vectors, *d_tokens, *weights),
        [vm()] * (4 + n + nw),
        [pltpu.VMEM((t, wide), F32)],
        cost(2 * tokens * 3 * wide * wide, 14e6),
        after,
    )


def finish(geo, idx, pairs, plan, name):
    n = len(pairs)
    half = pairs[0][0].shape[0]
    rows = 2 * half if geo.fast else half
    sides = 2 if geo.fast else 1

    def kernel(idx_ref, *refs):
        outs = refs[n * sides :]
        for side in range(sides):
            at = pl.ds(pl.multiple_of((idx_ref[3] ^ side) * half, 8), half) if geo.fast else slice(0, rows)
            plan([refs[i * sides + side] for i in range(n)], outs, at)

    return lambda shapes: call(
        kernel,
        name,
        shapes,
        (idx, *[a for pair in pairs for a in pair[:sides]]),
        [smem()] + [vm()] * (n * sides),
        [],
        cost(0, rows * 3072 * 6),
    )


def finish_qkv(geo, idx, first, last):
    half, cols = first[0].shape
    wide = geo.wide
    rows, sides = (2 * half, 2) if geo.fast else (half, 1)
    where = {unit: at for at, unit in enumerate(unit_order(geo.ranks))}
    first = first[:sides]

    def kernel(idx_ref, *refs):
        a_refs, b_refs, (o_ref, b_all) = refs[:sides], refs[sides:-2], refs[-2:]
        for side in range(sides):
            at = pl.ds(pl.multiple_of((idx_ref[3] ^ side) * half, 8), half) if geo.fast else slice(0, rows)
            if geo.fast:
                for i in range(2):
                    cut = pl.ds(pl.multiple_of((idx_ref[2] ^ i) * (wide // 2), 128), wide // 2)
                    b_all[:, cut] = b_refs[2 * side + i][...].astype(F32)
            else:
                b_all[...] = b_refs[0][...].astype(F32)

            def read(b, a_ref=a_refs[side]):
                if b < cols // 128:
                    return a_ref[:, b * 128 : (b + 1) * 128].astype(F32)
                return b_all[:, b * 128 - cols : (b + 1) * 128 - cols]

            for j in range(3 * wide // 128):
                o_ref[at, j * 128 : (j + 1) * 128] = pick_units(read, where[2 * j], where[2 * j + 1])

    return call(
        kernel,
        "finish_qkv",
        sd(rows, 3 * wide, dtype=F32),
        (idx, *first, *last),
        [smem()] + [vm()] * (len(first) + len(last)),
        [pltpu.VMEM((half, wide), F32)],
        cost(0, rows * 3072 * 6),
    )


def add_bf(*terms):
    total = terms[0].astype(F32)
    for term in terms[1:]:
        total = total + term.astype(F32)
    return total.astype(BF)


def xor_pairs(size, step):
    return [(i, i ^ step) for i in range(size)]


class Reduction:
    def __init__(self, geo, stages, parts, pieces):
        self.st, self.parts, self.fast = stages, parts, geo.fast
        self.size_z = geo.fsdp // 2
        self.from_x, self.terms = [], []
        if self.fast:
            self.n = parts[0].shape[0] // 2
            self.m = self.n // self.size_z
            ends = [round(self.n * sum(pieces[: i + 1]) / sum(pieces)) for i in range(len(pieces))]
            self.cuts = [e // self.m * self.m for e in ends]
            self.cuts = list(zip([0] + self.cuts, self.cuts))

    def over_cores(self):
        if self.fast:
            self.got = self.st.permute(self.parts[1], "c")
            return self.got

    def over_x(self):
        if self.fast:
            first, last = (self.n + at for at in self.cuts[len(self.from_x)])
            keep = self.st.now(self.parts[0])
            half = add_bf(keep[first:last], self.got[first:last])
            self.from_x.append(lax.ppermute(half, "x", SWAP))
            return self.from_x[-1]

    def over_z(self, *steps):
        if not self.fast:
            return self.scatter_z() if 0 in steps else None
        keep, m, sent = self.st.now(self.parts[0]), self.m, []
        for k in steps:
            rows = slice(k * m, (k + 1) * m)
            term = add_bf(keep[rows], self.got[rows], self.from_x[0][rows])
            if k:
                sent.append(lax.ppermute(term, "z", xor_pairs(self.size_z, k)))
            self.terms.append(sent[-1] if k else term)
        return sent or self.terms

    def scatter_z(self):
        part = self.st.now(self.parts[0])
        if self.fast:
            part = jnp.concatenate(
                [
                    add_bf(part[first:last], self.got[first:last], sent)
                    for (first, last), sent in zip(self.cuts, self.from_x)
                ],
                axis=0,
            )
            self.terms = [lax.psum_scatter(part, "z", scatter_dimension=0, tiled=True)]
        else:
            self.terms = [lax.psum_scatter(part, ("z", "x"), scatter_dimension=0, tiled=True)]

    def over_y(self, *after):
        if self.fast:
            self.share = lax.optimization_barrier((self.st.now(self.terms[0]), *after))[0]
            if len(self.terms) > 1:
                self.share = add_bf(self.share, *self.terms[1:])
            self.got_y = lax.ppermute(self.share, "y", SWAP)
            return self.got_y

    def total(self):
        if not self.fast:
            return lax.psum(self.terms[0], ("y", "c")), None
        total = add_bf(self.st.now(self.share), self.got_y)
        return total, lax.ppermute(total, "c", SWAP)


class LastReduction:
    def __init__(self, geo, stages, parts):
        self.geo, self.st, self.parts, self.fast = geo, stages, parts, geo.fast
        self.size_z = geo.fsdp // 2

    def over_cores(self):
        if self.fast:
            self.got = self.st.permute(self.parts[2], "c")
            return self.got

    def over_y(self):
        if self.fast:
            n = self.parts[0].shape[0]
            half = add_bf(self.st.now(self.parts[1]), self.got[n:])
            self.from_y = lax.ppermute(half, "y", SWAP)
            return self.from_y

    def over_x(self):
        if self.fast:
            n = self.parts[0].shape[0] // 2
            keep = self.st.now(self.parts[0])
            half = add_bf(keep[n:], self.got[n : 2 * n], self.from_y[n:])
            self.from_x = lax.ppermute(half, "x", SWAP)
            return self.from_x

    def over_z(self):
        if not self.fast:
            part = self.st.now(self.parts[0])
            self.terms = [lax.psum_scatter(part, ("z", "x"), scatter_dimension=0, tiled=True)]
            return self.terms
        m = self.parts[0].shape[0] // 2 // self.size_z
        keep = self.st.now(self.parts[0])
        self.terms = []
        for k in range(self.size_z):
            rows = slice(k * m, (k + 1) * m)
            term = add_bf(keep[rows], self.got[rows], self.from_y[rows], self.from_x[rows])
            self.terms.append(lax.ppermute(term, "z", xor_pairs(self.size_z, k)) if k else term)
        return self.terms

    def back_over_y(self):
        if self.fast:
            self.share = add_bf(self.st.now(self.terms[0]), *self.terms[1:])
            self.other = lax.ppermute(self.share, "y", SWAP)
            return self.other

    def total(self):
        if not self.fast:
            return [lax.psum(self.terms[0], ("y", "c"))]
        both = [self.share, self.other]
        return both + [self.st.permute(part, "c") for part in both]


def fold_in(v, axis, size, step=1):
    return v + lax.ppermute(v, axis, xor_pairs(size, step))


def gather_whole(own):
    return Parts([lax.all_gather(own, ("z", "x"), axis=0, tiled=True)])


class Geometry:
    pass


def local(
    geo,
    residual,
    out_grad,
    lengths,
    gain_one,
    qkv_weight,
    qv_bias,
    out_weight,
    out_bias,
    gain_two,
    fc_weight,
    fc_bias,
    proj_weight,
    proj_bias,
):
    geo.ranks = geo.seq
    geo.ns, geo.t, geo.narrow = residual.shape
    geo.wide, geo.ff = geo.narrow + 1, fc_weight.shape[1]
    narrow, wide, groups, ff = geo.narrow, geo.wide, geo.ranks, geo.ff
    heads, e = qv_bias.shape[0], qv_bias.shape[1] // 2
    size_z = geo.fsdp // 2
    geo.fast = (
        wide // geo.fsdp % 32 == 0
        and size_z & (size_z - 1) == 0
        and wide % (ff // size_z) == 0
        and ff // size_z % 64 == 0
    )
    z, x, y, c = (lax.axis_index(a) for a in ("z", "x", "y", "c"))
    idx = jnp.stack([z, x, y, c, 2 * y + c, z, z, z]).astype(jnp.int32)
    pad = lambda v: jnp.pad(v, (0, wide - narrow)).reshape(1, wide)
    gain1, gain2 = gain_one.reshape(1, wide), gain_two.reshape(1, wide)

    by_slot = qv_bias.reshape(groups, 3, 2 * e).transpose(1, 0, 2)
    q_bias = jnp.pad(by_slot[:, :, :e], ((0, 0), (0, 0), (0, e))).reshape(3, -1)
    bias = jnp.concatenate([q_bias, by_slot[:, :, e:].reshape(3, -1)], axis=1).reshape(1, -1)

    st = Stages(idx)
    own = prep_qkv(geo, idx, qkv_weight)
    bias_a, bias_b = bias[:, :wide], bias[:, wide:]
    if geo.fast:
        sides = [(dx, dc, 0, size_z, True) for dc in range(2) for dx in range(2)]
        whole = [own] + [lax.ppermute(own, "z", xor_pairs(size_z, i)) for i in range(1, size_z)]
        rest_own = prep_rest(geo, idx, out_weight, fc_weight, proj_weight)
        rest_own = lax.optimization_barrier((rest_own, whole[-1]))[0]
        rest = [lax.all_gather(rest_own, ("z", "x", "c"), axis=0, tiled=True)]
        st.end(whole)
        rows_a, rows_b = (
            jnp.concatenate([w[:, cut] for w in whole], axis=0)
            for cut in (slice(0, wide), slice(wide, 3 * wide))
        )
        other_a = st.permute(rows_a, "x")
        st.end(other_a)
        other_b = st.permute(rows_b, "x")
        w_a = [rows_a, other_a, st.permute(rows_a, "c"), st.permute(other_a, "c")]
        st.end(w_a)
        w_a = Parts(w_a, sides)
    else:
        w_a = gather_whole(own[:, :wide])
        w_b = gather_whole(own[:, wide:])
        widen = lambda w: jnp.pad(w, ((0, 0), (0, wide - narrow))).astype(BF)
        rest = [
            gather_whole(w).arrays[0]
            for w in (widen(out_weight), fc_weight.astype(BF), widen(proj_weight))
        ]
    sends, wq_a, (normed_one, normed_t) = qkv_forward(
        geo, st.token, residual, gain1, bias_a, w_a, (0,), True
    )
    st.end(sends)
    if geo.fast:
        w_b = Parts([rows_b, other_b, st.permute(rows_b, "c"), st.permute(other_b, "c")], sides)
    sends_b, wq_b, _ = qkv_forward(geo, idx, normed_one, gain1, bias_b, w_b, (1, 2), False)
    sends = list(sends) + list(sends_b)
    free = Stages(idx)
    slabs, saved, o_slabs = [], [], []
    for i in range(3):
        slabs.append(free.exchange(sends[4 * i : 4 * i + 4]))
    for i in range(3):
        o, stats = attention_forward(geo, idx, lengths, slabs[i])
        saved.append(stats)
        o_slabs += free.exchange(o)
    st.end(o_slabs)
    (output, d_pre, normed_two, attn, og, middle, bias_sums, out_w, d_norm), proj_parts = mlp_forward(
        geo,
        st.token,
        o_slabs,
        residual,
        out_grad,
        gain2,
        pad(out_bias),
        fc_bias.reshape(1, ff),
        pad(proj_bias),
        rest,
    )
    st.end(proj_parts)
    proj_red = Reduction(geo, st, proj_parts, (1, 1))
    got = proj_red.over_cores()
    (d_branch, d_mid, vectors), d_sends = mlp_backward(
        geo, st.token, d_norm, out_w, og, middle, gain2, bias_sums
    )
    st.end(got, d_branch)
    d_slabs = st.exchange(d_sends)
    got = proj_red.over_x()
    fo_red = Reduction(geo, st, grad_fo(geo, st.token, attn, d_branch, normed_two, d_pre), (1, 1))
    st.end(d_slabs, got, fo_red.parts)
    got = proj_red.over_x(), fo_red.over_cores()
    dq = attention_backward(geo, st.token, 0, lengths, slabs[0], saved[0], d_slabs)
    st.end(got, dq)
    dq_slabs = [st.exchange(dq)]
    proj_red.scatter_z()
    got = fo_red.over_x()
    dq = attention_backward(geo, st.token, 1, lengths, slabs[1], saved[1], d_slabs)
    st.end(got, dq, dq_slabs)
    dq_slabs.append(st.exchange(dq))
    got = fo_red.over_x()
    dq = attention_backward(geo, st.token, 2, lengths, slabs[2], saved[2], d_slabs)
    st.end(got, dq, dq_slabs)
    dq_slabs.append(st.exchange(dq))
    fo_red.scatter_z()
    parts_a, dt_a = grad_qkv(geo, st.token, dq_slabs[0] + dq_slabs[1], normed_t)
    red_a = Reduction(geo, st, parts_a, (1,))
    st.end(dq_slabs, parts_a)
    got = red_a.over_cores()
    parts_b, dt_b = grad_qkv(geo, st.token, dq_slabs[2], normed_t, last=True)
    red_b = LastReduction(geo, st, parts_b)
    st.end(got, parts_b)
    got = red_a.over_x(), proj_red.over_y(), red_b.over_cores(), red_b.over_y()
    input_grad, vecs = input_backward(
        geo,
        st.now(residual),
        gain1,
        (dt_a, dt_b),
        (wq_a, wq_b),
        d_mid,
        vectors,
    )
    if geo.fast:
        vecs = fold_in(vecs, "c", 2)
    else:
        vecs = lax.psum(vecs, ("z", "x", "y", "c"))
    st.end(got, vecs)
    got = red_a.over_z(*range(size_z)), red_b.over_x()
    if geo.fast:
        vecs = fold_in(st.now(vecs), "x", 2)
        got += (fo_red.over_y(vecs),)
    st.end(got, vecs)
    got = red_b.over_z(), red_a.over_y()
    proj_sum, fo_sum = proj_red.total(), fo_red.total()
    if geo.fast:
        vecs = fold_in(st.now(vecs), "y", 2)
    st.end(got, vecs, proj_sum, fo_sum)
    got = red_b.back_over_y()
    sum_a = red_a.total()
    if geo.fast:
        vecs = st.now(vecs)
        terms = [vecs] + [lax.ppermute(vecs, "z", xor_pairs(size_z, k)) for k in range(1, size_z)]
        while len(terms) > 1:
            terms = [a + b for a, b in zip(terms[::2], terms[1::2])]
        vecs = terms[0]
    st.end(got, vecs, sum_a)
    sum_b = red_b.total()
    sums = vecs[8:11].reshape(3, 3 * groups, e)
    q_sum = sums[:, : 2 * groups].reshape(3, groups, 2, e)[:, :, 0]
    v_sum = sums[:, 2 * groups :]
    qv_grad = jnp.concatenate([q_sum, v_sum], axis=2).transpose(1, 0, 2).reshape(heads, 2 * e)

    def plan_fo(ins, outs, at):
        outs[0][at, :] = ins[0][:, :narrow].astype(F32)
        outs[1][at, :] = ins[0][:, wide:].astype(F32)

    def plan_proj(ins, outs, at):
        outs[0][at, :] = ins[0][:, :narrow].astype(F32)

    block = wide // geo.fsdp
    qkv_grad = finish_qkv(geo, idx, sum_a, sum_b)
    out_w_grad, fc_w_grad = finish(geo, idx, [fo_sum], plan_fo, "finish_fo")(
        [sd(block, narrow, dtype=F32), sd(block, ff, dtype=F32)]
    )
    (proj_w_grad,) = finish(geo, idx, [proj_sum], plan_proj, "finish_proj")(
        [sd(ff // geo.fsdp, narrow, dtype=F32)]
    )
    return (
        output,
        input_grad,
        vecs[0],
        qkv_grad,
        qv_grad,
        out_w_grad,
        vecs[2, :narrow],
        vecs[1],
        fc_w_grad,
        vecs[4:8].reshape(-1),
        proj_w_grad,
        vecs[3, :narrow],
    )


def solution(mesh):
    geo = Geometry()
    geo.fsdp, geo.seq = mesh.devices.shape
    fine = Mesh(
        mesh.devices.reshape(geo.fsdp // 2, 2, geo.seq // 2, 2), ("z", "x", "y", "c")
    )
    fs, sq = ("z", "x"), ("y", "c")
    tokens, rows = P(fs, sq, None), P(fs, None)
    return jax.shard_map(
        functools.partial(local, geo),
        mesh=fine,
        in_specs=(
            tokens,
            tokens,
            rows,
            P(),
            rows,
            P(),
            rows,
            P(),
            P(),
            rows,
            P(),
            rows,
            P(),
        ),
        out_specs=(tokens, tokens, P(), rows, P(), rows, P(), P(), rows, P(), rows, P()),
        check_vma=False,
    )
```

```python
import functools

import jax
import jax.numpy as jnp
from jax import lax
from jax.experimental import pallas as pl
from jax.experimental.pallas import tpu as pltpu
from jax.sharding import Mesh, PartitionSpec as P

EPS = 1e-06
LONGEST = 512
BF = jnp.bfloat16
F32 = jnp.float32
VMEM_LIMIT = 60 * 1024 * 1024
SWAP = [(0, 1), (1, 0)]
GELU_K = 0.7978845608028654
GELU_C = 0.044715


def nn(a, b):
    return lax.dot_general(a, b, (((1,), (0,)), ((), ())), preferred_element_type=F32)


def nt(a, b):
    return lax.dot_general(a, b, (((1,), (1,)), ((), ())), preferred_element_type=F32)


def tn(a, b):
    return lax.dot_general(a, b, (((0,), (0,)), ((), ())), preferred_element_type=F32)


def lanes(shape):
    return lax.broadcasted_iota(jnp.int32, shape, 1)


def merge64(low, high):
    return jnp.where(lanes(low.shape) < 64, low, high)


def swap64(x):
    return pltpu.roll(x, 64, 1)


def fold_pair(x):
    n = x.shape[0] // 2
    top, bottom = x[:n], x[n:]
    return merge64(top, swap64(bottom)), merge64(swap64(top), bottom)


def unfold_pair(first, second):
    top = merge64(first, swap64(second))
    bottom = merge64(swap64(first), second)
    return jnp.concatenate([top, bottom], axis=0)


def vm():
    return pl.BlockSpec(memory_space=pltpu.VMEM)


def anyspace():
    return pl.BlockSpec(memory_space=pl.ANY)


def smem():
    return pl.BlockSpec(memory_space=pltpu.SMEM)


def cost(flops, nbytes, trans=0):
    scale = 0.1
    return pl.CostEstimate(
        flops=int(flops * scale), bytes_accessed=int(nbytes * scale), transcendentals=int(trans * scale)
    )


def params(**kw):
    return pltpu.CompilerParams(vmem_limit_bytes=VMEM_LIMIT, **kw)


def unit_order(groups):
    order = []
    for slot in range(3):
        for group in range(groups):
            order += [3 * (3 * group + slot), 3 * (3 * group + slot) + 1]
        for group in range(groups):
            order += [3 * (3 * group + slot) + 2]
    return order


def pick_units(load, low, high):
    def half(unit, side):
        block = load(unit // 2)
        return block if unit % 2 == side else swap64(block)

    return merge64(half(low, 0), half(high, 1))


def call(kernel, name, shapes, ins, specs, scratch, est, after=(), out_specs=None, **kw):
    if after:
        count, extra = len(ins), len(after)
        inner = kernel

        def kernel(*refs):
            inner(*refs[:count], *refs[count + extra :])

    many = isinstance(shapes, (tuple, list))
    return pl.pallas_call(
        kernel,
        out_shape=tuple(shapes) if many else shapes,
        in_specs=list(specs) + [anyspace()] * len(after),
        out_specs=out_specs or (tuple([vm()] * len(shapes)) if many else vm()),
        scratch_shapes=scratch,
        compiler_params=params(**kw),
        cost_estimate=est,
        name=name,
    )(*ins, *after)


def sd(*shape, dtype=BF):
    return jax.ShapeDtypeStruct(shape, dtype)


def prep_qkv(geo, idx, weight):
    rows = weight.shape[0] // 2 if geo.fast else weight.shape[0]
    width = weight.shape[1]
    order = unit_order(geo.ranks)

    def kernel(idx_ref, w_ref, o_ref):
        start = pl.multiple_of(idx_ref[3] * rows, 8) if geo.fast else 0
        for j in range(width // 128):
            o_ref[:, j * 128 : (j + 1) * 128] = pick_units(
                lambda b: w_ref[pl.ds(start, rows), b * 128 : (b + 1) * 128],
                order[2 * j],
                order[2 * j + 1],
            ).astype(BF)

    return call(
        kernel, "prep_qkv", sd(rows, width), (idx, weight), [smem(), vm()], [], cost(0, weight.size * 6)
    )


def prep_rest(geo, idx, out_w, fc_w, proj_w):
    div = 2 if geo.fast else 1
    rows = out_w.shape[0] // div
    wide, ff, narrow = geo.wide, fc_w.shape[1], out_w.shape[1]
    blocks = ff // wide

    def kernel(idx_ref, o_ref, f_ref, p_ref, all_ref):
        start = pl.multiple_of(idx_ref[3] * rows, 8) if geo.fast else 0
        pstart = pl.multiple_of(idx_ref[3] * rows * blocks, 8) if geo.fast else 0
        all_ref[...] = jnp.zeros(all_ref.shape, BF)
        all_ref[:, :narrow] = o_ref[pl.ds(start, rows), :].astype(BF)
        all_ref[:, wide : wide + ff] = f_ref[pl.ds(start, rows), :].astype(BF)
        for i in range(blocks):
            at = wide + ff + i * wide
            all_ref[:, at : at + narrow] = p_ref[pl.ds(pstart + i * rows, rows), :].astype(BF)

    return call(
        kernel,
        "prep_rest",
        sd(rows, wide + 2 * ff),
        (idx, out_w, fc_w, proj_w),
        [smem(), vm(), vm(), vm()],
        [],
        cost(0, 6 * (out_w.size + fc_w.size + proj_w.size)),
    )


class Parts:
    def __init__(self, arrays, coords=None):
        self.arrays, self.coords = list(arrays), coords

    def copies(self, geo, idx_ref, refs, dst, sem, src_cols=None):
        made = []
        if self.coords is None:
            src = refs[0] if src_cols is None else refs[0].at[:, src_cols]
            return [pltpu.make_async_copy(src, dst, sem)]
        for ref, (dx, dc, first, count, relative) in zip(refs, self.coords):
            n = ref.shape[0] // count
            for zz in range(count):
                z = idx_ref[0] ^ (first + zz) if relative else first + zz
                start = ((z * 2 + (idx_ref[1] ^ dx)) * 2 + (idx_ref[3] ^ dc)) * n
                rows = pl.ds(zz * n, n)
                src = ref.at[rows] if src_cols is None else ref.at[rows, src_cols]
                made.append(
                    pltpu.make_async_copy(src, dst.at[pl.ds(pl.multiple_of(start, 16), n)], sem)
                )
        return made


def norm_rows(x, narrow, wide):
    full = jnp.where(lanes(x.shape) == narrow, -jnp.sum(x, 1, keepdims=True), x)
    return full, lax.rsqrt(jnp.sum(full * full, 1, keepdims=True) * (1.0 / wide) + EPS)


def qkv_forward(geo, idx, source, gain, bias, parts, slots, first):
    groups, t, ns, narrow = geo.ranks, geo.t, geo.ns, geo.narrow
    wide, tokens = geo.wide, geo.ns * geo.t
    cols, slab_rows = len(slots) * geo.wide, tokens + tokens // 2
    count = len(parts.arrays)
    n_out = len(slots) * 4

    def kernel(idx_ref, x_ref, gain_ref, bias_ref, *refs):
        w_parts, outs = refs[:count], refs[count : count + n_out]
        refs = refs[count + n_out :]
        w_ref, refs = refs[0], refs[1:]
        if first:
            normed_ref, trans_ref, slab, sem, row = refs
        else:
            slab, sem = refs
            normed_ref = x_ref
        copies = parts.copies(geo, idx_ref, w_parts, w_ref, sem)
        for copy in copies:
            copy.start()
        if first:
            def norm(s, carry):
                at = pl.ds(pl.multiple_of(s * t, 16), t)
                row[at, :] = jnp.zeros((t, wide), F32)
                row[at, :narrow] = x_ref[s].astype(F32)
                full, inv = norm_rows(row[at, :], narrow, wide)
                normed_ref[at, :] = (full * inv * gain_ref[...]).astype(BF)
                return carry

            lax.fori_loop(0, ns, norm, 0)
            trans_ref[...] = normed_ref[...].T
        for copy in copies:
            copy.wait()

        def one(i, carry):
            base = pl.multiple_of(i * wide, 128)
            for j in range(groups // 2):
                at = pl.ds(base + 256 * j, 256)
                y = nn(normed_ref[...], w_ref[:, at]) + bias_ref[:, at]
                for half in range(2):
                    slab[i * groups + 2 * j + half, :tokens, :] = y[
                        :, half * 128 : (half + 1) * 128
                    ].astype(BF)
            at = pl.ds(base + 128 * groups, 64 * groups)
            y = nn(normed_ref[...], w_ref[:, at]) + bias_ref[:, at]
            for s in range(ns):
                rows = slice(tokens + s * (t // 2), tokens + (s + 1) * (t // 2))
                for p in range(groups // 2):
                    pair = fold_pair(y[s * t : (s + 1) * t, p * 128 : (p + 1) * 128])
                    for half in range(2):
                        slab[i * groups + 2 * p + half, rows, :] = pair[half].astype(BF)
            return carry

        lax.fori_loop(0, len(slots), one, 0)
        for i in range(len(slots)):
            store_slabs(outs[4 * i : 4 * i + 4], slab, idx_ref, i * groups)

    shapes = slab_set(slab_rows) * len(slots) + [sd(wide, cols)]
    scratch = [pltpu.VMEM((len(slots) * groups, slab_rows, 128), BF), pltpu.SemaphoreType.DMA]
    if first:
        shapes += [sd(tokens, wide), sd(wide, tokens)]
        scratch += [pltpu.VMEM((tokens, wide), F32)]
    out = call(
        kernel,
        "qkv_forward",
        shapes,
        (idx, source, gain, bias, *parts.arrays),
        [smem(), vm(), vm(), vm()] + [anyspace()] * count,
        scratch,
        cost(2 * tokens * wide * cols, 6e6),
    )
    return out[:n_out], out[n_out], out[n_out + 1 :]


def doc_start(len_ref, s, pos, ndoc):
    start = jnp.zeros(pos.shape, jnp.int32)
    edge = len_ref[s, 0]
    for n in range(1, ndoc):
        start = jnp.where(pos >= edge, edge, start)
        edge = edge + len_ref[s, n]
    return start


def first_key(block, t):
    return max(0, block * t - (LONGEST - 1)) // t


def allowed(start, block, key_block, t):
    k_pos = lax.broadcasted_iota(jnp.int32, (t, t), 0)
    seen = k_pos >= start - key_block * t
    if key_block == block:
        seen = seen & (k_pos <= lanes((1, t)))
    return seen


def store_slabs(outs, slab, idx_ref, base=0):
    for k, ref in enumerate(outs):
        ref[...] = slab[base + (idx_ref[4] ^ k)]


def load_slabs(slab, refs, idx_ref, base=0):
    for k, ref in enumerate(refs):
        slab[base + (idx_ref[4] ^ k)] = ref[...]


def slab_set(rows):
    return [sd(rows, 128)] * 4


class Stages:
    def __init__(self, idx):
        self.token = idx

    def end(self, *results):
        self.token = lax.optimization_barrier((self.token, *jax.tree.leaves(results)))[0]

    def now(self, x):
        return lax.optimization_barrier((x, self.token))[0]

    def permute(self, x, axis, pairs=SWAP):
        return lax.ppermute(self.now(x), axis, pairs)

    def exchange(self, slabs):
        return [slabs[0]] + [
            self.permute(slabs[k], ("y", "c"), xor_pairs(len(slabs), k)) for k in range(1, len(slabs))
        ]


def unfold_one(x):
    return jnp.concatenate([x, swap64(x)], axis=0)


def fold_one(x):
    n = x.shape[0] // 2
    return merge64(x[:n], swap64(x[n:]))


def attention_forward(geo, idx, lengths, slabs, after=()):
    groups, t, ns = geo.ranks, geo.t, geo.ns
    full, tokens, ndoc = groups * t, ns * t, lengths.shape[1]

    def kernel(idx_ref, len_ref, *refs):
        outs, lse_ref, ot_ref = refs[4:8], refs[8], refs[9]
        slab, qs, ks, vt, osl = refs[10:]
        load_slabs(slab, refs[:4], idx_ref)
        low = lanes((t, 128)) < 64

        def one(s, carry):
            at = pl.ds(pl.multiple_of(s * t, 16), t)
            folded = pl.ds(pl.multiple_of(tokens + s * (t // 2), 16), t // 2)
            for d in range(groups):
                rows = slice(d * t, (d + 1) * t)
                qk = slab[d, at, :].astype(F32)
                qs[rows, :] = jnp.where(low, qk * 0.125, 0.0).astype(BF)
                ks[rows, :] = swap64(qk).astype(BF)
                v = unfold_one(slab[d, folded, :].astype(F32))
                vt[:, rows] = jnp.where(low, v, 1.0).T.astype(BF)
            for d in range(groups):
                first = first_key(d, t)
                rows = slice(d * t, (d + 1) * t)
                start = doc_start(len_ref, s, d * t + lanes((1, t)), ndoc)
                blocks = []
                for b in range(first, d + 1):
                    scores = nt(ks[b * t : (b + 1) * t, :], qs[rows, :])
                    blocks.append(jnp.where(allowed(start, d, b, t), scores, -1e30))
                top = jnp.max(blocks[0], 0, keepdims=True)
                for block in blocks[1:]:
                    top = jnp.maximum(top, jnp.max(block, 0, keepdims=True))
                weight = jnp.concatenate([jnp.exp(block - top).astype(BF) for block in blocks], axis=0)
                o = nn(vt[:, first * t : (d + 1) * t], weight)
                total = o[64:65, :]
                lse_ref[s, d : d + 1, :] = top + jnp.log(total)
                o = o * (1.0 / total)
                ot_ref[s, d] = o[:64]
                osl[d, pl.ds(pl.multiple_of(s * (t // 2), 16), t // 2), :] = fold_one(o.T).astype(BF)
            return carry

        lax.fori_loop(0, ns, one, 0)
        store_slabs(outs, osl, idx_ref)

    shapes = slab_set(tokens // 2) + [sd(ns, 8, t, dtype=F32), sd(ns, groups, 64, t, dtype=F32)]
    out = call(
        kernel,
        "attention_forward",
        shapes,
        (idx, lengths, *slabs),
        [smem(), smem()] + [vm()] * 4,
        [
            pltpu.VMEM((groups, tokens + tokens // 2, 128), BF),
            pltpu.VMEM((full, 128), BF),
            pltpu.VMEM((full, 128), BF),
            pltpu.VMEM((128, full), BF),
            pltpu.VMEM((groups, tokens // 2, 128), BF),
        ],
        cost(4 * 4 * ns * full * full * 32, 4e6, ns * full * full // 2),
        after,
    )
    return out[:4], out[4:]


def attention_backward(geo, idx, slot, lengths, slabs, saved, d_slabs, after=()):
    groups, t, ns = geo.ranks, geo.t, geo.ns
    full, tokens, ndoc = groups * t, ns * t, lengths.shape[1]

    def kernel(idx_ref, len_ref, slot_ref, lse_ref, ot_ref, *refs):
        outs = refs[8:12]
        slab, gsl, qs, ks, kt, vs, right, delta, dvk, dq, dsl = refs[12:]
        load_slabs(slab, refs[:4], idx_ref)
        part = pl.ds(pl.multiple_of(slot_ref[0] * (tokens // 2), 128), tokens // 2)
        load_slabs(gsl, [ref.at[part] for ref in refs[4:8]], idx_ref)
        low = lanes((t, 128)) < 64

        def one(s, carry):
            at = pl.ds(pl.multiple_of(s * t, 16), t)
            folded = pl.ds(pl.multiple_of(tokens + s * (t // 2), 16), t // 2)
            o_rows = pl.ds(pl.multiple_of(s * (t // 2), 16), t // 2)
            for d in range(groups):
                rows = slice(d * t, (d + 1) * t)
                qk = slab[d, at, :].astype(F32)
                key = swap64(qk)
                q = jnp.where(low, qk * 0.125, 0.0)
                qs[rows, :] = q.astype(BF)
                ks[rows, :] = key.astype(BF)
                kt[:, rows] = key.T[:64].astype(BF)
                vs[rows, :] = unfold_one(slab[d, folded, :].astype(F32)).astype(BF)
                grad = jnp.where(low, unfold_one(gsl[d, o_rows, :].astype(F32)), 0.0)
                right[d, :t, :] = grad.astype(BF)
                right[d, t:, :] = swap64(q).astype(BF)
                delta[d : d + 1, :] = jnp.sum(grad.T[:64] * ot_ref[s, d], 0, keepdims=True)
            dvk[...] = jnp.zeros((full, 128), F32)
            for d in range(groups):
                rows = slice(d * t, (d + 1) * t)
                start = doc_start(len_ref, s, d * t + lanes((1, t)), ndoc)
                lse_row, delta_row = lse_ref[s, d : d + 1, :], delta[d : d + 1, :]
                total = jnp.zeros((64, t), F32)
                for b in range(first_key(d, t), d + 1):
                    keys = slice(b * t, (b + 1) * t)
                    scores = nt(ks[keys, :], qs[rows, :])
                    scores = jnp.where(allowed(start, d, b, t), scores, -1e30)
                    prob = jnp.exp(scores - lse_row)
                    d_prob = nt(vs[keys, :], right[d, :t, :])
                    ds = (prob * (d_prob - delta_row)).astype(BF)
                    dvk[keys, :] += nn(jnp.concatenate([prob.astype(BF), ds], axis=1), right[d])
                    total = total + nn(kt[:, keys], ds)
                dq[rows, :] = jnp.concatenate([total, total], axis=0).T * 0.125
            for d in range(groups):
                rows = slice(d * t, (d + 1) * t)
                both = dvk[rows, :]
                dsl[d, at, :] = merge64(dq[rows, :], both).astype(BF)
                dsl[d, folded, :] = fold_one(both).astype(BF)
            return carry

        lax.fori_loop(0, ns, one, 0)
        store_slabs(outs, dsl, idx_ref)

    slab_rows = tokens + tokens // 2
    flat = pltpu.VMEM((full, 128), BF)
    return call(
        kernel,
        "attention_backward",
        slab_set(slab_rows),
        (idx, lengths, jnp.array([slot], jnp.int32), *saved, *slabs, *d_slabs),
        [smem()] * 3 + [vm()] * 10,
        [
            pltpu.VMEM((groups, slab_rows, 128), BF),
            pltpu.VMEM((groups, tokens // 2, 128), BF),
            flat,
            flat,
            pltpu.VMEM((64, full), BF),
            flat,
            pltpu.VMEM((groups, 2 * t, 128), BF),
            pltpu.VMEM((8, t), F32),
            pltpu.VMEM((full, 128), F32),
            pltpu.VMEM((full, 128), F32),
            pltpu.VMEM((groups, slab_rows, 128), BF),
        ],
        cost(10 * 4 * ns * full * full * 32, 5e6, ns * full * full // 2),
        after,
    )


def mlp_forward(geo, idx, o_slabs, residual, out_grad, gain, out_bias, fc_bias, proj_bias, weights):
    groups, t, ns, narrow = geo.ranks, geo.t, geo.ns, geo.narrow
    wide, ff, tokens = geo.wide, geo.ff, geo.ns * geo.t
    n_slab, blocks = len(o_slabs), geo.ff // geo.wide
    rows = (wide // geo.fsdp) // (2 if geo.fast else 1)
    shares = wide // rows
    proj_shapes = part_shapes(geo, ff, wide)
    chunk = 512
    size_z = geo.fsdp // 2 if geo.fast else 1
    per_z = ff // size_z

    def kernel(idx_ref, *refs):
        slabs, refs = refs[:n_slab], refs[n_slab:]
        x_ref, og_ref, gain_ref, ob_ref, fb_ref, pb_ref = refs[:6]
        w_refs, refs = refs[6 : 6 + len(weights)], refs[6 + len(weights) :]
        out_ref, dpre_out, n_out, a_out, ogp_out, mid_out, bias_ref, wo_out, dn_ref = refs[:9]
        p_refs = refs[9 : 9 + len(proj_shapes)]
        refs = refs[9 + len(proj_shapes) :]
        wf, wp, osl, acc, tile, dpre_ref, n_ref, a_ref, ogp_ref, mid_ref, wo_ref, sem = refs
        early = [
            pltpu.make_async_copy(src, dst, sem.at[3 + i])
            for i, (src, dst) in enumerate(
                (
                    (ogp_ref, ogp_out),
                    (wo_ref, wo_out),
                    (a_ref, a_out),
                    (mid_ref, mid_out),
                    (n_ref, n_out),
                )
            )
        ]

        def d_pre_copy(i):
            cols = pl.ds(pl.multiple_of(i * chunk, 128), chunk)
            return pltpu.make_async_copy(dpre_ref.at[:, cols], dpre_out.at[:, cols], sem.at[8])

        def part_copies(zz):
            if not geo.fast:
                rows = pl.ds(zz * per_z, per_z)
                return [pltpu.make_async_copy(tile.at[rows], p_refs[0].at[rows], sem.at[9])]
            n = per_z // 4
            made = []
            for dx in range(2):
                for dc in range(2):
                    start = zz * per_z + ((idx_ref[1] ^ dx) * 2 + (idx_ref[3] ^ dc)) * n
                    made.append(
                        pltpu.make_async_copy(
                            tile.at[pl.ds(pl.multiple_of(start, 16), n)],
                            p_refs[dc].at[pl.ds((dx * size_z + zz) * n, n)],
                            sem.at[9],
                        )
                    )
            return made

        if geo.fast:
            (all_ref,) = w_refs
            out_src, fc_src = all_ref.at[:, pl.ds(0, wide)], all_ref.at[:, pl.ds(wide, ff)]
            to_proj = [
                pltpu.make_async_copy(
                    all_ref.at[pl.ds(share * rows, rows), pl.ds(wide + ff + i * wide, wide)],
                    wp.at[pl.ds((share * blocks + i) * rows, rows)],
                    sem.at[2],
                )
                for share in range(shares)
                for i in range(blocks)
            ]
        else:
            out_src, fc_src, proj_src = w_refs
            to_proj = [pltpu.make_async_copy(proj_src, wp, sem.at[2])]
        to_out = pltpu.make_async_copy(out_src, wp.at[pl.ds(0, wide)], sem.at[0])
        to_fc = pltpu.make_async_copy(fc_src, wf, sem.at[1])
        to_out.start()
        to_fc.start()
        for i in range(3):
            load_slabs(osl, slabs[4 * i : 4 * i + 4], idx_ref, i * groups)

        def load(s, carry):
            at = pl.ds(pl.multiple_of(s * t, 16), t)
            acc[at, :] = jnp.zeros((t, wide), F32)
            acc[at, :narrow] = og_ref[s].astype(F32)
            ogp_ref[at, :] = acc[at, :].astype(BF)
            acc[at, :narrow] = x_ref[s].astype(F32)
            dn_ref[at, :] = jnp.zeros((t, wide), F32)
            return carry

        lax.fori_loop(0, ns, load, 0)
        early[0].start()

        def assemble(i, carry):
            for p in range(groups // 2):
                at = pl.ds(pl.multiple_of(i * 64 * groups + 128 * p, 128), 128)
                for s in range(ns):
                    folded = slice(s * (t // 2), (s + 1) * (t // 2))
                    a_ref[s * t : (s + 1) * t, at] = unfold_pair(
                        osl[i * groups + 2 * p, folded, :].astype(F32),
                        osl[i * groups + 2 * p + 1, folded, :].astype(F32),
                    ).astype(BF)
            return carry

        lax.fori_loop(0, 3, assemble, 0)
        to_out.wait()
        for slot in range(3):
            for g in range(groups):
                at, head = 64 * (slot * groups + g), 3 * g + slot
                wo_ref[at : at + 64, :] = wp[64 * head : 64 * (head + 1), :]
        for copy in to_proj + early[1:3]:
            copy.start()

        def project(i, carry):
            cols = pl.ds(pl.multiple_of(i * 256, 128), 256)
            acc[:, cols] += nn(a_ref[...], wo_ref[:, cols]) + ob_ref[:, cols]
            return carry

        lax.fori_loop(0, wide // 256, project, 0)

        def norm(s, carry):
            at = pl.ds(pl.multiple_of(s * t, 16), t)
            full, inv = norm_rows(acc[at, :], narrow, wide)
            mid_ref[at, :] = full
            n_ref[at, :] = (full * inv * gain_ref[...]).astype(BF)
            return carry

        lax.fori_loop(0, ns, norm, 0)
        for copy in early[3:]:
            copy.start()
        to_fc.wait()
        for copy in to_proj:
            copy.wait()

        def one(i, carry):
            cols = pl.ds(pl.multiple_of(i * chunk, 128), chunk)
            w1, w2 = wf[:, cols], wp[cols, :]
            u = nn(n_ref[...], w1) + fb_ref[:, cols]
            square = u * u
            th = jnp.tanh(u * (GELU_K + GELU_K * GELU_C * square))
            half = 0.5 + 0.5 * th
            hidden = (u * half).astype(BF)
            slope = half + (0.5 * u) * (1.0 - th * th) * (GELU_K + 3.0 * GELU_K * GELU_C * square)
            acc[...] += nn(hidden, w2)
            d_pre = (nt(ogp_ref[...], w2) * slope).astype(BF)
            dpre_ref[:, cols] = d_pre
            d_pre_copy(i).start()
            bias_ref[0:1, cols] = jnp.sum(d_pre.astype(F32), 0, keepdims=True)
            dn_ref[...] += nt(d_pre, w1)
            tile[cols, :] = tn(hidden, ogp_ref[...]).astype(BF)
            for zz in range(size_z):

                @pl.when(i == ((zz + 1) * per_z - 1) // chunk)
                def _(zz=zz):
                    for copy in part_copies(zz):
                        copy.start()

            return carry

        lax.fori_loop(0, ff // chunk, one, 0)

        def store(s, carry):
            at = pl.ds(pl.multiple_of(s * t, 16), t)
            out_ref[s] = (acc[at, :] + pb_ref[...])[:, :narrow].astype(BF)
            return carry

        lax.fori_loop(0, ns, store, 0)
        for copy in early + [d_pre_copy(i) for i in range(ff // chunk)]:
            copy.wait()
        for zz in range(size_z):
            for copy in part_copies(zz):
                copy.wait()

    shapes = [
        sd(ns, t, narrow),
        sd(tokens, ff),
        sd(tokens, wide),
        sd(tokens, wide),
        sd(tokens, wide),
        sd(tokens, wide, dtype=F32),
        sd(8, ff, dtype=F32),
        sd(wide, wide),
        sd(tokens, wide, dtype=F32),
    ]
    out = call(
        kernel,
        "mlp_forward",
        shapes + proj_shapes,
        (idx, *o_slabs, residual, out_grad, gain, out_bias, fc_bias, proj_bias, *weights),
        [smem()] + [vm()] * (n_slab + 6) + [anyspace()] * len(weights),
        [
            pltpu.VMEM((wide, ff), BF),
            pltpu.VMEM((ff, wide), BF),
            pltpu.VMEM((3 * groups, tokens // 2, 128), BF),
            pltpu.VMEM((tokens, wide), F32),
            pltpu.VMEM((ff, wide), BF),
            pltpu.VMEM((tokens, ff), BF),
            pltpu.VMEM((tokens, wide), BF),
            pltpu.VMEM((tokens, wide), BF),
            pltpu.VMEM((tokens, wide), BF),
            pltpu.VMEM((tokens, wide), F32),
            pltpu.VMEM((wide, wide), BF),
            pltpu.SemaphoreType.DMA((10,)),
        ],
        cost(2 * tokens * wide * (5 * ff + wide), 34e6, tokens * ff),
        out_specs=tuple(
            vm() if i in (0, 6, 8) else anyspace() for i in range(len(shapes) + len(proj_shapes))
        ),
    )
    return out[: len(shapes)], out[len(shapes) :]


def mlp_backward(geo, idx, d_norm, out_w, og, middle, gain, bias_sums):
    groups, t, ns, narrow = geo.ranks, geo.t, geo.ns, geo.narrow
    wide, ff, tokens = geo.wide, geo.ff, geo.ns * geo.t
    n_slab = 4

    def kernel(idx_ref, dn, wo_ref, og_ref, mid_ref, gain_ref, bias_ref, *refs):
        db_ref, dmid_ref, vec_ref = refs[:3]
        outs = refs[3 : 3 + n_slab]
        da, dsl = refs[3 + n_slab :]
        vec_ref[0:1, :] = bias_ref[0:1, :]
        vec_ref[1:8, :] = jnp.zeros((7, ff), F32)

        def norm(s, carry):
            at = pl.ds(pl.multiple_of(s * t, 16), t)
            full = mid_ref[at, :]
            inv = lax.rsqrt(jnp.sum(full * full, 1, keepdims=True) * (1.0 / wide) + EPS)
            m, grad = full * inv, dn[at, :]
            dm = grad * gain_ref[...]
            d_full = inv * (dm - m * (jnp.sum(dm * m, 1, keepdims=True) * (1.0 / wide)))
            last = jnp.sum(jnp.where(lanes((t, wide)) == narrow, d_full, 0.0), 1, keepdims=True)
            og_f = og_ref[at, :].astype(F32)
            d_mid = og_f + (d_full - last)
            d_branch = d_mid.astype(BF)
            dmid_ref[at, :] = d_mid
            db_ref[at, :] = d_branch
            vec_ref[1:2, :wide] += jnp.sum(grad * m, 0, keepdims=True)
            vec_ref[2:3, :wide] += jnp.sum(d_branch.astype(F32), 0, keepdims=True)
            vec_ref[3:4, :wide] += jnp.sum(og_f, 0, keepdims=True)
            da[at, :] = nt(d_branch, wo_ref[...])
            return carry

        lax.fori_loop(0, ns, norm, 0)

        def fold(i, carry):
            for p in range(groups // 2):
                at = pl.ds(pl.multiple_of(i * 64 * groups + 128 * p, 128), 128)
                for s in range(ns):
                    pair = fold_pair(da[s * t : (s + 1) * t, at])
                    for half in range(2):
                        dest = pl.multiple_of(i * (tokens // 2) + s * (t // 2), 16)
                        dsl[2 * p + half, pl.ds(dest, t // 2), :] = pair[half].astype(BF)
            return carry

        lax.fori_loop(0, 3, fold, 0)
        store_slabs(outs, dsl, idx_ref)

    out = call(
        kernel,
        "mlp_backward",
        [sd(tokens, wide), sd(tokens, wide, dtype=F32), sd(8, ff, dtype=F32)] + slab_set(3 * tokens // 2),
        (idx, d_norm, out_w, og, middle, gain, bias_sums),
        [smem()] + [vm()] * 6,
        [
            pltpu.VMEM((tokens, wide), F32),
            pltpu.VMEM((groups, 3 * tokens // 2, 128), BF),
        ],
        cost(2 * tokens * wide * wide, 12e6),
    )
    return out[:3], out[3:]


def part_shapes(geo, rows, cols):
    return [sd(rows // 2, cols)] * 2 if geo.fast else [sd(rows, cols)]


def emit_rows(geo, idx_ref, outs, tile, total, cols, relative):
    if not geo.fast:
        outs[0][:, cols] = tile[...]
        return
    size_z = geo.fsdp // 2
    n = total // geo.fsdp // 2
    for dx in range(2):
        for zz in range(size_z):
            z = idx_ref[0] ^ zz if relative else zz
            for dc in range(2):
                start = ((z * 2 + (idx_ref[1] ^ dx)) * 2 + (idx_ref[3] ^ dc)) * n
                at = (dx * size_z + zz) * n
                outs[dc][at : at + n, cols] = tile[pl.ds(pl.multiple_of(start, 16), n), :]


def grad_fo(geo, idx, attn, d_branch, normed, d_pre, after=()):
    tokens, ff = d_pre.shape
    wide, groups, chunk = geo.wide, geo.ranks, 768
    shapes = part_shapes(geo, wide, wide + ff)

    def kernel(idx_ref, a_ref, db_ref, n_ref, dp_ref, *refs):
        outs, (trans, tile, nat) = refs[:-3], refs[-3:]
        trans[...] = n_ref[...].T
        nat[...] = tn(a_ref[...], db_ref[...]).astype(BF)
        for slot in range(3):
            for g in range(groups):
                at, head = 64 * (slot * groups + g), 3 * g + slot
                tile[64 * head : 64 * (head + 1), :] = nat[at : at + 64, :]
        emit_rows(geo, idx_ref, outs, tile, wide, slice(0, wide), False)

        def one(i, carry):
            at = pl.multiple_of(i * chunk, 128)
            tile[...] = nn(trans[...], dp_ref[:, pl.ds(at, chunk)]).astype(BF)
            emit_rows(geo, idx_ref, outs, tile, wide, pl.ds(at + wide, chunk), False)
            return carry

        lax.fori_loop(0, ff // chunk, one, 0)

    return call(
        kernel,
        "grad_fo",
        shapes,
        (idx, attn, d_branch, normed, d_pre),
        [smem()] + [vm()] * 4,
        [
            pltpu.VMEM((wide, tokens), BF),
            pltpu.VMEM((wide, wide), BF),
            pltpu.VMEM((wide, wide), BF),
        ],
        cost(2 * tokens * (ff + wide) * wide, 16e6),
        after,
    )


def grad_qkv(geo, idx, slabs, trans, last=False, after=()):
    groups, t, ns, wide = geo.ranks, geo.t, geo.ns, geo.wide
    slots, tokens = len(slabs) // 4, geo.ns * geo.t
    shapes = part_shapes(geo, wide, slots * wide)
    by_y = last and geo.fast
    width = wide // 2 if by_y else wide
    if by_y:
        shapes = [sd(wide // 2, width), sd(wide // 2, width), sd(wide, width)]

    def kernel(idx_ref, *refs):
        ins, t_ref = refs[: slots * 4], refs[slots * 4]
        refs = refs[slots * 4 + 1 :]
        outs = refs[: len(shapes)]
        dt_ref, tile = refs[len(shapes)], refs[len(shapes) + 1]
        slab = refs[-1]
        for i in range(slots):
            load_slabs(slab.at[i], ins[4 * i : 4 * i + 4], idx_ref)

        def one(i, carry):
            base = pl.multiple_of(i * wide, 128)
            for g in range(groups):
                dt_ref[:, pl.ds(base + 128 * g, 128)] = slab[i, g, :tokens, :]
            for p in range(groups // 2):
                at = pl.ds(base + 128 * (groups + p), 128)
                for s in range(ns):
                    folded = slice(tokens + s * (t // 2), tokens + (s + 1) * (t // 2))
                    dt_ref[s * t : (s + 1) * t, at] = unfold_pair(
                        slab[i, 2 * p, folded, :].astype(F32), slab[i, 2 * p + 1, folded, :].astype(F32)
                    ).astype(BF)
            return carry

        def multiply(i, carry):
            at = pl.ds(pl.multiple_of(i * width, 128), width)
            tile[...] = nn(t_ref[...], dt_ref[:, at]).astype(BF)
            emit_rows(geo, idx_ref, outs, tile, wide, at, True)
            return carry

        def multiply_half(i):
            at = pl.ds(pl.multiple_of((idx_ref[2] ^ i) * width, 128), width)
            tile[...] = nn(t_ref[...], dt_ref[:, at]).astype(BF)
            pair = (outs[i], outs[2].at[pl.ds(i * (wide // 2), wide // 2)])
            emit_rows(geo, idx_ref, pair, tile, wide, slice(0, width), True)

        lax.fori_loop(0, slots, one, 0)
        if by_y:
            multiply_half(0)
            multiply_half(1)
        else:
            lax.fori_loop(0, slots * wide // width, multiply, 0)

    out = call(
        kernel,
        "grad_qkv",
        shapes + [sd(tokens, slots * wide)],
        (idx, *slabs, trans),
        [smem()] + [vm()] * (slots * 4 + 1),
        [
            pltpu.VMEM((wide, width), BF),
            pltpu.VMEM((slots, groups, tokens + tokens // 2, 128), BF),
        ],
        cost(2 * tokens * slots * wide * wide, 4e6 * slots),
        after,
    )
    return out[:-1], out[-1]


def input_backward(geo, residual, gain, d_tokens, weights, d_mid, vectors, after=()):
    ns, t, narrow, wide, ff = geo.ns, geo.t, geo.narrow, geo.wide, geo.ff
    tokens, n, nw = ns * t, len(d_tokens), len(weights)

    def kernel(x_ref, gain_ref, dmid_ref, v_ref, *refs):
        dts, ws, (o_ref, vec_ref, row) = refs[:n], refs[n : n + nw], refs[n + nw :]
        vec_ref[...] = jnp.zeros(vec_ref.shape, F32)
        for i in range(3):
            vec_ref[1 + i : 2 + i, :] = v_ref[1 + i : 2 + i, :wide]
        for i in range(ff // wide):
            vec_ref[4 + i : 5 + i, :] = v_ref[0:1, i * wide : (i + 1) * wide]
        row[...] = jnp.zeros((t, wide), F32)
        slots = lambda refs: [
            (ref, slice(j * wide, (j + 1) * wide)) for ref in refs for j in range(ref.shape[1] // wide)
        ]

        def one(s, carry):
            rows = pl.ds(pl.multiple_of(s * t, 16), t)
            row[:, :narrow] = x_ref[s].astype(F32)
            full, inv = norm_rows(row[...], narrow, wide)
            grad = jnp.zeros((t, wide), F32)
            for i, ((dt, cols), (w, w_cols)) in enumerate(zip(slots(dts), slots(ws))):
                d_tok = dt[rows, cols]
                vec_ref[8 + i : 9 + i, :] += jnp.sum(d_tok.astype(F32), 0, keepdims=True)
                grad = grad + nt(d_tok, w[:, w_cols])
            m = full * inv
            vec_ref[0:1, :] += jnp.sum(grad * m, 0, keepdims=True)
            dm = grad * gain_ref[...]
            d_full = inv * (dm - m * (jnp.sum(dm * m, 1, keepdims=True) * (1.0 / wide)))
            last = jnp.sum(jnp.where(lanes((t, wide)) == narrow, d_full, 0.0), 1, keepdims=True)
            o_ref[s] = (dmid_ref[rows, :] + (d_full - last))[:, :narrow]
            return carry

        lax.fori_loop(0, ns, one, 0)

    return call(
        kernel,
        "input_backward",
        [sd(ns, t, narrow, dtype=F32), sd(16, wide, dtype=F32)],
        (residual, gain, d_mid, vectors, *d_tokens, *weights),
        [vm()] * (4 + n + nw),
        [pltpu.VMEM((t, wide), F32)],
        cost(2 * tokens * 3 * wide * wide, 14e6),
        after,
    )


def finish(geo, idx, pairs, plan, name):
    n = len(pairs)
    half = pairs[0][0].shape[0]
    rows = 2 * half if geo.fast else half
    sides = 2 if geo.fast else 1

    def kernel(idx_ref, *refs):
        outs = refs[n * sides :]
        for side in range(sides):
            at = pl.ds(pl.multiple_of((idx_ref[3] ^ side) * half, 8), half) if geo.fast else slice(0, rows)
            plan([refs[i * sides + side] for i in range(n)], outs, at)

    return lambda shapes: call(
        kernel,
        name,
        shapes,
        (idx, *[a for pair in pairs for a in pair[:sides]]),
        [smem()] + [vm()] * (n * sides),
        [],
        cost(0, rows * 3072 * 6),
    )


def finish_qkv(geo, idx, first, last):
    half, cols = first[0].shape
    wide = geo.wide
    rows, sides = (2 * half, 2) if geo.fast else (half, 1)
    where = {unit: at for at, unit in enumerate(unit_order(geo.ranks))}
    first = first[:sides]

    def kernel(idx_ref, *refs):
        a_refs, b_refs, (o_ref, b_all) = refs[:sides], refs[sides:-2], refs[-2:]
        for side in range(sides):
            at = pl.ds(pl.multiple_of((idx_ref[3] ^ side) * half, 8), half) if geo.fast else slice(0, rows)
            if geo.fast:
                for i in range(2):
                    cut = pl.ds(pl.multiple_of((idx_ref[2] ^ i) * (wide // 2), 128), wide // 2)
                    b_all[:, cut] = b_refs[2 * side + i][...].astype(F32)
            else:
                b_all[...] = b_refs[0][...].astype(F32)

            def read(b, a_ref=a_refs[side]):
                if b < cols // 128:
                    return a_ref[:, b * 128 : (b + 1) * 128].astype(F32)
                return b_all[:, b * 128 - cols : (b + 1) * 128 - cols]

            for j in range(3 * wide // 128):
                o_ref[at, j * 128 : (j + 1) * 128] = pick_units(read, where[2 * j], where[2 * j + 1])

    return call(
        kernel,
        "finish_qkv",
        sd(rows, 3 * wide, dtype=F32),
        (idx, *first, *last),
        [smem()] + [vm()] * (len(first) + len(last)),
        [pltpu.VMEM((half, wide), F32)],
        cost(0, rows * 3072 * 6),
    )


def add_bf(*terms):
    total = terms[0].astype(F32)
    for term in terms[1:]:
        total = total + term.astype(F32)
    return total.astype(BF)


def xor_pairs(size, step):
    return [(i, i ^ step) for i in range(size)]


class Reduction:
    def __init__(self, geo, stages, parts, pieces):
        self.st, self.parts, self.fast = stages, parts, geo.fast
        self.size_z = geo.fsdp // 2
        self.from_x, self.terms, self.sums, self.halves = [], [], [], None
        if self.fast:
            self.n = parts[0].shape[0] // 2
            self.m = self.n // self.size_z
            ends = [round(self.n * sum(pieces[: i + 1]) / sum(pieces)) for i in range(len(pieces))]
            self.cuts = [e // self.m * self.m for e in ends]
            self.cuts = list(zip([0] + self.cuts, self.cuts))

    def over_cores(self):
        if self.fast:
            self.got = self.st.permute(self.parts[1], "c")
            return self.got

    def prepare(self):
        if self.fast:
            keep, n = self.st.now(self.parts[0]), self.n
            self.halves = [add_bf(keep[n + a : n + b], self.got[n + a : n + b]) for a, b in self.cuts]
            return self.halves

    def over_x(self):
        if self.fast:
            k = len(self.from_x)
            if self.halves is None:
                first, last = (self.n + at for at in self.cuts[k])
                keep = self.st.now(self.parts[0])
                half = add_bf(keep[first:last], self.got[first:last])
            else:
                half = self.st.now(self.halves[k])
            self.from_x.append(lax.ppermute(half, "x", SWAP))
            return self.from_x[-1]

    def over_z(self, *steps):
        if not self.fast:
            return self.scatter_z() if 0 in steps else None
        keep, m, sent = self.st.now(self.parts[0]), self.m, []
        for k in steps:
            rows = slice(k * m, (k + 1) * m)
            term = add_bf(keep[rows], self.got[rows], self.from_x[0][rows])
            if k:
                sent.append(lax.ppermute(term, "z", xor_pairs(self.size_z, k)))
            self.terms.append(sent[-1] if k else term)
        return sent or self.terms

    def add_piece(self):
        if self.fast:
            k = len(self.sums)
            first, last = self.cuts[k]
            keep = self.st.now(self.parts[0])
            self.sums.append(add_bf(keep[first:last], self.got[first:last], self.from_x[k]))
            return self.sums[-1]

    def scatter_z(self):
        part = self.st.now(self.parts[0])
        if self.fast:
            while len(self.sums) < len(self.from_x):
                self.add_piece()
            part = jnp.concatenate(self.sums, axis=0)
            self.terms = [lax.psum_scatter(part, "z", scatter_dimension=0, tiled=True)]
        else:
            self.terms = [lax.psum_scatter(part, ("z", "x"), scatter_dimension=0, tiled=True)]

    def over_y(self, *after):
        if self.fast:
            self.share = lax.optimization_barrier((self.st.now(self.terms[0]), *after))[0]
            if len(self.terms) > 1:
                self.share = add_bf(self.share, *self.terms[1:])
            self.got_y = lax.ppermute(self.share, "y", SWAP)
            return self.got_y

    def total(self):
        if not self.fast:
            return lax.psum(self.terms[0], ("y", "c")), None
        total = add_bf(self.st.now(self.share), self.got_y)
        return total, lax.ppermute(total, "c", SWAP)


class LastReduction:
    def __init__(self, geo, stages, parts):
        self.geo, self.st, self.parts, self.fast = geo, stages, parts, geo.fast
        self.size_z = geo.fsdp // 2

    def over_cores(self):
        if self.fast:
            self.got = self.st.permute(self.parts[2], "c")
            return self.got

    def over_y(self):
        if self.fast:
            n = self.parts[0].shape[0]
            half = add_bf(self.st.now(self.parts[1]), self.got[n:])
            self.from_y = lax.ppermute(half, "y", SWAP)
            return self.from_y

    def over_x(self):
        if self.fast:
            n = self.parts[0].shape[0] // 2
            keep = self.st.now(self.parts[0])
            half = add_bf(keep[n:], self.got[n : 2 * n], self.from_y[n:])
            self.from_x = lax.ppermute(half, "x", SWAP)
            return self.from_x

    def over_z(self):
        if not self.fast:
            part = self.st.now(self.parts[0])
            self.terms = [lax.psum_scatter(part, ("z", "x"), scatter_dimension=0, tiled=True)]
            return self.terms
        m = self.parts[0].shape[0] // 2 // self.size_z
        keep = self.st.now(self.parts[0])
        self.terms = []
        for k in range(self.size_z):
            rows = slice(k * m, (k + 1) * m)
            term = add_bf(keep[rows], self.got[rows], self.from_y[rows], self.from_x[rows])
            self.terms.append(lax.ppermute(term, "z", xor_pairs(self.size_z, k)) if k else term)
        return self.terms

    def back_over_y(self):
        if self.fast:
            self.share = add_bf(self.st.now(self.terms[0]), *self.terms[1:])
            self.other = lax.ppermute(self.share, "y", SWAP)
            return self.other

    def total(self):
        if not self.fast:
            return [lax.psum(self.terms[0], ("y", "c"))]
        both = [self.share, self.other]
        return both + [self.st.permute(part, "c") for part in both]


def fold_in(v, axis, size, step=1):
    return v + lax.ppermute(v, axis, xor_pairs(size, step))


def gather_whole(own):
    return Parts([lax.all_gather(own, ("z", "x"), axis=0, tiled=True)])


class Geometry:
    pass


def local(
    geo,
    residual,
    out_grad,
    lengths,
    gain_one,
    qkv_weight,
    qv_bias,
    out_weight,
    out_bias,
    gain_two,
    fc_weight,
    fc_bias,
    proj_weight,
    proj_bias,
):
    geo.ranks = geo.seq
    geo.ns, geo.t, geo.narrow = residual.shape
    geo.wide, geo.ff = geo.narrow + 1, fc_weight.shape[1]
    narrow, wide, groups, ff = geo.narrow, geo.wide, geo.ranks, geo.ff
    heads, e = qv_bias.shape[0], qv_bias.shape[1] // 2
    size_z = geo.fsdp // 2
    geo.fast = (
        wide // geo.fsdp % 32 == 0
        and size_z & (size_z - 1) == 0
        and wide % (ff // size_z) == 0
        and ff // size_z % 64 == 0
    )
    z, x, y, c = (lax.axis_index(a) for a in ("z", "x", "y", "c"))
    idx = jnp.stack([z, x, y, c, 2 * y + c, z, z, z]).astype(jnp.int32)
    pad = lambda v: jnp.pad(v, (0, wide - narrow)).reshape(1, wide)
    gain1, gain2 = gain_one.reshape(1, wide), gain_two.reshape(1, wide)

    by_slot = qv_bias.reshape(groups, 3, 2 * e).transpose(1, 0, 2)
    q_bias = jnp.pad(by_slot[:, :, :e], ((0, 0), (0, 0), (0, e))).reshape(3, -1)
    bias = jnp.concatenate([q_bias, by_slot[:, :, e:].reshape(3, -1)], axis=1).reshape(1, -1)

    st = Stages(idx)
    own = prep_qkv(geo, idx, qkv_weight)
    bias_a, bias_b = bias[:, :wide], bias[:, wide:]
    if geo.fast:
        sides = [(dx, dc, 0, size_z, True) for dc in range(2) for dx in range(2)]
        whole = [own] + [lax.ppermute(own, "z", xor_pairs(size_z, i)) for i in range(1, size_z)]
        rest_own = prep_rest(geo, idx, out_weight, fc_weight, proj_weight)
        rest_own = lax.optimization_barrier((rest_own, whole[-1]))[0]
        rest = [lax.all_gather(rest_own, ("z", "x", "c"), axis=0, tiled=True)]
        st.end(whole)
        rows_a, rows_b = (
            jnp.concatenate([w[:, cut] for w in whole], axis=0)
            for cut in (slice(0, wide), slice(wide, 3 * wide))
        )
        other_a = st.permute(rows_a, "x")
        st.end(other_a)
        other_b = st.permute(rows_b, "x")
        w_a = [rows_a, other_a, st.permute(rows_a, "c"), st.permute(other_a, "c")]
        st.end(w_a)
        w_a = Parts(w_a, sides)
    else:
        w_a = gather_whole(own[:, :wide])
        w_b = gather_whole(own[:, wide:])
        widen = lambda w: jnp.pad(w, ((0, 0), (0, wide - narrow))).astype(BF)
        rest = [
            gather_whole(w).arrays[0]
            for w in (widen(out_weight), fc_weight.astype(BF), widen(proj_weight))
        ]
    sends, wq_a, (normed_one, normed_t) = qkv_forward(
        geo, st.token, residual, gain1, bias_a, w_a, (0,), True
    )
    st.end(sends)
    if geo.fast:
        w_b = Parts([rows_b, other_b, st.permute(rows_b, "c"), st.permute(other_b, "c")], sides)
    sends_b, wq_b, _ = qkv_forward(geo, idx, normed_one, gain1, bias_b, w_b, (1, 2), False)
    sends = list(sends) + list(sends_b)
    free = Stages(idx)
    slabs, saved, o_slabs = [], [], []
    for i in range(3):
        slabs.append(free.exchange(sends[4 * i : 4 * i + 4]))
    for i in range(3):
        o, stats = attention_forward(geo, idx, lengths, slabs[i])
        saved.append(stats)
        o_slabs += free.exchange(o)
    st.end(o_slabs)
    (output, d_pre, normed_two, attn, og, middle, bias_sums, out_w, d_norm), proj_parts = mlp_forward(
        geo,
        st.token,
        o_slabs,
        residual,
        out_grad,
        gain2,
        pad(out_bias),
        fc_bias.reshape(1, ff),
        pad(proj_bias),
        rest,
    )
    st.end(proj_parts)
    proj_red = Reduction(geo, st, proj_parts, (1, 1))
    got = proj_red.over_cores()
    (d_branch, d_mid, vectors), d_sends = mlp_backward(
        geo, st.token, d_norm, out_w, og, middle, gain2, bias_sums
    )
    st.end(got, d_branch)
    d_slabs = st.exchange(d_sends)
    got = proj_red.over_x()
    fo_red = Reduction(geo, st, grad_fo(geo, st.token, attn, d_branch, normed_two, d_pre), (1, 1))
    st.end(d_slabs, got, fo_red.parts)
    got = proj_red.over_x(), fo_red.over_cores(), fo_red.prepare()
    dq = attention_backward(geo, st.token, 0, lengths, slabs[0], saved[0], d_slabs)
    st.end(got, dq)
    dq_slabs = [st.exchange(dq)]
    proj_red.scatter_z()
    got = fo_red.over_x()
    dq = attention_backward(geo, st.token, 1, lengths, slabs[1], saved[1], d_slabs)
    st.end(got, dq, dq_slabs)
    dq_slabs.append(st.exchange(dq))
    got = fo_red.over_x()
    dq = attention_backward(geo, st.token, 2, lengths, slabs[2], saved[2], d_slabs)
    st.end(got, dq, dq_slabs)
    dq_slabs.append(st.exchange(dq))
    fo_red.scatter_z()
    parts_a, dt_a = grad_qkv(geo, st.token, dq_slabs[0] + dq_slabs[1], normed_t)
    red_a = Reduction(geo, st, parts_a, (1,))
    st.end(dq_slabs, parts_a)
    got = red_a.over_cores()
    parts_b, dt_b = grad_qkv(geo, st.token, dq_slabs[2], normed_t, last=True)
    red_b = LastReduction(geo, st, parts_b)
    st.end(got, parts_b)
    got = red_a.over_x(), proj_red.over_y(), red_b.over_cores(), red_b.over_y()
    input_grad, vecs = input_backward(
        geo,
        st.now(residual),
        gain1,
        (dt_a, dt_b),
        (wq_a, wq_b),
        d_mid,
        vectors,
    )
    if geo.fast:
        vecs = fold_in(vecs, "c", 2)
    else:
        vecs = lax.psum(vecs, ("z", "x", "y", "c"))
    st.end(got, vecs)
    got = red_a.over_z(*range(size_z)), red_b.over_x()
    if geo.fast:
        vecs = fold_in(st.now(vecs), "x", 2)
        got += (fo_red.over_y(vecs),)
    st.end(got, vecs)
    got = red_b.over_z(), red_a.over_y()
    proj_sum, fo_sum = proj_red.total(), fo_red.total()
    if geo.fast:
        vecs = fold_in(st.now(vecs), "y", 2)
    st.end(got, vecs, proj_sum, fo_sum)
    got = red_b.back_over_y()
    sum_a = red_a.total()
    if geo.fast:
        vecs = st.now(vecs)
        terms = [vecs] + [lax.ppermute(vecs, "z", xor_pairs(size_z, k)) for k in range(1, size_z)]
        while len(terms) > 1:
            terms = [a + b for a, b in zip(terms[::2], terms[1::2])]
        vecs = terms[0]
    st.end(got, vecs, sum_a)
    sum_b = red_b.total()
    sums = vecs[8:11].reshape(3, 3 * groups, e)
    q_sum = sums[:, : 2 * groups].reshape(3, groups, 2, e)[:, :, 0]
    v_sum = sums[:, 2 * groups :]
    qv_grad = jnp.concatenate([q_sum, v_sum], axis=2).transpose(1, 0, 2).reshape(heads, 2 * e)

    def plan_fo(ins, outs, at):
        outs[0][at, :] = ins[0][:, :narrow].astype(F32)
        outs[1][at, :] = ins[0][:, wide:].astype(F32)

    def plan_proj(ins, outs, at):
        outs[0][at, :] = ins[0][:, :narrow].astype(F32)

    block = wide // geo.fsdp
    qkv_grad = finish_qkv(geo, idx, sum_a, sum_b)
    out_w_grad, fc_w_grad = finish(geo, idx, [fo_sum], plan_fo, "finish_fo")(
        [sd(block, narrow, dtype=F32), sd(block, ff, dtype=F32)]
    )
    (proj_w_grad,) = finish(geo, idx, [proj_sum], plan_proj, "finish_proj")(
        [sd(ff // geo.fsdp, narrow, dtype=F32)]
    )
    return (
        output,
        input_grad,
        vecs[0],
        qkv_grad,
        qv_grad,
        out_w_grad,
        vecs[2, :narrow],
        vecs[1],
        fc_w_grad,
        vecs[4:8].reshape(-1),
        proj_w_grad,
        vecs[3, :narrow],
    )


def solution(mesh):
    geo = Geometry()
    geo.fsdp, geo.seq = mesh.devices.shape
    fine = Mesh(
        mesh.devices.reshape(geo.fsdp // 2, 2, geo.seq // 2, 2), ("z", "x", "y", "c")
    )
    fs, sq = ("z", "x"), ("y", "c")
    tokens, rows = P(fs, sq, None), P(fs, None)
    return jax.shard_map(
        functools.partial(local, geo),
        mesh=fine,
        in_specs=(
            tokens,
            tokens,
            rows,
            P(),
            rows,
            P(),
            rows,
            P(),
            P(),
            rows,
            P(),
            rows,
            P(),
        ),
        out_specs=(tokens, tokens, P(), rows, P(), rows, P(), P(), rows, P(), rows, P()),
        check_vma=False,
    )
```

```python
import functools

import jax
import jax.numpy as jnp
from jax import lax
from jax.experimental import pallas as pl
from jax.experimental.pallas import tpu as pltpu
from jax.sharding import Mesh, PartitionSpec as P

EPS = 1e-06
LONGEST = 512
BF = jnp.bfloat16
F32 = jnp.float32
VMEM_LIMIT = 60 * 1024 * 1024
SWAP = [(0, 1), (1, 0)]
GELU_K = 0.7978845608028654
GELU_C = 0.044715


def nn(a, b):
    return lax.dot_general(a, b, (((1,), (0,)), ((), ())), preferred_element_type=F32)


def nt(a, b):
    return lax.dot_general(a, b, (((1,), (1,)), ((), ())), preferred_element_type=F32)


def tn(a, b):
    return lax.dot_general(a, b, (((0,), (0,)), ((), ())), preferred_element_type=F32)


def lanes(shape):
    return lax.broadcasted_iota(jnp.int32, shape, 1)


def merge64(low, high):
    return jnp.where(lanes(low.shape) < 64, low, high)


def swap64(x):
    return pltpu.roll(x, 64, 1)


def fold_pair(x):
    n = x.shape[0] // 2
    top, bottom = x[:n], x[n:]
    return merge64(top, swap64(bottom)), merge64(swap64(top), bottom)


def unfold_pair(first, second):
    top = merge64(first, swap64(second))
    bottom = merge64(swap64(first), second)
    return jnp.concatenate([top, bottom], axis=0)


def vm():
    return pl.BlockSpec(memory_space=pltpu.VMEM)


def anyspace():
    return pl.BlockSpec(memory_space=pl.ANY)


def smem():
    return pl.BlockSpec(memory_space=pltpu.SMEM)


def cost(flops, nbytes, trans=0):
    scale = 0.1
    return pl.CostEstimate(
        flops=int(flops * scale), bytes_accessed=int(nbytes * scale), transcendentals=int(trans * scale)
    )


def params(**kw):
    return pltpu.CompilerParams(vmem_limit_bytes=VMEM_LIMIT, **kw)


def unit_order(groups):
    order = []
    for slot in range(3):
        for group in range(groups):
            order += [3 * (3 * group + slot), 3 * (3 * group + slot) + 1]
        for group in range(groups):
            order += [3 * (3 * group + slot) + 2]
    return order


def pick_units(load, low, high):
    def half(unit, side):
        block = load(unit // 2)
        return block if unit % 2 == side else swap64(block)

    return merge64(half(low, 0), half(high, 1))


def call(kernel, name, shapes, ins, specs, scratch, est, after=(), out_specs=None, **kw):
    if after:
        count, extra = len(ins), len(after)
        inner = kernel

        def kernel(*refs):
            inner(*refs[:count], *refs[count + extra :])

    many = isinstance(shapes, (tuple, list))
    return pl.pallas_call(
        kernel,
        out_shape=tuple(shapes) if many else shapes,
        in_specs=list(specs) + [anyspace()] * len(after),
        out_specs=out_specs or (tuple([vm()] * len(shapes)) if many else vm()),
        scratch_shapes=scratch,
        compiler_params=params(**kw),
        cost_estimate=est,
        name=name,
    )(*ins, *after)


def sd(*shape, dtype=BF):
    return jax.ShapeDtypeStruct(shape, dtype)


def prep_qkv(geo, idx, weight):
    rows = weight.shape[0] // 2 if geo.fast else weight.shape[0]
    width = weight.shape[1]
    order = unit_order(geo.ranks)

    def kernel(idx_ref, w_ref, o_ref):
        start = pl.multiple_of(idx_ref[3] * rows, 8) if geo.fast else 0
        for j in range(width // 128):
            o_ref[:, j * 128 : (j + 1) * 128] = pick_units(
                lambda b: w_ref[pl.ds(start, rows), b * 128 : (b + 1) * 128],
                order[2 * j],
                order[2 * j + 1],
            ).astype(BF)

    return call(
        kernel, "prep_qkv", sd(rows, width), (idx, weight), [smem(), vm()], [], cost(0, weight.size * 6)
    )


def prep_rest(geo, idx, out_w, fc_w, proj_w):
    div = 2 if geo.fast else 1
    rows = out_w.shape[0] // div
    wide, ff, narrow = geo.wide, fc_w.shape[1], out_w.shape[1]
    blocks = ff // wide

    def kernel(idx_ref, o_ref, f_ref, p_ref, all_ref):
        start = pl.multiple_of(idx_ref[3] * rows, 8) if geo.fast else 0
        pstart = pl.multiple_of(idx_ref[3] * rows * blocks, 8) if geo.fast else 0
        all_ref[...] = jnp.zeros(all_ref.shape, BF)
        all_ref[:, :narrow] = o_ref[pl.ds(start, rows), :].astype(BF)
        all_ref[:, wide : wide + ff] = f_ref[pl.ds(start, rows), :].astype(BF)
        for i in range(blocks):
            at = wide + ff + i * wide
            all_ref[:, at : at + narrow] = p_ref[pl.ds(pstart + i * rows, rows), :].astype(BF)

    return call(
        kernel,
        "prep_rest",
        sd(rows, wide + 2 * ff),
        (idx, out_w, fc_w, proj_w),
        [smem(), vm(), vm(), vm()],
        [],
        cost(0, 6 * (out_w.size + fc_w.size + proj_w.size)),
    )


class Parts:
    def __init__(self, arrays, coords=None):
        self.arrays, self.coords = list(arrays), coords

    def copies(self, geo, idx_ref, refs, dst, sem, src_cols=None):
        made = []
        if self.coords is None:
            src = refs[0] if src_cols is None else refs[0].at[:, src_cols]
            return [pltpu.make_async_copy(src, dst, sem)]
        for ref, (dx, dc, first, count, relative) in zip(refs, self.coords):
            n = ref.shape[0] // count
            for zz in range(count):
                z = idx_ref[0] ^ (first + zz) if relative else first + zz
                start = ((z * 2 + (idx_ref[1] ^ dx)) * 2 + (idx_ref[3] ^ dc)) * n
                rows = pl.ds(zz * n, n)
                src = ref.at[rows] if src_cols is None else ref.at[rows, src_cols]
                made.append(
                    pltpu.make_async_copy(src, dst.at[pl.ds(pl.multiple_of(start, 16), n)], sem)
                )
        return made


def norm_rows(x, narrow, wide):
    full = jnp.where(lanes(x.shape) == narrow, -jnp.sum(x, 1, keepdims=True), x)
    return full, lax.rsqrt(jnp.sum(full * full, 1, keepdims=True) * (1.0 / wide) + EPS)


def qkv_forward(geo, idx, source, gain, bias, parts, slots, first):
    groups, t, ns, narrow = geo.ranks, geo.t, geo.ns, geo.narrow
    wide, tokens = geo.wide, geo.ns * geo.t
    cols, slab_rows = len(slots) * geo.wide, tokens + tokens // 2
    count = len(parts.arrays)
    n_out = len(slots) * 4

    def kernel(idx_ref, x_ref, gain_ref, bias_ref, *refs):
        w_parts, outs = refs[:count], refs[count : count + n_out]
        refs = refs[count + n_out :]
        w_ref, refs = refs[0], refs[1:]
        if first:
            normed_ref, trans_ref, slab, sem, row = refs
        else:
            slab, sem = refs
            normed_ref = x_ref
        copies = parts.copies(geo, idx_ref, w_parts, w_ref, sem)
        for copy in copies:
            copy.start()
        if first:
            def norm(s, carry):
                at = pl.ds(pl.multiple_of(s * t, 16), t)
                row[at, :] = jnp.zeros((t, wide), F32)
                row[at, :narrow] = x_ref[s].astype(F32)
                full, inv = norm_rows(row[at, :], narrow, wide)
                normed_ref[at, :] = (full * inv * gain_ref[...]).astype(BF)
                return carry

            lax.fori_loop(0, ns, norm, 0)
            trans_ref[...] = normed_ref[...].T
        for copy in copies:
            copy.wait()

        def one(i, carry):
            base = pl.multiple_of(i * wide, 128)
            for j in range(groups // 2):
                at = pl.ds(base + 256 * j, 256)
                y = nn(normed_ref[...], w_ref[:, at]) + bias_ref[:, at]
                for half in range(2):
                    slab[i * groups + 2 * j + half, :tokens, :] = y[
                        :, half * 128 : (half + 1) * 128
                    ].astype(BF)
            at = pl.ds(base + 128 * groups, 64 * groups)
            y = nn(normed_ref[...], w_ref[:, at]) + bias_ref[:, at]
            for s in range(ns):
                rows = slice(tokens + s * (t // 2), tokens + (s + 1) * (t // 2))
                for p in range(groups // 2):
                    pair = fold_pair(y[s * t : (s + 1) * t, p * 128 : (p + 1) * 128])
                    for half in range(2):
                        slab[i * groups + 2 * p + half, rows, :] = pair[half].astype(BF)
            return carry

        lax.fori_loop(0, len(slots), one, 0)
        for i in range(len(slots)):
            store_slabs(outs[4 * i : 4 * i + 4], slab, idx_ref, i * groups)

    shapes = slab_set(slab_rows) * len(slots) + [sd(wide, cols)]
    scratch = [pltpu.VMEM((len(slots) * groups, slab_rows, 128), BF), pltpu.SemaphoreType.DMA]
    if first:
        shapes += [sd(tokens, wide), sd(wide, tokens)]
        scratch += [pltpu.VMEM((tokens, wide), F32)]
    out = call(
        kernel,
        "qkv_forward",
        shapes,
        (idx, source, gain, bias, *parts.arrays),
        [smem(), vm(), vm(), vm()] + [anyspace()] * count,
        scratch,
        cost(2 * tokens * wide * cols, 6e6),
    )
    return out[:n_out], out[n_out], out[n_out + 1 :]


def doc_start(len_ref, s, pos, ndoc):
    start = jnp.zeros(pos.shape, jnp.int32)
    edge = len_ref[s, 0]
    for n in range(1, ndoc):
        start = jnp.where(pos >= edge, edge, start)
        edge = edge + len_ref[s, n]
    return start


def first_key(block, t):
    return max(0, block * t - (LONGEST - 1)) // t


def allowed(start, block, key_block, t):
    k_pos = lax.broadcasted_iota(jnp.int32, (t, t), 0)
    seen = k_pos >= start - key_block * t
    if key_block == block:
        seen = seen & (k_pos <= lanes((1, t)))
    return seen


def store_slabs(outs, slab, idx_ref, base=0):
    for k, ref in enumerate(outs):
        ref[...] = slab[base + (idx_ref[4] ^ k)]


def load_slabs(slab, refs, idx_ref, base=0):
    for k, ref in enumerate(refs):
        slab[base + (idx_ref[4] ^ k)] = ref[...]


def slab_set(rows):
    return [sd(rows, 128)] * 4


class Stages:
    def __init__(self, idx):
        self.token = idx

    def end(self, *results):
        self.token = lax.optimization_barrier((self.token, *jax.tree.leaves(results)))[0]

    def now(self, x):
        return lax.optimization_barrier((x, self.token))[0]

    def permute(self, x, axis, pairs=SWAP):
        return lax.ppermute(self.now(x), axis, pairs)

    def exchange(self, slabs):
        return [slabs[0]] + [
            self.permute(slabs[k], ("y", "c"), xor_pairs(len(slabs), k)) for k in range(1, len(slabs))
        ]


def unfold_one(x):
    return jnp.concatenate([x, swap64(x)], axis=0)


def fold_one(x):
    n = x.shape[0] // 2
    return merge64(x[:n], swap64(x[n:]))


def attention_forward(geo, idx, lengths, slabs, after=()):
    groups, t, ns = geo.ranks, geo.t, geo.ns
    full, tokens, ndoc = groups * t, ns * t, lengths.shape[1]

    def kernel(idx_ref, len_ref, *refs):
        outs, lse_ref, ot_ref = refs[4:8], refs[8], refs[9]
        slab, qs, ks, vt, osl = refs[10:]
        load_slabs(slab, refs[:4], idx_ref)
        low = lanes((t, 128)) < 64

        def one(s, carry):
            at = pl.ds(pl.multiple_of(s * t, 16), t)
            folded = pl.ds(pl.multiple_of(tokens + s * (t // 2), 16), t // 2)
            for d in range(groups):
                rows = slice(d * t, (d + 1) * t)
                qk = slab[d, at, :].astype(F32)
                qs[rows, :] = jnp.where(low, qk * 0.125, 0.0).astype(BF)
                ks[rows, :] = swap64(qk).astype(BF)
                v = unfold_one(slab[d, folded, :].astype(F32))
                vt[:, rows] = jnp.where(low, v, 1.0).T.astype(BF)
            for d in range(groups):
                first = first_key(d, t)
                rows = slice(d * t, (d + 1) * t)
                start = doc_start(len_ref, s, d * t + lanes((1, t)), ndoc)
                blocks = []
                for b in range(first, d + 1):
                    scores = nt(ks[b * t : (b + 1) * t, :], qs[rows, :])
                    blocks.append(jnp.where(allowed(start, d, b, t), scores, -1e30))
                top = jnp.max(blocks[0], 0, keepdims=True)
                for block in blocks[1:]:
                    top = jnp.maximum(top, jnp.max(block, 0, keepdims=True))
                weight = jnp.concatenate([jnp.exp(block - top).astype(BF) for block in blocks], axis=0)
                o = nn(vt[:, first * t : (d + 1) * t], weight)
                total = o[64:65, :]
                lse_ref[s, d : d + 1, :] = top + jnp.log(total)
                o = o * (1.0 / total)
                ot_ref[s, d] = o[:64]
                osl[d, pl.ds(pl.multiple_of(s * (t // 2), 16), t // 2), :] = fold_one(o.T).astype(BF)
            return carry

        lax.fori_loop(0, ns, one, 0)
        store_slabs(outs, osl, idx_ref)

    shapes = slab_set(tokens // 2) + [sd(ns, 8, t, dtype=F32), sd(ns, groups, 64, t, dtype=F32)]
    out = call(
        kernel,
        "attention_forward",
        shapes,
        (idx, lengths, *slabs),
        [smem(), smem()] + [vm()] * 4,
        [
            pltpu.VMEM((groups, tokens + tokens // 2, 128), BF),
            pltpu.VMEM((full, 128), BF),
            pltpu.VMEM((full, 128), BF),
            pltpu.VMEM((128, full), BF),
            pltpu.VMEM((groups, tokens // 2, 128), BF),
        ],
        cost(4 * 4 * ns * full * full * 32, 4e6, ns * full * full // 2),
        after,
    )
    return out[:4], out[4:]


def attention_backward(geo, idx, slot, lengths, slabs, saved, d_slabs, after=()):
    groups, t, ns = geo.ranks, geo.t, geo.ns
    full, tokens, ndoc = groups * t, ns * t, lengths.shape[1]

    def kernel(idx_ref, len_ref, slot_ref, lse_ref, ot_ref, *refs):
        outs = refs[8:12]
        slab, gsl, qs, ks, kt, vs, right, delta, dvk, dq, dsl = refs[12:]
        load_slabs(slab, refs[:4], idx_ref)
        part = pl.ds(pl.multiple_of(slot_ref[0] * (tokens // 2), 128), tokens // 2)
        load_slabs(gsl, [ref.at[part] for ref in refs[4:8]], idx_ref)
        low = lanes((t, 128)) < 64

        def one(s, carry):
            at = pl.ds(pl.multiple_of(s * t, 16), t)
            folded = pl.ds(pl.multiple_of(tokens + s * (t // 2), 16), t // 2)
            o_rows = pl.ds(pl.multiple_of(s * (t // 2), 16), t // 2)
            for d in range(groups):
                rows = slice(d * t, (d + 1) * t)
                qk = slab[d, at, :].astype(F32)
                key = swap64(qk)
                q = jnp.where(low, qk * 0.125, 0.0)
                qs[rows, :] = q.astype(BF)
                ks[rows, :] = key.astype(BF)
                kt[:, rows] = key.T[:64].astype(BF)
                vs[rows, :] = unfold_one(slab[d, folded, :].astype(F32)).astype(BF)
                grad = jnp.where(low, unfold_one(gsl[d, o_rows, :].astype(F32)), 0.0)
                right[d, :t, :] = grad.astype(BF)
                right[d, t:, :] = swap64(q).astype(BF)
                delta[d : d + 1, :] = jnp.sum(grad.T[:64] * ot_ref[s, d], 0, keepdims=True)
            dvk[...] = jnp.zeros((full, 128), F32)
            for d in range(groups):
                rows = slice(d * t, (d + 1) * t)
                start = doc_start(len_ref, s, d * t + lanes((1, t)), ndoc)
                lse_row, delta_row = lse_ref[s, d : d + 1, :], delta[d : d + 1, :]
                total = jnp.zeros((64, t), F32)
                for b in range(first_key(d, t), d + 1):
                    keys = slice(b * t, (b + 1) * t)
                    scores = nt(ks[keys, :], qs[rows, :])
                    scores = jnp.where(allowed(start, d, b, t), scores, -1e30)
                    prob = jnp.exp(scores - lse_row)
                    d_prob = nt(vs[keys, :], right[d, :t, :])
                    ds = (prob * (d_prob - delta_row)).astype(BF)
                    dvk[keys, :] += nn(jnp.concatenate([prob.astype(BF), ds], axis=1), right[d])
                    total = total + nn(kt[:, keys], ds)
                dq[rows, :] = jnp.concatenate([total, total], axis=0).T * 0.125
            for d in range(groups):
                rows = slice(d * t, (d + 1) * t)
                both = dvk[rows, :]
                dsl[d, at, :] = merge64(dq[rows, :], both).astype(BF)
                dsl[d, folded, :] = fold_one(both).astype(BF)
            return carry

        lax.fori_loop(0, ns, one, 0)
        store_slabs(outs, dsl, idx_ref)

    slab_rows = tokens + tokens // 2
    flat = pltpu.VMEM((full, 128), BF)
    return call(
        kernel,
        "attention_backward",
        slab_set(slab_rows),
        (idx, lengths, jnp.array([slot], jnp.int32), *saved, *slabs, *d_slabs),
        [smem()] * 3 + [vm()] * 10,
        [
            pltpu.VMEM((groups, slab_rows, 128), BF),
            pltpu.VMEM((groups, tokens // 2, 128), BF),
            flat,
            flat,
            pltpu.VMEM((64, full), BF),
            flat,
            pltpu.VMEM((groups, 2 * t, 128), BF),
            pltpu.VMEM((8, t), F32),
            pltpu.VMEM((full, 128), F32),
            pltpu.VMEM((full, 128), F32),
            pltpu.VMEM((groups, slab_rows, 128), BF),
        ],
        cost(10 * 4 * ns * full * full * 32, 5e6, ns * full * full // 2),
        after,
    )


def mlp_forward(geo, idx, o_slabs, residual, out_grad, gain, out_bias, fc_bias, proj_bias, weights):
    groups, t, ns, narrow = geo.ranks, geo.t, geo.ns, geo.narrow
    wide, ff, tokens = geo.wide, geo.ff, geo.ns * geo.t
    n_slab, blocks = len(o_slabs), geo.ff // geo.wide
    rows = (wide // geo.fsdp) // (2 if geo.fast else 1)
    shares = wide // rows
    proj_shapes = part_shapes(geo, ff, wide)
    chunk = 512
    size_z = geo.fsdp // 2 if geo.fast else 1
    per_z = ff // size_z

    def kernel(idx_ref, *refs):
        slabs, refs = refs[:n_slab], refs[n_slab:]
        x_ref, og_ref, gain_ref, ob_ref, fb_ref, pb_ref = refs[:6]
        w_refs, refs = refs[6 : 6 + len(weights)], refs[6 + len(weights) :]
        out_ref, dpre_out, n_out, a_out, ogp_out, mid_out, bias_ref, wo_out, dn_ref = refs[:9]
        p_refs = refs[9 : 9 + len(proj_shapes)]
        refs = refs[9 + len(proj_shapes) :]
        wf, wp, osl, acc, tile, dpre_ref, n_ref, a_ref, ogp_ref, mid_ref, wo_ref, sem = refs
        early = [
            pltpu.make_async_copy(src, dst, sem.at[3 + i])
            for i, (src, dst) in enumerate(
                (
                    (ogp_ref, ogp_out),
                    (wo_ref, wo_out),
                    (a_ref, a_out),
                    (mid_ref, mid_out),
                    (n_ref, n_out),
                )
            )
        ]

        def d_pre_copy(i):
            cols = pl.ds(pl.multiple_of(i * chunk, 128), chunk)
            return pltpu.make_async_copy(dpre_ref.at[:, cols], dpre_out.at[:, cols], sem.at[8])

        def part_copies(zz):
            if not geo.fast:
                rows = pl.ds(zz * per_z, per_z)
                return [pltpu.make_async_copy(tile.at[rows], p_refs[0].at[rows], sem.at[9])]
            n = per_z // 4
            made = []
            for dx in range(2):
                for dc in range(2):
                    start = zz * per_z + ((idx_ref[1] ^ dx) * 2 + (idx_ref[3] ^ dc)) * n
                    made.append(
                        pltpu.make_async_copy(
                            tile.at[pl.ds(pl.multiple_of(start, 16), n)],
                            p_refs[dc].at[pl.ds((dx * size_z + zz) * n, n)],
                            sem.at[9],
                        )
                    )
            return made

        if geo.fast:
            (all_ref,) = w_refs
            out_src, fc_src = all_ref.at[:, pl.ds(0, wide)], all_ref.at[:, pl.ds(wide, ff)]
            to_proj = [
                pltpu.make_async_copy(
                    all_ref.at[pl.ds(share * rows, rows), pl.ds(wide + ff + i * wide, wide)],
                    wp.at[pl.ds((share * blocks + i) * rows, rows)],
                    sem.at[2],
                )
                for share in range(shares)
                for i in range(blocks)
            ]
        else:
            out_src, fc_src, proj_src = w_refs
            to_proj = [pltpu.make_async_copy(proj_src, wp, sem.at[2])]
        to_out = pltpu.make_async_copy(out_src, wp.at[pl.ds(0, wide)], sem.at[0])
        to_fc = pltpu.make_async_copy(fc_src, wf, sem.at[1])
        to_out.start()
        to_fc.start()
        for i in range(3):
            load_slabs(osl, slabs[4 * i : 4 * i + 4], idx_ref, i * groups)

        def load(s, carry):
            at = pl.ds(pl.multiple_of(s * t, 16), t)
            acc[at, :] = jnp.zeros((t, wide), F32)
            acc[at, :narrow] = og_ref[s].astype(F32)
            ogp_ref[at, :] = acc[at, :].astype(BF)
            acc[at, :narrow] = x_ref[s].astype(F32)
            dn_ref[at, :] = jnp.zeros((t, wide), F32)
            return carry

        lax.fori_loop(0, ns, load, 0)
        early[0].start()

        def assemble(i, carry):
            for p in range(groups // 2):
                at = pl.ds(pl.multiple_of(i * 64 * groups + 128 * p, 128), 128)
                for s in range(ns):
                    folded = slice(s * (t // 2), (s + 1) * (t // 2))
                    a_ref[s * t : (s + 1) * t, at] = unfold_pair(
                        osl[i * groups + 2 * p, folded, :].astype(F32),
                        osl[i * groups + 2 * p + 1, folded, :].astype(F32),
                    ).astype(BF)
            return carry

        lax.fori_loop(0, 3, assemble, 0)
        to_out.wait()
        for slot in range(3):
            for g in range(groups):
                at, head = 64 * (slot * groups + g), 3 * g + slot
                wo_ref[at : at + 64, :] = wp[64 * head : 64 * (head + 1), :]
        for copy in to_proj + early[1:3]:
            copy.start()

        def project(i, carry):
            cols = pl.ds(pl.multiple_of(i * 256, 128), 256)
            acc[:, cols] += nn(a_ref[...], wo_ref[:, cols]) + ob_ref[:, cols]
            return carry

        lax.fori_loop(0, wide // 256, project, 0)

        def norm(s, carry):
            at = pl.ds(pl.multiple_of(s * t, 16), t)
            full, inv = norm_rows(acc[at, :], narrow, wide)
            mid_ref[at, :] = full
            n_ref[at, :] = (full * inv * gain_ref[...]).astype(BF)
            return carry

        lax.fori_loop(0, ns, norm, 0)
        for copy in early[3:]:
            copy.start()
        to_fc.wait()
        for copy in to_proj:
            copy.wait()

        def one(i, carry):
            cols = pl.ds(pl.multiple_of(i * chunk, 128), chunk)
            w1, w2 = wf[:, cols], wp[cols, :]
            u = nn(n_ref[...], w1) + fb_ref[:, cols]
            square = u * u
            th = jnp.tanh(u * (GELU_K + GELU_K * GELU_C * square))
            half = 0.5 + 0.5 * th
            hidden = (u * half).astype(BF)
            slope = half + (0.5 * u) * (1.0 - th * th) * (GELU_K + 3.0 * GELU_K * GELU_C * square)
            acc[...] += nn(hidden, w2)
            d_pre = (nt(ogp_ref[...], w2) * slope).astype(BF)
            dpre_ref[:, cols] = d_pre
            d_pre_copy(i).start()
            bias_ref[0:1, cols] = jnp.sum(d_pre.astype(F32), 0, keepdims=True)
            dn_ref[...] += nt(d_pre, w1)
            tile[cols, :] = tn(hidden, ogp_ref[...]).astype(BF)
            for zz in range(size_z):

                @pl.when(i == ((zz + 1) * per_z - 1) // chunk)
                def _(zz=zz):
                    for copy in part_copies(zz):
                        copy.start()

            return carry

        lax.fori_loop(0, ff // chunk, one, 0)

        def store(s, carry):
            at = pl.ds(pl.multiple_of(s * t, 16), t)
            out_ref[s] = (acc[at, :] + pb_ref[...])[:, :narrow].astype(BF)
            return carry

        lax.fori_loop(0, ns, store, 0)
        for copy in early + [d_pre_copy(i) for i in range(ff // chunk)]:
            copy.wait()
        for zz in range(size_z):
            for copy in part_copies(zz):
                copy.wait()

    shapes = [
        sd(ns, t, narrow),
        sd(tokens, ff),
        sd(tokens, wide),
        sd(tokens, wide),
        sd(tokens, wide),
        sd(tokens, wide, dtype=F32),
        sd(8, ff, dtype=F32),
        sd(wide, wide),
        sd(tokens, wide, dtype=F32),
    ]
    out = call(
        kernel,
        "mlp_forward",
        shapes + proj_shapes,
        (idx, *o_slabs, residual, out_grad, gain, out_bias, fc_bias, proj_bias, *weights),
        [smem()] + [vm()] * (n_slab + 6) + [anyspace()] * len(weights),
        [
            pltpu.VMEM((wide, ff), BF),
            pltpu.VMEM((ff, wide), BF),
            pltpu.VMEM((3 * groups, tokens // 2, 128), BF),
            pltpu.VMEM((tokens, wide), F32),
            pltpu.VMEM((ff, wide), BF),
            pltpu.VMEM((tokens, ff), BF),
            pltpu.VMEM((tokens, wide), BF),
            pltpu.VMEM((tokens, wide), BF),
            pltpu.VMEM((tokens, wide), BF),
            pltpu.VMEM((tokens, wide), F32),
            pltpu.VMEM((wide, wide), BF),
            pltpu.SemaphoreType.DMA((10,)),
        ],
        cost(2 * tokens * wide * (5 * ff + wide), 34e6, tokens * ff),
        out_specs=tuple(
            vm() if i in (0, 6, 8) else anyspace() for i in range(len(shapes) + len(proj_shapes))
        ),
    )
    return out[: len(shapes)], out[len(shapes) :]


def mlp_backward(geo, idx, d_norm, out_w, og, middle, gain, bias_sums):
    groups, t, ns, narrow = geo.ranks, geo.t, geo.ns, geo.narrow
    wide, ff, tokens = geo.wide, geo.ff, geo.ns * geo.t
    n_slab = 4

    def kernel(idx_ref, dn, wo_ref, og_ref, mid_ref, gain_ref, bias_ref, *refs):
        db_ref, dmid_ref, vec_ref = refs[:3]
        outs = refs[3 : 3 + n_slab]
        da, dsl = refs[3 + n_slab :]
        vec_ref[0:1, :] = bias_ref[0:1, :]
        vec_ref[1:8, :] = jnp.zeros((7, ff), F32)

        def norm(s, carry):
            at = pl.ds(pl.multiple_of(s * t, 16), t)
            full = mid_ref[at, :]
            inv = lax.rsqrt(jnp.sum(full * full, 1, keepdims=True) * (1.0 / wide) + EPS)
            m, grad = full * inv, dn[at, :]
            dm = grad * gain_ref[...]
            d_full = inv * (dm - m * (jnp.sum(dm * m, 1, keepdims=True) * (1.0 / wide)))
            last = jnp.sum(jnp.where(lanes((t, wide)) == narrow, d_full, 0.0), 1, keepdims=True)
            og_f = og_ref[at, :].astype(F32)
            d_mid = og_f + (d_full - last)
            d_branch = d_mid.astype(BF)
            dmid_ref[at, :] = d_mid
            db_ref[at, :] = d_branch
            vec_ref[1:2, :wide] += jnp.sum(grad * m, 0, keepdims=True)
            vec_ref[2:3, :wide] += jnp.sum(d_branch.astype(F32), 0, keepdims=True)
            vec_ref[3:4, :wide] += jnp.sum(og_f, 0, keepdims=True)
            da[at, :] = nt(d_branch, wo_ref[...])
            return carry

        lax.fori_loop(0, ns, norm, 0)

        def fold(i, carry):
            for p in range(groups // 2):
                at = pl.ds(pl.multiple_of(i * 64 * groups + 128 * p, 128), 128)
                for s in range(ns):
                    pair = fold_pair(da[s * t : (s + 1) * t, at])
                    for half in range(2):
                        dest = pl.multiple_of(i * (tokens // 2) + s * (t // 2), 16)
                        dsl[2 * p + half, pl.ds(dest, t // 2), :] = pair[half].astype(BF)
            return carry

        lax.fori_loop(0, 3, fold, 0)
        store_slabs(outs, dsl, idx_ref)

    out = call(
        kernel,
        "mlp_backward",
        [sd(tokens, wide), sd(tokens, wide, dtype=F32), sd(8, ff, dtype=F32)] + slab_set(3 * tokens // 2),
        (idx, d_norm, out_w, og, middle, gain, bias_sums),
        [smem()] + [vm()] * 6,
        [
            pltpu.VMEM((tokens, wide), F32),
            pltpu.VMEM((groups, 3 * tokens // 2, 128), BF),
        ],
        cost(2 * tokens * wide * wide, 12e6),
    )
    return out[:3], out[3:]


def part_shapes(geo, rows, cols):
    return [sd(rows // 2, cols)] * 2 if geo.fast else [sd(rows, cols)]


def emit_rows(geo, idx_ref, outs, tile, total, cols, relative):
    if not geo.fast:
        outs[0][:, cols] = tile[...]
        return
    size_z = geo.fsdp // 2
    n = total // geo.fsdp // 2
    for dx in range(2):
        for zz in range(size_z):
            z = idx_ref[0] ^ zz if relative else zz
            for dc in range(2):
                start = ((z * 2 + (idx_ref[1] ^ dx)) * 2 + (idx_ref[3] ^ dc)) * n
                at = (dx * size_z + zz) * n
                outs[dc][at : at + n, cols] = tile[pl.ds(pl.multiple_of(start, 16), n), :]


def grad_fo(geo, idx, attn, d_branch, normed, d_pre, after=()):
    tokens, ff = d_pre.shape
    wide, groups, chunk = geo.wide, geo.ranks, 768
    shapes = part_shapes(geo, wide, wide + ff)

    def kernel(idx_ref, a_ref, db_ref, n_ref, dp_ref, *refs):
        outs, (trans, tile, nat) = refs[:-3], refs[-3:]
        trans[...] = n_ref[...].T
        nat[...] = tn(a_ref[...], db_ref[...]).astype(BF)
        for slot in range(3):
            for g in range(groups):
                at, head = 64 * (slot * groups + g), 3 * g + slot
                tile[64 * head : 64 * (head + 1), :] = nat[at : at + 64, :]
        emit_rows(geo, idx_ref, outs, tile, wide, slice(0, wide), False)

        def one(i, carry):
            at = pl.multiple_of(i * chunk, 128)
            tile[...] = nn(trans[...], dp_ref[:, pl.ds(at, chunk)]).astype(BF)
            emit_rows(geo, idx_ref, outs, tile, wide, pl.ds(at + wide, chunk), False)
            return carry

        lax.fori_loop(0, ff // chunk, one, 0)

    return call(
        kernel,
        "grad_fo",
        shapes,
        (idx, attn, d_branch, normed, d_pre),
        [smem()] + [vm()] * 4,
        [
            pltpu.VMEM((wide, tokens), BF),
            pltpu.VMEM((wide, wide), BF),
            pltpu.VMEM((wide, wide), BF),
        ],
        cost(2 * tokens * (ff + wide) * wide, 16e6),
        after,
    )


def grad_qkv(geo, idx, slabs, trans, last=False, after=()):
    groups, t, ns, wide = geo.ranks, geo.t, geo.ns, geo.wide
    slots, tokens = len(slabs) // 4, geo.ns * geo.t
    shapes = part_shapes(geo, wide, slots * wide)
    by_y = last and geo.fast
    width = wide // 2 if by_y else wide
    if by_y:
        shapes = [sd(wide // 2, width), sd(wide // 2, width), sd(wide, width)]

    def kernel(idx_ref, *refs):
        ins, t_ref = refs[: slots * 4], refs[slots * 4]
        refs = refs[slots * 4 + 1 :]
        outs = refs[: len(shapes)]
        dt_ref, tile = refs[len(shapes)], refs[len(shapes) + 1]
        slab = refs[-1]
        for i in range(slots):
            load_slabs(slab.at[i], ins[4 * i : 4 * i + 4], idx_ref)

        def one(i, carry):
            base = pl.multiple_of(i * wide, 128)
            for g in range(groups):
                dt_ref[:, pl.ds(base + 128 * g, 128)] = slab[i, g, :tokens, :]
            for p in range(groups // 2):
                at = pl.ds(base + 128 * (groups + p), 128)
                for s in range(ns):
                    folded = slice(tokens + s * (t // 2), tokens + (s + 1) * (t // 2))
                    dt_ref[s * t : (s + 1) * t, at] = unfold_pair(
                        slab[i, 2 * p, folded, :].astype(F32), slab[i, 2 * p + 1, folded, :].astype(F32)
                    ).astype(BF)
            return carry

        def multiply(i, carry):
            at = pl.ds(pl.multiple_of(i * width, 128), width)
            tile[...] = nn(t_ref[...], dt_ref[:, at]).astype(BF)
            emit_rows(geo, idx_ref, outs, tile, wide, at, True)
            return carry

        def multiply_half(i):
            at = pl.ds(pl.multiple_of((idx_ref[2] ^ i) * width, 128), width)
            tile[...] = nn(t_ref[...], dt_ref[:, at]).astype(BF)
            pair = (outs[i], outs[2].at[pl.ds(i * (wide // 2), wide // 2)])
            emit_rows(geo, idx_ref, pair, tile, wide, slice(0, width), True)

        lax.fori_loop(0, slots, one, 0)
        if by_y:
            multiply_half(0)
            multiply_half(1)
        else:
            lax.fori_loop(0, slots * wide // width, multiply, 0)

    out = call(
        kernel,
        "grad_qkv",
        shapes + [sd(tokens, slots * wide)],
        (idx, *slabs, trans),
        [smem()] + [vm()] * (slots * 4 + 1),
        [
            pltpu.VMEM((wide, width), BF),
            pltpu.VMEM((slots, groups, tokens + tokens // 2, 128), BF),
        ],
        cost(2 * tokens * slots * wide * wide, 4e6 * slots),
        after,
    )
    return out[:-1], out[-1]


def input_backward(geo, residual, gain, d_tokens, weights, d_mid, vectors, after=()):
    ns, t, narrow, wide, ff = geo.ns, geo.t, geo.narrow, geo.wide, geo.ff
    tokens, n, nw = ns * t, len(d_tokens), len(weights)

    def kernel(x_ref, gain_ref, dmid_ref, v_ref, *refs):
        dts, ws, (o_ref, vec_ref, row) = refs[:n], refs[n : n + nw], refs[n + nw :]
        vec_ref[...] = jnp.zeros(vec_ref.shape, F32)
        for i in range(3):
            vec_ref[1 + i : 2 + i, :] = v_ref[1 + i : 2 + i, :wide]
        for i in range(ff // wide):
            vec_ref[4 + i : 5 + i, :] = v_ref[0:1, i * wide : (i + 1) * wide]
        row[...] = jnp.zeros((t, wide), F32)
        slots = lambda refs: [
            (ref, slice(j * wide, (j + 1) * wide)) for ref in refs for j in range(ref.shape[1] // wide)
        ]

        def one(s, carry):
            rows = pl.ds(pl.multiple_of(s * t, 16), t)
            row[:, :narrow] = x_ref[s].astype(F32)
            full, inv = norm_rows(row[...], narrow, wide)
            grad = jnp.zeros((t, wide), F32)
            for i, ((dt, cols), (w, w_cols)) in enumerate(zip(slots(dts), slots(ws))):
                d_tok = dt[rows, cols]
                vec_ref[8 + i : 9 + i, :] += jnp.sum(d_tok.astype(F32), 0, keepdims=True)
                grad = grad + nt(d_tok, w[:, w_cols])
            m = full * inv
            vec_ref[0:1, :] += jnp.sum(grad * m, 0, keepdims=True)
            dm = grad * gain_ref[...]
            d_full = inv * (dm - m * (jnp.sum(dm * m, 1, keepdims=True) * (1.0 / wide)))
            last = jnp.sum(jnp.where(lanes((t, wide)) == narrow, d_full, 0.0), 1, keepdims=True)
            o_ref[s] = (dmid_ref[rows, :] + (d_full - last))[:, :narrow]
            return carry

        lax.fori_loop(0, ns, one, 0)

    return call(
        kernel,
        "input_backward",
        [sd(ns, t, narrow, dtype=F32), sd(16, wide, dtype=F32)],
        (residual, gain, d_mid, vectors, *d_tokens, *weights),
        [vm()] * (4 + n + nw),
        [pltpu.VMEM((t, wide), F32)],
        cost(2 * tokens * 3 * wide * wide, 14e6),
        after,
    )


def finish(geo, idx, pairs, plan, name):
    n = len(pairs)
    half = pairs[0][0].shape[0]
    rows = 2 * half if geo.fast else half
    sides = 2 if geo.fast else 1

    def kernel(idx_ref, *refs):
        outs = refs[n * sides :]
        for side in range(sides):
            at = pl.ds(pl.multiple_of((idx_ref[3] ^ side) * half, 8), half) if geo.fast else slice(0, rows)
            plan([refs[i * sides + side] for i in range(n)], outs, at)

    return lambda shapes: call(
        kernel,
        name,
        shapes,
        (idx, *[a for pair in pairs for a in pair[:sides]]),
        [smem()] + [vm()] * (n * sides),
        [],
        cost(0, rows * 3072 * 6),
    )


def finish_qkv(geo, idx, first, last):
    half, cols = first[0].shape
    wide = geo.wide
    rows, sides = (2 * half, 2) if geo.fast else (half, 1)
    where = {unit: at for at, unit in enumerate(unit_order(geo.ranks))}
    first = first[:sides]

    def kernel(idx_ref, *refs):
        a_refs, b_refs, (o_ref, b_all) = refs[:sides], refs[sides:-2], refs[-2:]
        for side in range(sides):
            at = pl.ds(pl.multiple_of((idx_ref[3] ^ side) * half, 8), half) if geo.fast else slice(0, rows)
            if geo.fast:
                for i in range(2):
                    cut = pl.ds(pl.multiple_of((idx_ref[2] ^ i) * (wide // 2), 128), wide // 2)
                    b_all[:, cut] = b_refs[2 * side + i][...].astype(F32)
            else:
                b_all[...] = b_refs[0][...].astype(F32)

            def read(b, a_ref=a_refs[side]):
                if b < cols // 128:
                    return a_ref[:, b * 128 : (b + 1) * 128].astype(F32)
                return b_all[:, b * 128 - cols : (b + 1) * 128 - cols]

            for j in range(3 * wide // 128):
                o_ref[at, j * 128 : (j + 1) * 128] = pick_units(read, where[2 * j], where[2 * j + 1])

    return call(
        kernel,
        "finish_qkv",
        sd(rows, 3 * wide, dtype=F32),
        (idx, *first, *last),
        [smem()] + [vm()] * (len(first) + len(last)),
        [pltpu.VMEM((half, wide), F32)],
        cost(0, rows * 3072 * 6),
    )


def add_bf(*terms):
    total = terms[0].astype(F32)
    for term in terms[1:]:
        total = total + term.astype(F32)
    return total.astype(BF)


def xor_pairs(size, step):
    return [(i, i ^ step) for i in range(size)]


class Reduction:
    def __init__(self, geo, stages, parts, pieces):
        self.st, self.parts, self.fast = stages, parts, geo.fast
        self.size_z = geo.fsdp // 2
        self.from_x, self.terms, self.sums, self.halves = [], [], [], None
        if self.fast:
            self.n = parts[0].shape[0] // 2
            self.m = self.n // self.size_z
            ends = [round(self.n * sum(pieces[: i + 1]) / sum(pieces)) for i in range(len(pieces))]
            self.cuts = [e // self.m * self.m for e in ends]
            self.cuts = list(zip([0] + self.cuts, self.cuts))

    def over_cores(self):
        if self.fast:
            self.got = self.st.permute(self.parts[1], "c")
            return self.got

    def prepare(self):
        if self.fast:
            keep, n = self.st.now(self.parts[0]), self.n
            self.halves = [add_bf(keep[n + a : n + b], self.got[n + a : n + b]) for a, b in self.cuts]
            return self.halves

    def over_x(self):
        if self.fast:
            k = len(self.from_x)
            if self.halves is None:
                first, last = (self.n + at for at in self.cuts[k])
                keep = self.st.now(self.parts[0])
                half = add_bf(keep[first:last], self.got[first:last])
            else:
                half = self.st.now(self.halves[k])
            self.from_x.append(lax.ppermute(half, "x", SWAP))
            return self.from_x[-1]

    def over_z(self, *steps):
        if not self.fast:
            return self.scatter_z() if 0 in steps else None
        keep, m, sent = self.st.now(self.parts[0]), self.m, []
        for k in steps:
            rows = slice(k * m, (k + 1) * m)
            term = add_bf(keep[rows], self.got[rows], self.from_x[0][rows])
            if k:
                sent.append(lax.ppermute(term, "z", xor_pairs(self.size_z, k)))
            self.terms.append(sent[-1] if k else term)
        return sent or self.terms

    def add_piece(self):
        if self.fast:
            k = len(self.sums)
            first, last = self.cuts[k]
            keep = self.st.now(self.parts[0])
            self.sums.append(add_bf(keep[first:last], self.got[first:last], self.from_x[k]))
            return self.sums[-1]

    def scatter_z(self):
        part = self.st.now(self.parts[0])
        if self.fast:
            while len(self.sums) < len(self.from_x):
                self.add_piece()
            part = jnp.concatenate(self.sums, axis=0)
            self.terms = [lax.psum_scatter(part, "z", scatter_dimension=0, tiled=True)]
        else:
            self.terms = [lax.psum_scatter(part, ("z", "x"), scatter_dimension=0, tiled=True)]

    def over_y(self, *after):
        if self.fast:
            self.share = lax.optimization_barrier((self.st.now(self.terms[0]), *after))[0]
            if len(self.terms) > 1:
                self.share = add_bf(self.share, *self.terms[1:])
            self.got_y = lax.ppermute(self.share, "y", SWAP)
            return self.got_y

    def total(self):
        if not self.fast:
            return lax.psum(self.terms[0], ("y", "c")), None
        total = add_bf(self.st.now(self.share), self.got_y)
        return total, lax.ppermute(total, "c", SWAP)


class LastReduction:
    def __init__(self, geo, stages, parts):
        self.geo, self.st, self.parts, self.fast = geo, stages, parts, geo.fast
        self.size_z = geo.fsdp // 2

    def over_cores(self):
        if self.fast:
            self.got = self.st.permute(self.parts[2], "c")
            return self.got

    def over_y(self):
        if self.fast:
            n = self.parts[0].shape[0]
            half = add_bf(self.st.now(self.parts[1]), self.got[n:])
            self.from_y = lax.ppermute(half, "y", SWAP)
            return self.from_y

    def over_x(self):
        if self.fast:
            n = self.parts[0].shape[0] // 2
            keep = self.st.now(self.parts[0])
            half = add_bf(keep[n:], self.got[n : 2 * n], self.from_y[n:])
            self.from_x = lax.ppermute(half, "x", SWAP)
            return self.from_x

    def over_z(self):
        if not self.fast:
            part = self.st.now(self.parts[0])
            self.terms = [lax.psum_scatter(part, ("z", "x"), scatter_dimension=0, tiled=True)]
            return self.terms
        m = self.parts[0].shape[0] // 2 // self.size_z
        keep = self.st.now(self.parts[0])
        self.terms = []
        for k in range(self.size_z):
            rows = slice(k * m, (k + 1) * m)
            term = add_bf(keep[rows], self.got[rows], self.from_y[rows], self.from_x[rows])
            self.terms.append(lax.ppermute(term, "z", xor_pairs(self.size_z, k)) if k else term)
        return self.terms

    def back_over_y(self):
        if self.fast:
            self.share = add_bf(self.st.now(self.terms[0]), *self.terms[1:])
            self.other = lax.ppermute(self.share, "y", SWAP)
            return self.other

    def total(self):
        if not self.fast:
            return [lax.psum(self.terms[0], ("y", "c"))]
        both = [self.share, self.other]
        return both + [self.st.permute(part, "c") for part in both]


def fold_in(v, axis, size, step=1):
    return v + lax.ppermute(v, axis, xor_pairs(size, step))


def gather_whole(own):
    return Parts([lax.all_gather(own, ("z", "x"), axis=0, tiled=True)])


class Geometry:
    pass


def local(
    geo,
    residual,
    out_grad,
    lengths,
    gain_one,
    qkv_weight,
    qv_bias,
    out_weight,
    out_bias,
    gain_two,
    fc_weight,
    fc_bias,
    proj_weight,
    proj_bias,
):
    geo.ranks = geo.seq
    geo.ns, geo.t, geo.narrow = residual.shape
    geo.wide, geo.ff = geo.narrow + 1, fc_weight.shape[1]
    narrow, wide, groups, ff = geo.narrow, geo.wide, geo.ranks, geo.ff
    heads, e = qv_bias.shape[0], qv_bias.shape[1] // 2
    size_z = geo.fsdp // 2
    geo.fast = (
        wide // geo.fsdp % 32 == 0
        and size_z & (size_z - 1) == 0
        and wide % (ff // size_z) == 0
        and ff // size_z % 64 == 0
    )
    z, x, y, c = (lax.axis_index(a) for a in ("z", "x", "y", "c"))
    idx = jnp.stack([z, x, y, c, 2 * y + c, z, z, z]).astype(jnp.int32)
    pad = lambda v: jnp.pad(v, (0, wide - narrow)).reshape(1, wide)
    gain1, gain2 = gain_one.reshape(1, wide), gain_two.reshape(1, wide)

    by_slot = qv_bias.reshape(groups, 3, 2 * e).transpose(1, 0, 2)
    q_bias = jnp.pad(by_slot[:, :, :e], ((0, 0), (0, 0), (0, e))).reshape(3, -1)
    bias = jnp.concatenate([q_bias, by_slot[:, :, e:].reshape(3, -1)], axis=1).reshape(1, -1)

    st = Stages(idx)
    own = prep_qkv(geo, idx, qkv_weight)
    bias_a, bias_b = bias[:, :wide], bias[:, wide:]
    if geo.fast:
        sides = [(dx, dc, 0, size_z, True) for dc in range(2) for dx in range(2)]
        whole = [own] + [lax.ppermute(own, "z", xor_pairs(size_z, i)) for i in range(1, size_z)]
        rest_own = prep_rest(geo, idx, out_weight, fc_weight, proj_weight)
        rest_own = lax.optimization_barrier((rest_own, whole[-1]))[0]
        rest = [lax.all_gather(rest_own, ("z", "x", "c"), axis=0, tiled=True)]
        st.end(whole)
        rows_a, rows_b = (
            jnp.concatenate([w[:, cut] for w in whole], axis=0)
            for cut in (slice(0, wide), slice(wide, 3 * wide))
        )
        other_a = st.permute(rows_a, "x")
        st.end(other_a)
        other_b = st.permute(rows_b, "x")
        w_a = [rows_a, other_a, st.permute(rows_a, "c"), st.permute(other_a, "c")]
        st.end(w_a)
        w_a = Parts(w_a, sides)
    else:
        w_a = gather_whole(own[:, :wide])
        w_b = gather_whole(own[:, wide:])
        widen = lambda w: jnp.pad(w, ((0, 0), (0, wide - narrow))).astype(BF)
        rest = [
            gather_whole(w).arrays[0]
            for w in (widen(out_weight), fc_weight.astype(BF), widen(proj_weight))
        ]
    sends, wq_a, (normed_one, normed_t) = qkv_forward(
        geo, st.token, residual, gain1, bias_a, w_a, (0,), True
    )
    st.end(sends)
    if geo.fast:
        w_b = Parts([rows_b, other_b, st.permute(rows_b, "c"), st.permute(other_b, "c")], sides)
    sends_b, wq_b, _ = qkv_forward(geo, idx, normed_one, gain1, bias_b, w_b, (1, 2), False)
    sends = list(sends) + list(sends_b)
    free = Stages(idx)
    slabs, saved, o_slabs = [], [], []
    for i in range(3):
        slabs.append(free.exchange(sends[4 * i : 4 * i + 4]))
    for i in range(3):
        o, stats = attention_forward(geo, idx, lengths, slabs[i])
        saved.append(stats)
        o_slabs += free.exchange(o)
    st.end(o_slabs)
    (output, d_pre, normed_two, attn, og, middle, bias_sums, out_w, d_norm), proj_parts = mlp_forward(
        geo,
        st.token,
        o_slabs,
        residual,
        out_grad,
        gain2,
        pad(out_bias),
        fc_bias.reshape(1, ff),
        pad(proj_bias),
        rest,
    )
    st.end(proj_parts)
    proj_red = Reduction(geo, st, proj_parts, (1, 1))
    got = proj_red.over_cores(), proj_red.prepare()
    (d_branch, d_mid, vectors), d_sends = mlp_backward(
        geo, st.token, d_norm, out_w, og, middle, gain2, bias_sums
    )
    st.end(got, d_branch)
    d_slabs = st.exchange(d_sends)
    got = proj_red.over_x()
    fo_red = Reduction(geo, st, grad_fo(geo, st.token, attn, d_branch, normed_two, d_pre), (1, 1))
    st.end(d_slabs, got, fo_red.parts)
    got = proj_red.over_x(), fo_red.over_cores(), fo_red.prepare()
    dq = attention_backward(geo, st.token, 0, lengths, slabs[0], saved[0], d_slabs)
    st.end(got, dq)
    dq_slabs = [st.exchange(dq)]
    proj_red.scatter_z()
    got = fo_red.over_x()
    dq = attention_backward(geo, st.token, 1, lengths, slabs[1], saved[1], d_slabs)
    st.end(got, dq, dq_slabs)
    dq_slabs.append(st.exchange(dq))
    got = fo_red.over_x()
    dq = attention_backward(geo, st.token, 2, lengths, slabs[2], saved[2], d_slabs)
    st.end(got, dq, dq_slabs)
    dq_slabs.append(st.exchange(dq))
    fo_red.scatter_z()
    parts_a, dt_a = grad_qkv(geo, st.token, dq_slabs[0] + dq_slabs[1], normed_t)
    red_a = Reduction(geo, st, parts_a, (1,))
    st.end(dq_slabs, parts_a)
    got = red_a.over_cores()
    parts_b, dt_b = grad_qkv(geo, st.token, dq_slabs[2], normed_t, last=True)
    red_b = LastReduction(geo, st, parts_b)
    st.end(got, parts_b)
    got = red_a.over_x(), proj_red.over_y(), red_b.over_cores(), red_b.over_y()
    input_grad, vecs = input_backward(
        geo,
        st.now(residual),
        gain1,
        (dt_a, dt_b),
        (wq_a, wq_b),
        d_mid,
        vectors,
    )
    if geo.fast:
        vecs = fold_in(vecs, "c", 2)
    else:
        vecs = lax.psum(vecs, ("z", "x", "y", "c"))
    st.end(got, vecs)
    got = red_a.over_z(*range(size_z)), red_b.over_x()
    if geo.fast:
        vecs = fold_in(st.now(vecs), "x", 2)
        got += (fo_red.over_y(vecs),)
    st.end(got, vecs)
    got = red_b.over_z(), red_a.over_y()
    proj_sum, fo_sum = proj_red.total(), fo_red.total()
    if geo.fast:
        vecs = fold_in(st.now(vecs), "y", 2)
    st.end(got, vecs, proj_sum, fo_sum)
    got = red_b.back_over_y()
    sum_a = red_a.total()
    if geo.fast:
        vecs = st.now(vecs)
        terms = [vecs] + [lax.ppermute(vecs, "z", xor_pairs(size_z, k)) for k in range(1, size_z)]
        while len(terms) > 1:
            terms = [a + b for a, b in zip(terms[::2], terms[1::2])]
        vecs = terms[0]
    st.end(got, vecs, sum_a)
    sum_b = red_b.total()
    sums = vecs[8:11].reshape(3, 3 * groups, e)
    q_sum = sums[:, : 2 * groups].reshape(3, groups, 2, e)[:, :, 0]
    v_sum = sums[:, 2 * groups :]
    qv_grad = jnp.concatenate([q_sum, v_sum], axis=2).transpose(1, 0, 2).reshape(heads, 2 * e)

    def plan_fo(ins, outs, at):
        outs[0][at, :] = ins[0][:, :narrow].astype(F32)
        outs[1][at, :] = ins[0][:, wide:].astype(F32)

    def plan_proj(ins, outs, at):
        outs[0][at, :] = ins[0][:, :narrow].astype(F32)

    block = wide // geo.fsdp
    qkv_grad = finish_qkv(geo, idx, sum_a, sum_b)
    out_w_grad, fc_w_grad = finish(geo, idx, [fo_sum], plan_fo, "finish_fo")(
        [sd(block, narrow, dtype=F32), sd(block, ff, dtype=F32)]
    )
    (proj_w_grad,) = finish(geo, idx, [proj_sum], plan_proj, "finish_proj")(
        [sd(ff // geo.fsdp, narrow, dtype=F32)]
    )
    return (
        output,
        input_grad,
        vecs[0],
        qkv_grad,
        qv_grad,
        out_w_grad,
        vecs[2, :narrow],
        vecs[1],
        fc_w_grad,
        vecs[4:8].reshape(-1),
        proj_w_grad,
        vecs[3, :narrow],
    )


def solution(mesh):
    geo = Geometry()
    geo.fsdp, geo.seq = mesh.devices.shape
    fine = Mesh(
        mesh.devices.reshape(geo.fsdp // 2, 2, geo.seq // 2, 2), ("z", "x", "y", "c")
    )
    fs, sq = ("z", "x"), ("y", "c")
    tokens, rows = P(fs, sq, None), P(fs, None)
    return jax.shard_map(
        functools.partial(local, geo),
        mesh=fine,
        in_specs=(
            tokens,
            tokens,
            rows,
            P(),
            rows,
            P(),
            rows,
            P(),
            P(),
            rows,
            P(),
            rows,
            P(),
        ),
        out_specs=(tokens, tokens, P(), rows, P(), rows, P(), P(), rows, P(), rows, P()),
        check_vma=False,
    )
```

```python
import functools

import jax
import jax.numpy as jnp
from jax import lax
from jax.experimental import pallas as pl
from jax.experimental.pallas import tpu as pltpu
from jax.sharding import Mesh, PartitionSpec as P

EPS = 1e-06
LONGEST = 512
BF = jnp.bfloat16
F32 = jnp.float32
VMEM_LIMIT = 60 * 1024 * 1024
SWAP = [(0, 1), (1, 0)]
GELU_K = 0.7978845608028654
GELU_C = 0.044715


def nn(a, b):
    return lax.dot_general(a, b, (((1,), (0,)), ((), ())), preferred_element_type=F32)


def nt(a, b):
    return lax.dot_general(a, b, (((1,), (1,)), ((), ())), preferred_element_type=F32)


def tn(a, b):
    return lax.dot_general(a, b, (((0,), (0,)), ((), ())), preferred_element_type=F32)


def lanes(shape):
    return lax.broadcasted_iota(jnp.int32, shape, 1)


def merge64(low, high):
    return jnp.where(lanes(low.shape) < 64, low, high)


def swap64(x):
    return pltpu.roll(x, 64, 1)


def fold_pair(x):
    n = x.shape[0] // 2
    top, bottom = x[:n], x[n:]
    return merge64(top, swap64(bottom)), merge64(swap64(top), bottom)


def unfold_pair(first, second):
    top = merge64(first, swap64(second))
    bottom = merge64(swap64(first), second)
    return jnp.concatenate([top, bottom], axis=0)


def vm():
    return pl.BlockSpec(memory_space=pltpu.VMEM)


def anyspace():
    return pl.BlockSpec(memory_space=pl.ANY)


def smem():
    return pl.BlockSpec(memory_space=pltpu.SMEM)


def cost(flops, nbytes, trans=0):
    scale = 0.1
    return pl.CostEstimate(
        flops=int(flops * scale), bytes_accessed=int(nbytes * scale), transcendentals=int(trans * scale)
    )


def params(**kw):
    return pltpu.CompilerParams(vmem_limit_bytes=VMEM_LIMIT, **kw)


def unit_order(groups):
    order = []
    for slot in range(3):
        for group in range(groups):
            order += [3 * (3 * group + slot), 3 * (3 * group + slot) + 1]
        for group in range(groups):
            order += [3 * (3 * group + slot) + 2]
    return order


def pick_units(load, low, high):
    def half(unit, side):
        block = load(unit // 2)
        return block if unit % 2 == side else swap64(block)

    return merge64(half(low, 0), half(high, 1))


def call(kernel, name, shapes, ins, specs, scratch, est, after=(), out_specs=None, **kw):
    if after:
        count, extra = len(ins), len(after)
        inner = kernel

        def kernel(*refs):
            inner(*refs[:count], *refs[count + extra :])

    many = isinstance(shapes, (tuple, list))
    return pl.pallas_call(
        kernel,
        out_shape=tuple(shapes) if many else shapes,
        in_specs=list(specs) + [anyspace()] * len(after),
        out_specs=out_specs or (tuple([vm()] * len(shapes)) if many else vm()),
        scratch_shapes=scratch,
        compiler_params=params(**kw),
        cost_estimate=est,
        name=name,
    )(*ins, *after)


def sd(*shape, dtype=BF):
    return jax.ShapeDtypeStruct(shape, dtype)


def prep_qkv(geo, idx, weight):
    rows = weight.shape[0] // 2 if geo.fast else weight.shape[0]
    width = weight.shape[1]
    order = unit_order(geo.ranks)

    def kernel(idx_ref, w_ref, o_ref):
        start = pl.multiple_of(idx_ref[3] * rows, 8) if geo.fast else 0
        for j in range(width // 128):
            o_ref[:, j * 128 : (j + 1) * 128] = pick_units(
                lambda b: w_ref[pl.ds(start, rows), b * 128 : (b + 1) * 128],
                order[2 * j],
                order[2 * j + 1],
            ).astype(BF)

    return call(
        kernel, "prep_qkv", sd(rows, width), (idx, weight), [smem(), vm()], [], cost(0, weight.size * 6)
    )


def prep_rest(geo, idx, out_w, fc_w, proj_w):
    div = 2 if geo.fast else 1
    rows = out_w.shape[0] // div
    wide, ff, narrow = geo.wide, fc_w.shape[1], out_w.shape[1]
    blocks = ff // wide

    def kernel(idx_ref, o_ref, f_ref, p_ref, all_ref):
        start = pl.multiple_of(idx_ref[3] * rows, 8) if geo.fast else 0
        pstart = pl.multiple_of(idx_ref[3] * rows * blocks, 8) if geo.fast else 0
        all_ref[...] = jnp.zeros(all_ref.shape, BF)
        all_ref[:, :narrow] = o_ref[pl.ds(start, rows), :].astype(BF)
        all_ref[:, wide : wide + ff] = f_ref[pl.ds(start, rows), :].astype(BF)
        for i in range(blocks):
            at = wide + ff + i * wide
            all_ref[:, at : at + narrow] = p_ref[pl.ds(pstart + i * rows, rows), :].astype(BF)

    return call(
        kernel,
        "prep_rest",
        sd(rows, wide + 2 * ff),
        (idx, out_w, fc_w, proj_w),
        [smem(), vm(), vm(), vm()],
        [],
        cost(0, 6 * (out_w.size + fc_w.size + proj_w.size)),
    )


class Parts:
    def __init__(self, arrays, coords=None):
        self.arrays, self.coords = list(arrays), coords

    def copies(self, geo, idx_ref, refs, dst, sem, src_cols=None):
        made = []
        if self.coords is None:
            src = refs[0] if src_cols is None else refs[0].at[:, src_cols]
            return [pltpu.make_async_copy(src, dst, sem)]
        for ref, (dx, dc, first, count, relative) in zip(refs, self.coords):
            n = ref.shape[0] // count
            for zz in range(count):
                z = idx_ref[0] ^ (first + zz) if relative else first + zz
                start = ((z * 2 + (idx_ref[1] ^ dx)) * 2 + (idx_ref[3] ^ dc)) * n
                rows = pl.ds(zz * n, n)
                src = ref.at[rows] if src_cols is None else ref.at[rows, src_cols]
                made.append(
                    pltpu.make_async_copy(src, dst.at[pl.ds(pl.multiple_of(start, 16), n)], sem)
                )
        return made


def norm_rows(x, narrow, wide):
    full = jnp.where(lanes(x.shape) == narrow, -jnp.sum(x, 1, keepdims=True), x)
    return full, lax.rsqrt(jnp.sum(full * full, 1, keepdims=True) * (1.0 / wide) + EPS)


def qkv_forward(geo, idx, source, gain, bias, parts, slots, first):
    groups, t, ns, narrow = geo.ranks, geo.t, geo.ns, geo.narrow
    wide, tokens = geo.wide, geo.ns * geo.t
    cols, slab_rows = len(slots) * geo.wide, tokens + tokens // 2
    count = len(parts.arrays)
    n_out = len(slots) * 4

    def kernel(idx_ref, x_ref, gain_ref, bias_ref, *refs):
        w_parts, outs = refs[:count], refs[count : count + n_out]
        refs = refs[count + n_out :]
        w_ref, refs = refs[0], refs[1:]
        if first:
            normed_ref, trans_ref, slab, sem, row = refs
        else:
            slab, sem = refs
            normed_ref = x_ref
        copies = parts.copies(geo, idx_ref, w_parts, w_ref, sem)
        for copy in copies:
            copy.start()
        if first:
            def norm(s, carry):
                at = pl.ds(pl.multiple_of(s * t, 16), t)
                row[at, :] = jnp.zeros((t, wide), F32)
                row[at, :narrow] = x_ref[s].astype(F32)
                full, inv = norm_rows(row[at, :], narrow, wide)
                normed_ref[at, :] = (full * inv * gain_ref[...]).astype(BF)
                return carry

            lax.fori_loop(0, ns, norm, 0)
            trans_ref[...] = normed_ref[...].T
        for copy in copies:
            copy.wait()

        def one(i, carry):
            base = pl.multiple_of(i * wide, 128)
            for j in range(groups // 2):
                at = pl.ds(base + 256 * j, 256)
                y = nn(normed_ref[...], w_ref[:, at]) + bias_ref[:, at]
                for half in range(2):
                    slab[i * groups + 2 * j + half, :tokens, :] = y[
                        :, half * 128 : (half + 1) * 128
                    ].astype(BF)
            at = pl.ds(base + 128 * groups, 64 * groups)
            y = nn(normed_ref[...], w_ref[:, at]) + bias_ref[:, at]
            for s in range(ns):
                rows = slice(tokens + s * (t // 2), tokens + (s + 1) * (t // 2))
                for p in range(groups // 2):
                    pair = fold_pair(y[s * t : (s + 1) * t, p * 128 : (p + 1) * 128])
                    for half in range(2):
                        slab[i * groups + 2 * p + half, rows, :] = pair[half].astype(BF)
            return carry

        lax.fori_loop(0, len(slots), one, 0)
        for i in range(len(slots)):
            store_slabs(outs[4 * i : 4 * i + 4], slab, idx_ref, i * groups)

    shapes = slab_set(slab_rows) * len(slots) + [sd(wide, cols)]
    scratch = [pltpu.VMEM((len(slots) * groups, slab_rows, 128), BF), pltpu.SemaphoreType.DMA]
    if first:
        shapes += [sd(tokens, wide), sd(wide, tokens)]
        scratch += [pltpu.VMEM((tokens, wide), F32)]
    out = call(
        kernel,
        "qkv_forward",
        shapes,
        (idx, source, gain, bias, *parts.arrays),
        [smem(), vm(), vm(), vm()] + [anyspace()] * count,
        scratch,
        cost(2 * tokens * wide * cols, 6e6),
    )
    return out[:n_out], out[n_out], out[n_out + 1 :]


def doc_start(len_ref, s, pos, ndoc):
    start = jnp.zeros(pos.shape, jnp.int32)
    edge = len_ref[s, 0]
    for n in range(1, ndoc):
        start = jnp.where(pos >= edge, edge, start)
        edge = edge + len_ref[s, n]
    return start


def first_key(block, t):
    return max(0, block * t - (LONGEST - 1)) // t


def allowed(start, block, key_block, t):
    k_pos = lax.broadcasted_iota(jnp.int32, (t, t), 0)
    seen = k_pos >= start - key_block * t
    if key_block == block:
        seen = seen & (k_pos <= lanes((1, t)))
    return seen


def store_slabs(outs, slab, idx_ref, base=0):
    for k, ref in enumerate(outs):
        ref[...] = slab[base + (idx_ref[4] ^ k)]


def load_slabs(slab, refs, idx_ref, base=0):
    for k, ref in enumerate(refs):
        slab[base + (idx_ref[4] ^ k)] = ref[...]


def slab_set(rows):
    return [sd(rows, 128)] * 4


class Stages:
    def __init__(self, idx):
        self.token = idx

    def end(self, *results):
        self.token = lax.optimization_barrier((self.token, *jax.tree.leaves(results)))[0]

    def now(self, x):
        return lax.optimization_barrier((x, self.token))[0]

    def permute(self, x, axis, pairs=SWAP):
        return lax.ppermute(self.now(x), axis, pairs)

    def exchange(self, slabs):
        return [slabs[0]] + [
            self.permute(slabs[k], ("y", "c"), xor_pairs(len(slabs), k)) for k in range(1, len(slabs))
        ]


def unfold_one(x):
    return jnp.concatenate([x, swap64(x)], axis=0)


def fold_one(x):
    n = x.shape[0] // 2
    return merge64(x[:n], swap64(x[n:]))


def attention_forward(geo, idx, lengths, slabs, after=()):
    groups, t, ns = geo.ranks, geo.t, geo.ns
    full, tokens, ndoc = groups * t, ns * t, lengths.shape[1]

    def kernel(idx_ref, len_ref, *refs):
        outs, lse_ref, ot_ref = refs[4:8], refs[8], refs[9]
        slab, qs, ks, vt, osl = refs[10:]
        load_slabs(slab, refs[:4], idx_ref)
        low = lanes((t, 128)) < 64

        def one(s, carry):
            at = pl.ds(pl.multiple_of(s * t, 16), t)
            folded = pl.ds(pl.multiple_of(tokens + s * (t // 2), 16), t // 2)
            for d in range(groups):
                rows = slice(d * t, (d + 1) * t)
                qk = slab[d, at, :].astype(F32)
                qs[rows, :] = jnp.where(low, qk * 0.125, 0.0).astype(BF)
                ks[rows, :] = swap64(qk).astype(BF)
                v = unfold_one(slab[d, folded, :].astype(F32))
                vt[:, rows] = jnp.where(low, v, 1.0).T.astype(BF)
            for d in range(groups):
                first = first_key(d, t)
                rows = slice(d * t, (d + 1) * t)
                start = doc_start(len_ref, s, d * t + lanes((1, t)), ndoc)
                blocks = []
                for b in range(first, d + 1):
                    scores = nt(ks[b * t : (b + 1) * t, :], qs[rows, :])
                    blocks.append(jnp.where(allowed(start, d, b, t), scores, -1e30))
                top = jnp.max(blocks[0], 0, keepdims=True)
                for block in blocks[1:]:
                    top = jnp.maximum(top, jnp.max(block, 0, keepdims=True))
                weight = jnp.concatenate([jnp.exp(block - top).astype(BF) for block in blocks], axis=0)
                o = nn(vt[:, first * t : (d + 1) * t], weight)
                total = o[64:65, :]
                lse_ref[s, d : d + 1, :] = top + jnp.log(total)
                o = o * (1.0 / total)
                ot_ref[s, d] = o[:64]
                osl[d, pl.ds(pl.multiple_of(s * (t // 2), 16), t // 2), :] = fold_one(o.T).astype(BF)
            return carry

        lax.fori_loop(0, ns, one, 0)
        store_slabs(outs, osl, idx_ref)

    shapes = slab_set(tokens // 2) + [sd(ns, 8, t, dtype=F32), sd(ns, groups, 64, t, dtype=F32)]
    out = call(
        kernel,
        "attention_forward",
        shapes,
        (idx, lengths, *slabs),
        [smem(), smem()] + [vm()] * 4,
        [
            pltpu.VMEM((groups, tokens + tokens // 2, 128), BF),
            pltpu.VMEM((full, 128), BF),
            pltpu.VMEM((full, 128), BF),
            pltpu.VMEM((128, full), BF),
            pltpu.VMEM((groups, tokens // 2, 128), BF),
        ],
        cost(4 * 4 * ns * full * full * 32, 4e6, ns * full * full // 2),
        after,
    )
    return out[:4], out[4:]


def attention_backward(geo, idx, slot, lengths, slabs, saved, d_slabs, after=()):
    groups, t, ns = geo.ranks, geo.t, geo.ns
    full, tokens, ndoc = groups * t, ns * t, lengths.shape[1]

    def kernel(idx_ref, len_ref, slot_ref, lse_ref, ot_ref, *refs):
        outs = refs[8:12]
        slab, gsl, qs, ks, kt, vs, right, delta, dvk, dq, dsl = refs[12:]
        load_slabs(slab, refs[:4], idx_ref)
        part = pl.ds(pl.multiple_of(slot_ref[0] * (tokens // 2), 128), tokens // 2)
        load_slabs(gsl, [ref.at[part] for ref in refs[4:8]], idx_ref)
        low = lanes((t, 128)) < 64

        def one(s, carry):
            at = pl.ds(pl.multiple_of(s * t, 16), t)
            folded = pl.ds(pl.multiple_of(tokens + s * (t // 2), 16), t // 2)
            o_rows = pl.ds(pl.multiple_of(s * (t // 2), 16), t // 2)
            for d in range(groups):
                rows = slice(d * t, (d + 1) * t)
                qk = slab[d, at, :].astype(F32)
                key = swap64(qk)
                q = jnp.where(low, qk * 0.125, 0.0)
                qs[rows, :] = q.astype(BF)
                ks[rows, :] = key.astype(BF)
                kt[:, rows] = key.T[:64].astype(BF)
                vs[rows, :] = unfold_one(slab[d, folded, :].astype(F32)).astype(BF)
                grad = jnp.where(low, unfold_one(gsl[d, o_rows, :].astype(F32)), 0.0)
                right[d, :t, :] = grad.astype(BF)
                right[d, t:, :] = swap64(q).astype(BF)
                delta[d : d + 1, :] = jnp.sum(grad.T[:64] * ot_ref[s, d], 0, keepdims=True)
            dvk[...] = jnp.zeros((full, 128), F32)
            for d in range(groups):
                rows = slice(d * t, (d + 1) * t)
                start = doc_start(len_ref, s, d * t + lanes((1, t)), ndoc)
                lse_row, delta_row = lse_ref[s, d : d + 1, :], delta[d : d + 1, :]
                total = jnp.zeros((64, t), F32)
                for b in range(first_key(d, t), d + 1):
                    keys = slice(b * t, (b + 1) * t)
                    scores = nt(ks[keys, :], qs[rows, :])
                    scores = jnp.where(allowed(start, d, b, t), scores, -1e30)
                    prob = jnp.exp(scores - lse_row)
                    d_prob = nt(vs[keys, :], right[d, :t, :])
                    ds = (prob * (d_prob - delta_row)).astype(BF)
                    dvk[keys, :] += nn(jnp.concatenate([prob.astype(BF), ds], axis=1), right[d])
                    total = total + nn(kt[:, keys], ds)
                dq[rows, :] = jnp.concatenate([total, total], axis=0).T * 0.125
            for d in range(groups):
                rows = slice(d * t, (d + 1) * t)
                both = dvk[rows, :]
                dsl[d, at, :] = merge64(dq[rows, :], both).astype(BF)
                dsl[d, folded, :] = fold_one(both).astype(BF)
            return carry

        lax.fori_loop(0, ns, one, 0)
        store_slabs(outs, dsl, idx_ref)

    slab_rows = tokens + tokens // 2
    flat = pltpu.VMEM((full, 128), BF)
    return call(
        kernel,
        "attention_backward",
        slab_set(slab_rows),
        (idx, lengths, jnp.array([slot], jnp.int32), *saved, *slabs, *d_slabs),
        [smem()] * 3 + [vm()] * 10,
        [
            pltpu.VMEM((groups, slab_rows, 128), BF),
            pltpu.VMEM((groups, tokens // 2, 128), BF),
            flat,
            flat,
            pltpu.VMEM((64, full), BF),
            flat,
            pltpu.VMEM((groups, 2 * t, 128), BF),
            pltpu.VMEM((8, t), F32),
            pltpu.VMEM((full, 128), F32),
            pltpu.VMEM((full, 128), F32),
            pltpu.VMEM((groups, slab_rows, 128), BF),
        ],
        cost(10 * 4 * ns * full * full * 32, 5e6, ns * full * full // 2),
        after,
    )


def mlp_forward(geo, idx, o_slabs, residual, out_grad, gain, out_bias, fc_bias, proj_bias, weights):
    groups, t, ns, narrow = geo.ranks, geo.t, geo.ns, geo.narrow
    wide, ff, tokens = geo.wide, geo.ff, geo.ns * geo.t
    n_slab, blocks = len(o_slabs), geo.ff // geo.wide
    rows = (wide // geo.fsdp) // (2 if geo.fast else 1)
    shares = wide // rows
    proj_shapes = part_shapes(geo, ff, wide)
    chunk = 512
    size_z = geo.fsdp // 2 if geo.fast else 1
    per_z = ff // size_z

    def kernel(idx_ref, *refs):
        slabs, refs = refs[:n_slab], refs[n_slab:]
        x_ref, og_ref, gain_ref, ob_ref, fb_ref, pb_ref = refs[:6]
        w_refs, refs = refs[6 : 6 + len(weights)], refs[6 + len(weights) :]
        out_ref, dpre_out, n_out, a_out, ogp_out, mid_out, bias_ref, wo_out, dn_ref = refs[:9]
        p_refs = refs[9 : 9 + len(proj_shapes)]
        refs = refs[9 + len(proj_shapes) :]
        wf, wp, osl, acc, tile, dpre_ref, n_ref, a_ref, ogp_ref, mid_ref, wo_ref, sem = refs
        early = [
            pltpu.make_async_copy(src, dst, sem.at[3 + i])
            for i, (src, dst) in enumerate(
                (
                    (ogp_ref, ogp_out),
                    (wo_ref, wo_out),
                    (a_ref, a_out),
                    (mid_ref, mid_out),
                    (n_ref, n_out),
                )
            )
        ]

        def d_pre_copy(i):
            cols = pl.ds(pl.multiple_of(i * chunk, 128), chunk)
            return pltpu.make_async_copy(dpre_ref.at[:, cols], dpre_out.at[:, cols], sem.at[8])

        def part_copies(zz):
            if not geo.fast:
                rows = pl.ds(zz * per_z, per_z)
                return [pltpu.make_async_copy(tile.at[rows], p_refs[0].at[rows], sem.at[9])]
            n = per_z // 4
            made = []
            for dx in range(2):
                for dc in range(2):
                    start = zz * per_z + ((idx_ref[1] ^ dx) * 2 + (idx_ref[3] ^ dc)) * n
                    made.append(
                        pltpu.make_async_copy(
                            tile.at[pl.ds(pl.multiple_of(start, 16), n)],
                            p_refs[dc].at[pl.ds((dx * size_z + zz) * n, n)],
                            sem.at[9],
                        )
                    )
            return made

        if geo.fast:
            (all_ref,) = w_refs
            out_src, fc_src = all_ref.at[:, pl.ds(0, wide)], all_ref.at[:, pl.ds(wide, ff)]
            to_proj = [
                pltpu.make_async_copy(
                    all_ref.at[pl.ds(share * rows, rows), pl.ds(wide + ff + i * wide, wide)],
                    wp.at[pl.ds((share * blocks + i) * rows, rows)],
                    sem.at[2],
                )
                for share in range(shares)
                for i in range(blocks)
            ]
        else:
            out_src, fc_src, proj_src = w_refs
            to_proj = [pltpu.make_async_copy(proj_src, wp, sem.at[2])]
        to_out = pltpu.make_async_copy(out_src, wp.at[pl.ds(0, wide)], sem.at[0])
        to_fc = pltpu.make_async_copy(fc_src, wf, sem.at[1])
        to_out.start()
        to_fc.start()
        for i in range(3):
            load_slabs(osl, slabs[4 * i : 4 * i + 4], idx_ref, i * groups)

        def load(s, carry):
            at = pl.ds(pl.multiple_of(s * t, 16), t)
            acc[at, :] = jnp.zeros((t, wide), F32)
            acc[at, :narrow] = og_ref[s].astype(F32)
            ogp_ref[at, :] = acc[at, :].astype(BF)
            acc[at, :narrow] = x_ref[s].astype(F32)
            dn_ref[at, :] = jnp.zeros((t, wide), F32)
            return carry

        lax.fori_loop(0, ns, load, 0)
        early[0].start()

        def assemble(i, carry):
            for p in range(groups // 2):
                at = pl.ds(pl.multiple_of(i * 64 * groups + 128 * p, 128), 128)
                for s in range(ns):
                    folded = slice(s * (t // 2), (s + 1) * (t // 2))
                    a_ref[s * t : (s + 1) * t, at] = unfold_pair(
                        osl[i * groups + 2 * p, folded, :].astype(F32),
                        osl[i * groups + 2 * p + 1, folded, :].astype(F32),
                    ).astype(BF)
            return carry

        lax.fori_loop(0, 3, assemble, 0)
        to_out.wait()
        for slot in range(3):
            for g in range(groups):
                at, head = 64 * (slot * groups + g), 3 * g + slot
                wo_ref[at : at + 64, :] = wp[64 * head : 64 * (head + 1), :]
        for copy in to_proj + early[1:3]:
            copy.start()

        def project(i, carry):
            cols = pl.ds(pl.multiple_of(i * 256, 128), 256)
            acc[:, cols] += nn(a_ref[...], wo_ref[:, cols]) + ob_ref[:, cols]
            return carry

        lax.fori_loop(0, wide // 256, project, 0)

        def norm(s, carry):
            at = pl.ds(pl.multiple_of(s * t, 16), t)
            full, inv = norm_rows(acc[at, :], narrow, wide)
            mid_ref[at, :] = full
            n_ref[at, :] = (full * inv * gain_ref[...]).astype(BF)
            return carry

        lax.fori_loop(0, ns, norm, 0)
        for copy in early[3:]:
            copy.start()
        to_fc.wait()
        for copy in to_proj:
            copy.wait()

        def one(i, carry):
            cols = pl.ds(pl.multiple_of(i * chunk, 128), chunk)
            w1, w2 = wf[:, cols], wp[cols, :]
            u = nn(n_ref[...], w1) + fb_ref[:, cols]
            square = u * u
            th = jnp.tanh(u * (GELU_K + GELU_K * GELU_C * square))
            half = 0.5 + 0.5 * th
            hidden = (u * half).astype(BF)
            slope = half + (0.5 * u) * (1.0 - th * th) * (GELU_K + 3.0 * GELU_K * GELU_C * square)
            acc[...] += nn(hidden, w2)
            d_pre = (nt(ogp_ref[...], w2) * slope).astype(BF)
            dpre_ref[:, cols] = d_pre
            d_pre_copy(i).start()
            bias_ref[0:1, cols] = jnp.sum(d_pre.astype(F32), 0, keepdims=True)
            dn_ref[...] += nt(d_pre, w1)
            tile[cols, :] = tn(hidden, ogp_ref[...]).astype(BF)
            for zz in range(size_z):

                @pl.when(i == ((zz + 1) * per_z - 1) // chunk)
                def _(zz=zz):
                    for copy in part_copies(zz):
                        copy.start()

            return carry

        lax.fori_loop(0, ff // chunk, one, 0)

        def store(s, carry):
            at = pl.ds(pl.multiple_of(s * t, 16), t)
            out_ref[s] = (acc[at, :] + pb_ref[...])[:, :narrow].astype(BF)
            return carry

        lax.fori_loop(0, ns, store, 0)
        for copy in early + [d_pre_copy(i) for i in range(ff // chunk)]:
            copy.wait()
        for zz in range(size_z):
            for copy in part_copies(zz):
                copy.wait()

    shapes = [
        sd(ns, t, narrow),
        sd(tokens, ff),
        sd(tokens, wide),
        sd(tokens, wide),
        sd(tokens, wide),
        sd(tokens, wide, dtype=F32),
        sd(8, ff, dtype=F32),
        sd(wide, wide),
        sd(tokens, wide, dtype=F32),
    ]
    out = call(
        kernel,
        "mlp_forward",
        shapes + proj_shapes,
        (idx, *o_slabs, residual, out_grad, gain, out_bias, fc_bias, proj_bias, *weights),
        [smem()] + [vm()] * (n_slab + 6) + [anyspace()] * len(weights),
        [
            pltpu.VMEM((wide, ff), BF),
            pltpu.VMEM((ff, wide), BF),
            pltpu.VMEM((3 * groups, tokens // 2, 128), BF),
            pltpu.VMEM((tokens, wide), F32),
            pltpu.VMEM((ff, wide), BF),
            pltpu.VMEM((tokens, ff), BF),
            pltpu.VMEM((tokens, wide), BF),
            pltpu.VMEM((tokens, wide), BF),
            pltpu.VMEM((tokens, wide), BF),
            pltpu.VMEM((tokens, wide), F32),
            pltpu.VMEM((wide, wide), BF),
            pltpu.SemaphoreType.DMA((10,)),
        ],
        cost(2 * tokens * wide * (5 * ff + wide), 34e6, tokens * ff),
        out_specs=tuple(
            vm() if i in (0, 6, 8) else anyspace() for i in range(len(shapes) + len(proj_shapes))
        ),
    )
    return out[: len(shapes)], out[len(shapes) :]


def mlp_backward(geo, idx, d_norm, out_w, og, middle, gain, bias_sums):
    groups, t, ns, narrow = geo.ranks, geo.t, geo.ns, geo.narrow
    wide, ff, tokens = geo.wide, geo.ff, geo.ns * geo.t
    n_slab = 4

    def kernel(idx_ref, dn, wo_ref, og_ref, mid_ref, gain_ref, bias_ref, *refs):
        db_ref, dmid_ref, vec_ref = refs[:3]
        outs = refs[3 : 3 + n_slab]
        da, dsl = refs[3 + n_slab :]
        vec_ref[0:1, :] = bias_ref[0:1, :]
        vec_ref[1:8, :] = jnp.zeros((7, ff), F32)

        def norm(s, carry):
            at = pl.ds(pl.multiple_of(s * t, 16), t)
            full = mid_ref[at, :]
            inv = lax.rsqrt(jnp.sum(full * full, 1, keepdims=True) * (1.0 / wide) + EPS)
            m, grad = full * inv, dn[at, :]
            dm = grad * gain_ref[...]
            d_full = inv * (dm - m * (jnp.sum(dm * m, 1, keepdims=True) * (1.0 / wide)))
            last = jnp.sum(jnp.where(lanes((t, wide)) == narrow, d_full, 0.0), 1, keepdims=True)
            og_f = og_ref[at, :].astype(F32)
            d_mid = og_f + (d_full - last)
            d_branch = d_mid.astype(BF)
            dmid_ref[at, :] = d_mid
            db_ref[at, :] = d_branch
            vec_ref[1:2, :wide] += jnp.sum(grad * m, 0, keepdims=True)
            vec_ref[2:3, :wide] += jnp.sum(d_branch.astype(F32), 0, keepdims=True)
            vec_ref[3:4, :wide] += jnp.sum(og_f, 0, keepdims=True)
            da[at, :] = nt(d_branch, wo_ref[...])
            return carry

        lax.fori_loop(0, ns, norm, 0)

        def fold(i, carry):
            for p in range(groups // 2):
                at = pl.ds(pl.multiple_of(i * 64 * groups + 128 * p, 128), 128)
                for s in range(ns):
                    pair = fold_pair(da[s * t : (s + 1) * t, at])
                    for half in range(2):
                        dest = pl.multiple_of(i * (tokens // 2) + s * (t // 2), 16)
                        dsl[2 * p + half, pl.ds(dest, t // 2), :] = pair[half].astype(BF)
            return carry

        lax.fori_loop(0, 3, fold, 0)
        store_slabs(outs, dsl, idx_ref)

    out = call(
        kernel,
        "mlp_backward",
        [sd(tokens, wide), sd(tokens, wide, dtype=F32), sd(8, ff, dtype=F32)] + slab_set(3 * tokens // 2),
        (idx, d_norm, out_w, og, middle, gain, bias_sums),
        [smem()] + [vm()] * 6,
        [
            pltpu.VMEM((tokens, wide), F32),
            pltpu.VMEM((groups, 3 * tokens // 2, 128), BF),
        ],
        cost(2 * tokens * wide * wide, 12e6),
    )
    return out[:3], out[3:]


def part_shapes(geo, rows, cols):
    return [sd(rows // 2, cols)] * 2 if geo.fast else [sd(rows, cols)]


def emit_rows(geo, idx_ref, outs, tile, total, cols, relative):
    if not geo.fast:
        outs[0][:, cols] = tile[...]
        return
    size_z = geo.fsdp // 2
    n = total // geo.fsdp // 2
    for dx in range(2):
        for zz in range(size_z):
            z = idx_ref[0] ^ zz if relative else zz
            for dc in range(2):
                start = ((z * 2 + (idx_ref[1] ^ dx)) * 2 + (idx_ref[3] ^ dc)) * n
                at = (dx * size_z + zz) * n
                outs[dc][at : at + n, cols] = tile[pl.ds(pl.multiple_of(start, 16), n), :]


def grad_fo(geo, idx, attn, d_branch, normed, d_pre, after=()):
    tokens, ff = d_pre.shape
    wide, groups, chunk = geo.wide, geo.ranks, 768
    shapes = part_shapes(geo, wide, wide + ff)

    def kernel(idx_ref, a_ref, db_ref, n_ref, dp_ref, *refs):
        outs, (trans, tile, nat) = refs[:-3], refs[-3:]
        trans[...] = n_ref[...].T
        nat[...] = tn(a_ref[...], db_ref[...]).astype(BF)
        for slot in range(3):
            for g in range(groups):
                at, head = 64 * (slot * groups + g), 3 * g + slot
                tile[64 * head : 64 * (head + 1), :] = nat[at : at + 64, :]
        emit_rows(geo, idx_ref, outs, tile, wide, slice(0, wide), False)

        def one(i, carry):
            at = pl.multiple_of(i * chunk, 128)
            tile[...] = nn(trans[...], dp_ref[:, pl.ds(at, chunk)]).astype(BF)
            emit_rows(geo, idx_ref, outs, tile, wide, pl.ds(at + wide, chunk), False)
            return carry

        lax.fori_loop(0, ff // chunk, one, 0)

    return call(
        kernel,
        "grad_fo",
        shapes,
        (idx, attn, d_branch, normed, d_pre),
        [smem()] + [vm()] * 4,
        [
            pltpu.VMEM((wide, tokens), BF),
            pltpu.VMEM((wide, wide), BF),
            pltpu.VMEM((wide, wide), BF),
        ],
        cost(2 * tokens * (ff + wide) * wide, 16e6),
        after,
    )


def grad_qkv(geo, idx, slabs, trans, last=False, after=()):
    groups, t, ns, wide = geo.ranks, geo.t, geo.ns, geo.wide
    slots, tokens = len(slabs) // 4, geo.ns * geo.t
    shapes = part_shapes(geo, wide, slots * wide)
    by_y = last and geo.fast
    width = wide // 2 if by_y else wide
    if by_y:
        shapes = [sd(wide // 2, width), sd(wide // 2, width), sd(wide, width)]

    def kernel(idx_ref, *refs):
        ins, t_ref = refs[: slots * 4], refs[slots * 4]
        refs = refs[slots * 4 + 1 :]
        outs = refs[: len(shapes)]
        dt_ref, tile = refs[len(shapes)], refs[len(shapes) + 1]
        slab = refs[-1]
        for i in range(slots):
            load_slabs(slab.at[i], ins[4 * i : 4 * i + 4], idx_ref)

        def one(i, carry):
            base = pl.multiple_of(i * wide, 128)
            for g in range(groups):
                dt_ref[:, pl.ds(base + 128 * g, 128)] = slab[i, g, :tokens, :]
            for p in range(groups // 2):
                at = pl.ds(base + 128 * (groups + p), 128)
                for s in range(ns):
                    folded = slice(tokens + s * (t // 2), tokens + (s + 1) * (t // 2))
                    dt_ref[s * t : (s + 1) * t, at] = unfold_pair(
                        slab[i, 2 * p, folded, :].astype(F32), slab[i, 2 * p + 1, folded, :].astype(F32)
                    ).astype(BF)
            return carry

        def multiply(i, carry):
            at = pl.ds(pl.multiple_of(i * width, 128), width)
            tile[...] = nn(t_ref[...], dt_ref[:, at]).astype(BF)
            emit_rows(geo, idx_ref, outs, tile, wide, at, True)
            return carry

        def multiply_half(i):
            at = pl.ds(pl.multiple_of((idx_ref[2] ^ i) * width, 128), width)
            tile[...] = nn(t_ref[...], dt_ref[:, at]).astype(BF)
            pair = (outs[i], outs[2].at[pl.ds(i * (wide // 2), wide // 2)])
            emit_rows(geo, idx_ref, pair, tile, wide, slice(0, width), True)

        lax.fori_loop(0, slots, one, 0)
        if by_y:
            multiply_half(0)
            multiply_half(1)
        else:
            lax.fori_loop(0, slots * wide // width, multiply, 0)

    out = call(
        kernel,
        "grad_qkv",
        shapes + [sd(tokens, slots * wide)],
        (idx, *slabs, trans),
        [smem()] + [vm()] * (slots * 4 + 1),
        [
            pltpu.VMEM((wide, width), BF),
            pltpu.VMEM((slots, groups, tokens + tokens // 2, 128), BF),
        ],
        cost(2 * tokens * slots * wide * wide, 4e6 * slots),
        after,
    )
    return out[:-1], out[-1]


def input_backward(geo, residual, gain, d_tokens, weights, d_mid, vectors, after=()):
    ns, t, narrow, wide, ff = geo.ns, geo.t, geo.narrow, geo.wide, geo.ff
    tokens, n, nw = ns * t, len(d_tokens), len(weights)

    def kernel(x_ref, gain_ref, dmid_ref, v_ref, *refs):
        dts, ws, (o_ref, vec_ref, row) = refs[:n], refs[n : n + nw], refs[n + nw :]
        vec_ref[...] = jnp.zeros(vec_ref.shape, F32)
        for i in range(3):
            vec_ref[1 + i : 2 + i, :] = v_ref[1 + i : 2 + i, :wide]
        for i in range(ff // wide):
            vec_ref[4 + i : 5 + i, :] = v_ref[0:1, i * wide : (i + 1) * wide]
        row[...] = jnp.zeros((t, wide), F32)
        slots = lambda refs: [
            (ref, slice(j * wide, (j + 1) * wide)) for ref in refs for j in range(ref.shape[1] // wide)
        ]

        def one(s, carry):
            rows = pl.ds(pl.multiple_of(s * t, 16), t)
            row[:, :narrow] = x_ref[s].astype(F32)
            full, inv = norm_rows(row[...], narrow, wide)
            grad = jnp.zeros((t, wide), F32)
            for i, ((dt, cols), (w, w_cols)) in enumerate(zip(slots(dts), slots(ws))):
                d_tok = dt[rows, cols]
                vec_ref[8 + i : 9 + i, :] += jnp.sum(d_tok.astype(F32), 0, keepdims=True)
                grad = grad + nt(d_tok, w[:, w_cols])
            m = full * inv
            vec_ref[0:1, :] += jnp.sum(grad * m, 0, keepdims=True)
            dm = grad * gain_ref[...]
            d_full = inv * (dm - m * (jnp.sum(dm * m, 1, keepdims=True) * (1.0 / wide)))
            last = jnp.sum(jnp.where(lanes((t, wide)) == narrow, d_full, 0.0), 1, keepdims=True)
            o_ref[s] = (dmid_ref[rows, :] + (d_full - last))[:, :narrow]
            return carry

        lax.fori_loop(0, ns, one, 0)

    return call(
        kernel,
        "input_backward",
        [sd(ns, t, narrow, dtype=F32), sd(16, wide, dtype=F32)],
        (residual, gain, d_mid, vectors, *d_tokens, *weights),
        [vm()] * (4 + n + nw),
        [pltpu.VMEM((t, wide), F32)],
        cost(2 * tokens * 3 * wide * wide, 14e6),
        after,
    )


def finish(geo, idx, pairs, plan, name):
    n = len(pairs)
    half = pairs[0][0].shape[0]
    rows = 2 * half if geo.fast else half
    sides = 2 if geo.fast else 1

    def kernel(idx_ref, *refs):
        outs = refs[n * sides :]
        for side in range(sides):
            at = pl.ds(pl.multiple_of((idx_ref[3] ^ side) * half, 8), half) if geo.fast else slice(0, rows)
            plan([refs[i * sides + side] for i in range(n)], outs, at)

    return lambda shapes: call(
        kernel,
        name,
        shapes,
        (idx, *[a for pair in pairs for a in pair[:sides]]),
        [smem()] + [vm()] * (n * sides),
        [],
        cost(0, rows * 3072 * 6),
    )


def finish_qkv(geo, idx, first, last):
    half, cols = first[0].shape
    wide = geo.wide
    rows, sides = (2 * half, 2) if geo.fast else (half, 1)
    where = {unit: at for at, unit in enumerate(unit_order(geo.ranks))}
    first = first[:sides]

    def kernel(idx_ref, *refs):
        a_refs, b_refs, (o_ref, b_all) = refs[:sides], refs[sides:-2], refs[-2:]
        for side in range(sides):
            at = pl.ds(pl.multiple_of((idx_ref[3] ^ side) * half, 8), half) if geo.fast else slice(0, rows)
            if geo.fast:
                for i in range(2):
                    cut = pl.ds(pl.multiple_of((idx_ref[2] ^ i) * (wide // 2), 128), wide // 2)
                    b_all[:, cut] = b_refs[2 * side + i][...].astype(F32)
            else:
                b_all[...] = b_refs[0][...].astype(F32)

            def read(b, a_ref=a_refs[side]):
                if b < cols // 128:
                    return a_ref[:, b * 128 : (b + 1) * 128].astype(F32)
                return b_all[:, b * 128 - cols : (b + 1) * 128 - cols]

            for j in range(3 * wide // 128):
                o_ref[at, j * 128 : (j + 1) * 128] = pick_units(read, where[2 * j], where[2 * j + 1])

    return call(
        kernel,
        "finish_qkv",
        sd(rows, 3 * wide, dtype=F32),
        (idx, *first, *last),
        [smem()] + [vm()] * (len(first) + len(last)),
        [pltpu.VMEM((half, wide), F32)],
        cost(0, rows * 3072 * 6),
    )


def add_bf(*terms):
    total = terms[0].astype(F32)
    for term in terms[1:]:
        total = total + term.astype(F32)
    return total.astype(BF)


def xor_pairs(size, step):
    return [(i, i ^ step) for i in range(size)]


class Reduction:
    def __init__(self, geo, stages, parts, pieces):
        self.st, self.parts, self.fast = stages, parts, geo.fast
        self.size_z = geo.fsdp // 2
        self.from_x, self.terms, self.sums, self.halves = [], [], [], None
        if self.fast:
            self.n = parts[0].shape[0] // 2
            self.m = self.n // self.size_z
            ends = [round(self.n * sum(pieces[: i + 1]) / sum(pieces)) for i in range(len(pieces))]
            self.cuts = [e // self.m * self.m for e in ends]
            self.cuts = list(zip([0] + self.cuts, self.cuts))

    def over_cores(self):
        if self.fast:
            self.got = self.st.permute(self.parts[1], "c")
            return self.got

    def prepare(self):
        if self.fast:
            keep, n = self.st.now(self.parts[0]), self.n
            self.halves = [add_bf(keep[n + a : n + b], self.got[n + a : n + b]) for a, b in self.cuts]
            return self.halves

    def over_x(self):
        if self.fast:
            k = len(self.from_x)
            if self.halves is None:
                first, last = (self.n + at for at in self.cuts[k])
                keep = self.st.now(self.parts[0])
                half = add_bf(keep[first:last], self.got[first:last])
            else:
                half = self.st.now(self.halves[k])
            self.from_x.append(lax.ppermute(half, "x", SWAP))
            return self.from_x[-1]

    def over_z(self, *steps):
        if not self.fast:
            return self.scatter_z() if 0 in steps else None
        keep, m, sent = self.st.now(self.parts[0]), self.m, []
        for k in steps:
            rows = slice(k * m, (k + 1) * m)
            term = add_bf(keep[rows], self.got[rows], self.from_x[0][rows])
            if k:
                sent.append(lax.ppermute(term, "z", xor_pairs(self.size_z, k)))
            self.terms.append(sent[-1] if k else term)
        return sent or self.terms

    def add_piece(self):
        if self.fast:
            k = len(self.sums)
            first, last = self.cuts[k]
            keep = self.st.now(self.parts[0])
            self.sums.append(add_bf(keep[first:last], self.got[first:last], self.from_x[k]))
            return self.sums[-1]

    def scatter_z(self):
        part = self.st.now(self.parts[0])
        if self.fast:
            while len(self.sums) < len(self.from_x):
                self.add_piece()
            part = jnp.concatenate(self.sums, axis=0)
            self.terms = [lax.psum_scatter(part, "z", scatter_dimension=0, tiled=True)]
        else:
            self.terms = [lax.psum_scatter(part, ("z", "x"), scatter_dimension=0, tiled=True)]

    def over_y(self, *after):
        if self.fast:
            self.share = lax.optimization_barrier((self.st.now(self.terms[0]), *after))[0]
            if len(self.terms) > 1:
                self.share = add_bf(self.share, *self.terms[1:])
            self.got_y = lax.ppermute(self.share, "y", SWAP)
            return self.got_y

    def total(self):
        if not self.fast:
            return lax.psum(self.terms[0], ("y", "c")), None
        total = add_bf(self.st.now(self.share), self.got_y)
        return total, lax.ppermute(total, "c", SWAP)


class LastReduction:
    def __init__(self, geo, stages, parts):
        self.geo, self.st, self.parts, self.fast = geo, stages, parts, geo.fast
        self.size_z = geo.fsdp // 2

    def over_cores(self):
        if self.fast:
            self.got = self.st.permute(self.parts[2], "c")
            return self.got

    def over_y(self):
        if self.fast:
            n = self.parts[0].shape[0]
            half = add_bf(self.st.now(self.parts[1]), self.got[n:])
            self.from_y = lax.ppermute(half, "y", SWAP)
            return self.from_y

    def over_x(self):
        if self.fast:
            n = self.parts[0].shape[0] // 2
            keep = self.st.now(self.parts[0])
            half = add_bf(keep[n:], self.got[n : 2 * n], self.from_y[n:])
            self.from_x = lax.ppermute(half, "x", SWAP)
            return self.from_x

    def over_z(self):
        if not self.fast:
            part = self.st.now(self.parts[0])
            self.terms = [lax.psum_scatter(part, ("z", "x"), scatter_dimension=0, tiled=True)]
            return self.terms
        m = self.parts[0].shape[0] // 2 // self.size_z
        keep = self.st.now(self.parts[0])
        self.terms = []
        for k in range(self.size_z):
            rows = slice(k * m, (k + 1) * m)
            term = add_bf(keep[rows], self.got[rows], self.from_y[rows], self.from_x[rows])
            self.terms.append(lax.ppermute(term, "z", xor_pairs(self.size_z, k)) if k else term)
        return self.terms

    def back_over_y(self):
        if self.fast:
            self.share = add_bf(self.st.now(self.terms[0]), *self.terms[1:])
            self.other = lax.ppermute(self.share, "y", SWAP)
            return self.other

    def total(self):
        if not self.fast:
            return [lax.psum(self.terms[0], ("y", "c"))]
        both = [self.share, self.other]
        return both + [self.st.permute(part, "c") for part in both]


def fold_in(v, axis, size, step=1):
    return v + lax.ppermute(v, axis, xor_pairs(size, step))


def gather_whole(own):
    return Parts([lax.all_gather(own, ("z", "x"), axis=0, tiled=True)])


class Geometry:
    pass


def local(
    geo,
    residual,
    out_grad,
    lengths,
    gain_one,
    qkv_weight,
    qv_bias,
    out_weight,
    out_bias,
    gain_two,
    fc_weight,
    fc_bias,
    proj_weight,
    proj_bias,
):
    geo.ranks = geo.seq
    geo.ns, geo.t, geo.narrow = residual.shape
    geo.wide, geo.ff = geo.narrow + 1, fc_weight.shape[1]
    narrow, wide, groups, ff = geo.narrow, geo.wide, geo.ranks, geo.ff
    heads, e = qv_bias.shape[0], qv_bias.shape[1] // 2
    size_z = geo.fsdp // 2
    geo.fast = (
        wide // geo.fsdp % 32 == 0
        and size_z & (size_z - 1) == 0
        and wide % (ff // size_z) == 0
        and ff // size_z % 64 == 0
    )
    z, x, y, c = (lax.axis_index(a) for a in ("z", "x", "y", "c"))
    idx = jnp.stack([z, x, y, c, 2 * y + c, z, z, z]).astype(jnp.int32)
    pad = lambda v: jnp.pad(v, (0, wide - narrow)).reshape(1, wide)
    gain1, gain2 = gain_one.reshape(1, wide), gain_two.reshape(1, wide)

    by_slot = qv_bias.reshape(groups, 3, 2 * e).transpose(1, 0, 2)
    q_bias = jnp.pad(by_slot[:, :, :e], ((0, 0), (0, 0), (0, e))).reshape(3, -1)
    bias = jnp.concatenate([q_bias, by_slot[:, :, e:].reshape(3, -1)], axis=1).reshape(1, -1)

    st = Stages(idx)
    own = prep_qkv(geo, idx, qkv_weight)
    bias_a, bias_b = bias[:, :wide], bias[:, wide:]
    if geo.fast:
        sides = [(dx, dc, 0, size_z, True) for dc in range(2) for dx in range(2)]
        whole = [own] + [lax.ppermute(own, "z", xor_pairs(size_z, i)) for i in range(1, size_z)]
        rest_own = prep_rest(geo, idx, out_weight, fc_weight, proj_weight)
        rest_own = lax.optimization_barrier((rest_own, whole[-1]))[0]
        rest = [lax.all_gather(rest_own, ("z", "x", "c"), axis=0, tiled=True)]
        st.end(whole)
        rows_a, rows_b = (
            jnp.concatenate([w[:, cut] for w in whole], axis=0)
            for cut in (slice(0, wide), slice(wide, 3 * wide))
        )
        other_a = st.permute(rows_a, "x")
        st.end(other_a)
        other_b = st.permute(rows_b, "x")
        w_a = [rows_a, other_a, st.permute(rows_a, "c"), st.permute(other_a, "c")]
        st.end(w_a)
        w_a = Parts(w_a, sides)
    else:
        w_a = gather_whole(own[:, :wide])
        w_b = gather_whole(own[:, wide:])
        widen = lambda w: jnp.pad(w, ((0, 0), (0, wide - narrow))).astype(BF)
        rest = [
            gather_whole(w).arrays[0]
            for w in (widen(out_weight), fc_weight.astype(BF), widen(proj_weight))
        ]
    sends, wq_a, (normed_one, normed_t) = qkv_forward(
        geo, st.token, residual, gain1, bias_a, w_a, (0,), True
    )
    st.end(sends)
    if geo.fast:
        w_b = Parts([rows_b, other_b, st.permute(rows_b, "c"), st.permute(other_b, "c")], sides)
    sends_b, wq_b, _ = qkv_forward(geo, idx, normed_one, gain1, bias_b, w_b, (1, 2), False)
    sends = list(sends) + list(sends_b)
    free = Stages(idx)
    slabs, saved, o_slabs = [], [], []
    for i in range(3):
        slabs.append(free.exchange(sends[4 * i : 4 * i + 4]))
    for i in range(3):
        o, stats = attention_forward(geo, idx, lengths, slabs[i])
        saved.append(stats)
        o_slabs += free.exchange(o)
    st.end(o_slabs)
    (output, d_pre, normed_two, attn, og, middle, bias_sums, out_w, d_norm), proj_parts = mlp_forward(
        geo,
        st.token,
        o_slabs,
        residual,
        out_grad,
        gain2,
        pad(out_bias),
        fc_bias.reshape(1, ff),
        pad(proj_bias),
        rest,
    )
    st.end(proj_parts)
    proj_red = Reduction(geo, st, proj_parts, (1, 1))
    got = proj_red.over_cores(), proj_red.prepare()
    (d_branch, d_mid, vectors), d_sends = mlp_backward(
        geo, st.token, d_norm, out_w, og, middle, gain2, bias_sums
    )
    st.end(got, d_branch)
    d_slabs = st.exchange(d_sends)
    got = proj_red.over_x()
    fo_red = Reduction(geo, st, grad_fo(geo, st.token, attn, d_branch, normed_two, d_pre), (1, 1))
    st.end(d_slabs, got, fo_red.parts)
    got = proj_red.over_x(), fo_red.over_cores(), fo_red.prepare()
    dq = attention_backward(geo, st.token, 0, lengths, slabs[0], saved[0], d_slabs)
    st.end(got, dq)
    dq_slabs = [st.exchange(dq)]
    proj_red.scatter_z()
    got = fo_red.over_x()
    dq = attention_backward(geo, st.token, 1, lengths, slabs[1], saved[1], d_slabs)
    st.end(got, dq, dq_slabs)
    dq_slabs.append(st.exchange(dq))
    got = fo_red.over_x()
    dq = attention_backward(geo, st.token, 2, lengths, slabs[2], saved[2], d_slabs)
    st.end(got, dq, dq_slabs)
    dq_slabs.append(free.exchange(dq))
    fo_red.scatter_z()
    parts_a, dt_a = grad_qkv(geo, st.token, dq_slabs[0] + dq_slabs[1], normed_t)
    red_a = Reduction(geo, st, parts_a, (1,))
    st.end(dq_slabs, parts_a)
    got = red_a.over_cores()
    parts_b, dt_b = grad_qkv(geo, st.token, dq_slabs[2], normed_t, last=True)
    red_b = LastReduction(geo, st, parts_b)
    st.end(got, parts_b)
    got = red_a.over_x(), proj_red.over_y(), red_b.over_cores(), red_b.over_y()
    input_grad, vecs = input_backward(
        geo,
        st.now(residual),
        gain1,
        (dt_a, dt_b),
        (wq_a, wq_b),
        d_mid,
        vectors,
    )
    if geo.fast:
        vecs = fold_in(vecs, "c", 2)
    else:
        vecs = lax.psum(vecs, ("z", "x", "y", "c"))
    st.end(got, vecs)
    got = red_a.over_z(*range(size_z)), red_b.over_x()
    if geo.fast:
        vecs = fold_in(st.now(vecs), "x", 2)
        got += (fo_red.over_y(vecs),)
    st.end(got, vecs)
    got = red_b.over_z(), red_a.over_y()
    proj_sum, fo_sum = proj_red.total(), fo_red.total()
    if geo.fast:
        vecs = fold_in(st.now(vecs), "y", 2)
    st.end(got, vecs, proj_sum, fo_sum)
    got = red_b.back_over_y()
    sum_a = red_a.total()
    if geo.fast:
        vecs = st.now(vecs)
        terms = [vecs] + [lax.ppermute(vecs, "z", xor_pairs(size_z, k)) for k in range(1, size_z)]
        while len(terms) > 1:
            terms = [a + b for a, b in zip(terms[::2], terms[1::2])]
        vecs = terms[0]
    st.end(got, vecs, sum_a)
    sum_b = red_b.total()
    sums = vecs[8:11].reshape(3, 3 * groups, e)
    q_sum = sums[:, : 2 * groups].reshape(3, groups, 2, e)[:, :, 0]
    v_sum = sums[:, 2 * groups :]
    qv_grad = jnp.concatenate([q_sum, v_sum], axis=2).transpose(1, 0, 2).reshape(heads, 2 * e)

    def plan_fo(ins, outs, at):
        outs[0][at, :] = ins[0][:, :narrow].astype(F32)
        outs[1][at, :] = ins[0][:, wide:].astype(F32)

    def plan_proj(ins, outs, at):
        outs[0][at, :] = ins[0][:, :narrow].astype(F32)

    block = wide // geo.fsdp
    qkv_grad = finish_qkv(geo, idx, sum_a, sum_b)
    out_w_grad, fc_w_grad = finish(geo, idx, [fo_sum], plan_fo, "finish_fo")(
        [sd(block, narrow, dtype=F32), sd(block, ff, dtype=F32)]
    )
    (proj_w_grad,) = finish(geo, idx, [proj_sum], plan_proj, "finish_proj")(
        [sd(ff // geo.fsdp, narrow, dtype=F32)]
    )
    return (
        output,
        input_grad,
        vecs[0],
        qkv_grad,
        qv_grad,
        out_w_grad,
        vecs[2, :narrow],
        vecs[1],
        fc_w_grad,
        vecs[4:8].reshape(-1),
        proj_w_grad,
        vecs[3, :narrow],
    )


def solution(mesh):
    geo = Geometry()
    geo.fsdp, geo.seq = mesh.devices.shape
    fine = Mesh(
        mesh.devices.reshape(geo.fsdp // 2, 2, geo.seq // 2, 2), ("z", "x", "y", "c")
    )
    fs, sq = ("z", "x"), ("y", "c")
    tokens, rows = P(fs, sq, None), P(fs, None)
    return jax.shard_map(
        functools.partial(local, geo),
        mesh=fine,
        in_specs=(
            tokens,
            tokens,
            rows,
            P(),
            rows,
            P(),
            rows,
            P(),
            P(),
            rows,
            P(),
            rows,
            P(),
        ),
        out_specs=(tokens, tokens, P(), rows, P(), rows, P(), P(), rows, P(), rows, P()),
        check_vma=False,
    )
```
